128 devices in a mesh: section: 2 (over core), head: 4 (over x), tok: 16 (over z, y).
Axes of the slice: x: 4, y: 4, z: 4, core: 2. Of those that a mesh axis runs over, the one named last changes fastest.
Arguments:
- hidden: bfloat16 [16, 384, 3072], P('tok'), may hold values from -6 to 6
- latent: float32 [16, 384, 64], P('tok', ('section', 'head')), may hold values from -6 to 6
- w_qkv: bfloat16 [2, 3072, 3, 3072], P(None, None, None, ('section', 'head')), may hold values from -0.109375 to 0.109375
- w_out: bfloat16 [2, 3072, 3072], P(None, ('section', 'head')), may hold values from -0.109375 to 0.109375
- w_final: bfloat16 [3072, 64], replicated, may hold values from -0.109375 to 0.109375
- qk_gain: float32 [2, 2, 128], replicated, may hold values from 0.5 to 2.5
- modulation: float32 [2, 3, 3072], replicated, may hold values from -3 to 3
- stale_kv: bfloat16 [2, 2, 16, 384, 3072], P(None, None, 'tok', None, ('section', 'head')), may hold values from -60 to 60
- request_patches: int32 [4], replicated, may hold values from 1 to 8, 16 in all
- patch_order: int32 [16], replicated, may hold values from 0 to 15, each once
- step_index: int32 [1], replicated, may hold values from 0 to 27
Outputs:
- layer_out: bfloat16 [2, 16, 384, 3072], P(None, 'tok', ('section', 'head'))
- latent_next: float32 [16, 384, 64], P('tok', ('section', 'head'))
- denoised: float32 [16, 384, 64], P('tok', ('section', 'head'))
The draws below stay inside these ranges and needn't reach their ends.
Inputs may be any that keep to these rules, and one draw needn't show every extreme that they name: `request_patches`: the lengths sum to 16; the longest is exactly 8. `patch_order`: each patch appears once.
All inputs are finite; a program needn't handle non-finite values.
Results may differ from the reference program's by a relative error of at most 0.03.
Values may be sent and summed in bfloat16 or wider, within the bound.
A program may use at most 192 MiB of HBM per device.

```python
import math
import jax
import jax.numpy as jnp
import numpy as np
from jax import lax

D = 3072
HEADS = 24
HEAD_DIM = 128
LATENT = 64
PATCH = 384
STEPS = 28
LAYERS = 2
NP = 16
REQS = 4
MOST = 8


def draw_stale_kv(key, part):
    shape = (LAYERS, 2, NP, PATCH, D)
    return jnp.clip(jax.random.normal(key, shape, jnp.float32), -6.0, 6.0).astype(jnp.bfloat16)


def block_levels(rng, extent, cuts, least, largest):
    factor_of = 1.0
    for dim, blocks in cuts:
        draws = jax.random.uniform(jax.random.fold_in(jax.random.fold_in(rng, 6), dim), (blocks,), jnp.float32, least / len(cuts), largest / len(cuts))
        factor_of = factor_of * jnp.repeat(jnp.exp(draws), extent[dim] // blocks).reshape((-1,) + (1,) * (len(extent) - 1 - dim))
    return factor_of


def length_profile(number_of, total, reach, skew):
    weights = [(1 << 20) // math.isqrt(grade ** skew) + 1 for grade in range(2, number_of + 1)]
    surplus, counts = total - reach - (number_of - 1), [1] * (number_of - 1)
    while surplus > 0:
        movable = [i for i in range(number_of - 1) if counts[i] < reach]
        mass, remaining = sum([weights[i] for i in movable]), surplus
        for i in movable:
            addition = min(reach - counts[i], max(1, remaining * weights[i] // mass), surplus)
            counts[i] = counts[i] + addition
            surplus = surplus - addition
    return np.array([reach] + counts)


def uneven_parts(own_key, count, total, bound, slope):
    if count == 2:
        one = jax.random.randint(own_key, (), max(1, total - bound), min(bound, total - 1) + 1)
        return jnp.stack([one, total - one])
    lengths = jnp.asarray(length_profile(count, total, bound, slope), jnp.int32)
    pairs = (count - 1) // 2
    source_of, sink = lengths[1:1 + 2 * pairs:2], lengths[2:2 + 2 * pairs:2]
    margin = jnp.minimum(source_of - 1, bound - sink)
    passed = jax.random.randint(jax.random.fold_in(own_key, 1), (pairs,), 0, 1 << 20) % (margin + 1)
    lengths = lengths.at[1:1 + 2 * pairs:2].set(source_of - passed).at[2:2 + 2 * pairs:2].set(sink + passed)
    return lengths[jax.random.permutation(jax.random.fold_in(own_key, 2), count)]


def scatter_about(key, extent, spread, limit, split=(), held_as=jnp.bfloat16):
    gain = block_levels(key, extent, split, -0.22, 0.18) if split else 1.0
    entries = jax.random.normal(key, extent, jnp.float32) * spread * gain
    return jnp.minimum(jnp.maximum(entries, -limit), limit).astype(held_as)


def setup_inputs(seed: int = 0) -> dict:
    arg_keys = jax.random.split(jax.random.key(seed), 12)
    return {
        "hidden": scatter_about(arg_keys[0], (NP, PATCH, D), 1.0, 6.0, ((0, 16),)),
        "latent": scatter_about(arg_keys[1], (NP, PATCH, LATENT), 1.0, 6.0, ((0, 16), (1, 8)), jnp.float32),
        "w_qkv": scatter_about(arg_keys[2], (LAYERS, D, 3, D), D ** -0.5, 0.109375, ((3, 8),)),
        "w_out": scatter_about(arg_keys[3], (LAYERS, D, D), D ** -0.5, 0.109375, ((1, 8),)),
        "w_final": scatter_about(arg_keys[4], (D, LATENT), D ** -0.5, 0.109375),
        "qk_gain": jnp.clip(jax.random.uniform(arg_keys[5], (LAYERS, 2, HEAD_DIM), jnp.float32, 0.5, 2.5), 0.5, 2.5),
        "modulation": scatter_about(arg_keys[6], (LAYERS, 3, D), 0.5, 3.0, (), jnp.float32),
        "stale_kv": draw_stale_kv(jax.random.fold_in(arg_keys[11], 71), 0),
        "request_patches": uneven_parts(arg_keys[8], REQS, NP, MOST, 2).astype(jnp.int32),
        "patch_order": jax.random.permutation(arg_keys[9], NP).astype(jnp.int32),
        "step_index": jax.random.randint(arg_keys[10], (1,), 0, STEPS).astype(jnp.int32),
    }


norm_eps = 1e-06
time_shift = 3.0
rope_base = 10000.0

def layer_norm(inputs):
    average = lax.optimization_barrier(jnp.mean(inputs, axis=-1, keepdims=True))
    centred = inputs - average
    variance = lax.optimization_barrier(jnp.mean(centred * centred, axis=-1, keepdims=True))
    return centred * lax.rsqrt(variance + norm_eps)

def rms_norm(inputs, gains):
    return inputs * lax.rsqrt(lax.optimization_barrier(jnp.mean(inputs * inputs, axis=-1, keepdims=True)) + norm_eps) * gains

def rotate(inputs, positions):
    half_dim = inputs.shape[-1] // 2
    frequency = rope_base ** (-2.0 * jnp.arange(half_dim, dtype=jnp.float32) / inputs.shape[-1])
    angles = positions[..., None, None] * frequency
    pairs = inputs.reshape(inputs.shape[:-1] + (half_dim, 2))
    even_lane = pairs[..., 0]
    odd_lane = pairs[..., 1]
    cosine = jnp.cos(angles)
    sine = jnp.sin(angles)
    turned = jnp.stack([even_lane * cosine - odd_lane * sine, even_lane * sine + odd_lane * cosine], axis=-1)
    return turned.reshape(inputs.shape)

def slot_layout(request_patches, patch_order):
    request_ends = jnp.cumsum(request_patches).astype(jnp.int32)
    starts = (request_ends - request_patches).astype(jnp.int32)
    request_of = lax.optimization_barrier(jnp.sum((request_ends[None, :] <= patch_order[:, None]).astype(jnp.int32), axis=1)).astype(jnp.int32)
    chosen = request_of[:, None] == jnp.arange(request_patches.shape[0], dtype=jnp.int32)[None, :]
    first_patch = lax.optimization_barrier(jnp.sum(jnp.where(chosen, starts[None, :], 0), axis=1)).astype(jnp.int32)
    return (request_of, (patch_order - first_patch).astype(jnp.int32))

def project(inputs, layer_mod, weight, gains, positions):
    normed = (layer_norm(inputs.astype(jnp.float32)) * (1.0 + layer_mod[1]) + layer_mod[0]).astype(jnp.bfloat16)
    model_width = weight.shape[0]
    column_count = weight.shape[2]
    projected = jnp.dot(normed.reshape(-1, model_width), weight.reshape(model_width, 3 * column_count), preferred_element_type=jnp.float32)
    pieces = projected.reshape(inputs.shape[:-1] + (3, column_count // gains.shape[-1], gains.shape[-1]))
    queries = rotate(rms_norm(pieces[..., 0, :, :], gains[0]), positions).astype(jnp.bfloat16)
    keys_fresh = rotate(rms_norm(pieces[..., 1, :, :], gains[1]), positions).astype(jnp.bfloat16)
    values_fresh = pieces[..., 2, :, :].astype(jnp.bfloat16)
    return (queries, keys_fresh, values_fresh)

def attend_all(queries, keys_fresh, values_fresh, stale_keys, stale_values, request_of):
    queries, keys_fresh, values_fresh = lax.optimization_barrier((queries, keys_fresh, values_fresh))
    slot_ids = jnp.arange(request_of.shape[0], dtype=jnp.int32)
    scaling = 1.0 / math.sqrt(queries.shape[-1])

    def per_slot(slot):
        is_self = (slot_ids == slot)[:, None, None, None]
        keys_all = jnp.where(is_self, keys_fresh[slot][None], stale_keys).astype(jnp.float32)
        values_all = jnp.where(is_self, values_fresh[slot][None], stale_values).astype(jnp.float32)
        related = request_of == request_of[slot]
        scores = jnp.einsum('qhd,nkhd->hqnk', queries[slot].astype(jnp.float32), keys_all) * scaling
        scores = jnp.where(related[None, None, :, None], scores, -jnp.inf)
        row_max = lax.optimization_barrier(jnp.max(scores, axis=(2, 3), keepdims=True))
        weights = jnp.exp(scores - row_max)
        totals = lax.optimization_barrier(jnp.sum(weights, axis=(2, 3)))
        rounded = lax.optimization_barrier(weights.astype(jnp.bfloat16)).astype(jnp.float32)
        attended = jnp.einsum('hqnk,nkhd->qhd', rounded, values_all)
        return (attended / jnp.transpose(totals)[:, :, None]).astype(jnp.bfloat16)
    return lax.map(per_slot, slot_ids)

def noise_level(position):
    time_left = 1.0 - position.astype(jnp.float32) / STEPS
    return time_shift * time_left / (1.0 + (time_shift - 1.0) * time_left)

def reference(hidden, latent, w_qkv, w_out, w_final, qk_gain, modulation, stale_kv, request_patches, patch_order, step_index):
    request_of, offsets = slot_layout(request_patches, patch_order)
    positions = (offsets[:, None] * PATCH + jnp.arange(PATCH, dtype=jnp.int32)[None, :]).astype(jnp.float32)
    current = hidden
    outputs = []
    for layer_idx in range(LAYERS):
        queries, keys_fresh, values_fresh = project(current, modulation[layer_idx], w_qkv[layer_idx], qk_gain[layer_idx], positions)
        stale = stale_kv[layer_idx].reshape(2, NP, PATCH, HEADS, HEAD_DIM)
        attended = attend_all(queries, keys_fresh, values_fresh, stale[0], stale[1], request_of)
        update = jnp.dot(attended.reshape(-1, D), w_out[layer_idx], preferred_element_type=jnp.float32).reshape(NP, PATCH, D)
        current = (current.astype(jnp.float32) + modulation[layer_idx, 2] * update).astype(jnp.bfloat16)
        outputs.append(current)
        current = lax.optimization_barrier(current)
    normed = layer_norm(current.astype(jnp.float32)).astype(jnp.bfloat16)
    velocity = jnp.dot(normed.reshape(-1, D), w_final, preferred_element_type=jnp.float32).reshape(NP, PATCH, LATENT)
    level_now = noise_level(step_index[0])
    level_next = noise_level(step_index[0] + 1)
    return (jnp.stack(outputs), latent + (level_next - level_now) * velocity, latent - level_now * velocity)
```

```python
import functools
import math

import jax
import jax.numpy as jnp
from jax import lax
from jax.experimental import pallas as pl
from jax.experimental.pallas import tpu as pltpu
from jax.sharding import PartitionSpec as P

STEPS = 28


norm_eps = 1e-06
time_shift = 3.0
rope_base = 10000.0


def layer_norm(inputs):
    average = jnp.mean(inputs, axis=-1, keepdims=True)
    centred = inputs - average
    variance = jnp.mean(centred * centred, axis=-1, keepdims=True)
    return centred * lax.rsqrt(variance + norm_eps)


def rms_norm(inputs, gains):
    return inputs * lax.rsqrt(jnp.mean(inputs * inputs, axis=-1, keepdims=True) + norm_eps) * gains


def rotate(inputs, positions):
    half_dim = inputs.shape[-1] // 2
    frequency = rope_base ** (-2.0 * jnp.arange(half_dim, dtype=jnp.float32) / inputs.shape[-1])
    angles = positions[..., None, None] * frequency
    pairs = inputs.reshape(inputs.shape[:-1] + (half_dim, 2))
    even_lane = pairs[..., 0]
    odd_lane = pairs[..., 1]
    cosine = jnp.cos(angles)
    sine = jnp.sin(angles)
    turned = jnp.stack(
        [even_lane * cosine - odd_lane * sine, even_lane * sine + odd_lane * cosine], axis=-1
    )
    return turned.reshape(inputs.shape)


def slot_layout(request_patches, patch_order):
    request_ends = jnp.cumsum(request_patches)
    starts = request_ends - request_patches
    request_of = jnp.sum((request_ends[None, :] <= patch_order[:, None]).astype(jnp.int32), axis=1)
    chosen = request_of[:, None] == jnp.arange(request_patches.shape[0], dtype=jnp.int32)[None, :]
    first_patch = jnp.sum(jnp.where(chosen, starts[None, :], 0), axis=1)
    return (request_of, patch_order - first_patch)


def project(inputs, layer_mod, weight, gains, positions, head_dim):
    normed = (layer_norm(inputs.astype(jnp.float32)) * (1.0 + layer_mod[1]) + layer_mod[0]).astype(
        jnp.bfloat16
    )
    rows = inputs.shape[0]
    column_count = weight.shape[2]
    heads = column_count // head_dim
    pieces = [
        jnp.dot(normed, weight[:, part, :], preferred_element_type=jnp.float32).reshape(
            rows, heads, head_dim
        )
        for part in range(3)
    ]
    queries = rotate(rms_norm(pieces[0], gains[0]), positions).astype(jnp.bfloat16)
    keys_fresh = rotate(rms_norm(pieces[1], gains[1]), positions).astype(jnp.bfloat16)
    values_fresh = pieces[2].astype(jnp.bfloat16)
    return (
        queries.reshape(rows, column_count),
        keys_fresh.reshape(rows, column_count),
        values_fresh.reshape(rows, column_count),
    )


def attention_kernel(
    head_dim, fetch_ref, allow_ref, q_ref, kf_ref, vf_ref, ks_ref, vs_ref, o_ref, m_sc, l_sc, acc_sc
):
    slot = pl.program_id(0)
    heads = q_ref.shape[1] // head_dim
    scaling = 1.0 / math.sqrt(head_dim)
    contract = (((1,), (1,)), ((), ()))

    @pl.when(slot == 0)
    def _fresh():
        for h in range(heads):
            lanes = slice(h * head_dim, (h + 1) * head_dim)
            scores = (
                lax.dot_general(
                    q_ref[:, lanes], kf_ref[:, lanes], contract, preferred_element_type=jnp.float32
                )
                * scaling
            )
            row_max = jnp.max(scores, axis=1, keepdims=True)
            weights = jnp.exp(scores - row_max)
            m_sc[h] = row_max
            l_sc[h] = jnp.sum(weights, axis=1, keepdims=True)
            acc_sc[h] = jnp.dot(
                weights.astype(jnp.bfloat16), vf_ref[:, lanes], preferred_element_type=jnp.float32
            )

    @pl.when(allow_ref[slot] != 0)
    def _stale():
        for h in range(heads):
            lanes = slice(h * head_dim, (h + 1) * head_dim)
            scores = (
                lax.dot_general(
                    q_ref[:, lanes], ks_ref[:, lanes], contract, preferred_element_type=jnp.float32
                )
                * scaling
            )
            old_max = m_sc[h]
            new_max = jnp.maximum(old_max, jnp.max(scores, axis=1, keepdims=True))
            factor = jnp.exp(old_max - new_max)
            weights = jnp.exp(scores - new_max)
            l_sc[h] = l_sc[h] * factor + jnp.sum(weights, axis=1, keepdims=True)
            acc_sc[h] = acc_sc[h] * factor + jnp.dot(
                weights.astype(jnp.bfloat16), vs_ref[:, lanes], preferred_element_type=jnp.float32
            )
            m_sc[h] = new_max

    @pl.when(slot == pl.num_programs(0) - 1)
    def _finish():
        for h in range(heads):
            lanes = slice(h * head_dim, (h + 1) * head_dim)
            o_ref[:, lanes] = (acc_sc[h] / l_sc[h]).astype(o_ref.dtype)


def attend(queries, keys_fresh, values_fresh, stale_all, layer_idx, fetch, allow, head_dim):
    rows, features = queries.shape
    slot_total = stale_all.shape[2]
    heads = features // head_dim
    whole = pl.BlockSpec((rows, features), lambda j, f, a: (0, 0))
    key_spec = pl.BlockSpec(
        (None, None, None, rows, features), lambda j, f, a: (layer_idx, 0, f[j], 0, 0)
    )
    value_spec = pl.BlockSpec(
        (None, None, None, rows, features), lambda j, f, a: (layer_idx, 1, f[j], 0, 0)
    )
    return pl.pallas_call(
        functools.partial(attention_kernel, head_dim),
        out_shape=jax.ShapeDtypeStruct((rows, features), jnp.bfloat16),
        grid_spec=pltpu.PrefetchScalarGridSpec(
            num_scalar_prefetch=2,
            grid=(slot_total,),
            in_specs=[whole, whole, whole, key_spec, value_spec],
            out_specs=whole,
            scratch_shapes=[
                pltpu.VMEM((heads, rows, 1), jnp.float32),
                pltpu.VMEM((heads, rows, 1), jnp.float32),
                pltpu.VMEM((heads, rows, head_dim), jnp.float32),
            ],
        ),
        compiler_params=pltpu.CompilerParams(dimension_semantics=("arbitrary",)),
    )(fetch, allow, queries, keys_fresh, values_fresh, stale_all, stale_all)


def noise_level(position):
    time_left = 1.0 - position.astype(jnp.float32) / STEPS
    return time_shift * time_left / (1.0 + (time_shift - 1.0) * time_left)


def shards(
    hidden,
    latent,
    w_qkv,
    w_out,
    w_final,
    qk_gain,
    modulation,
    stale_kv,
    request_patches,
    patch_order,
    step_index,
):
    section_count = lax.axis_size("section")
    head_count = lax.axis_size("head")
    group_count = section_count * head_count
    section_index = lax.axis_index("section")
    head_index = lax.axis_index("head")
    tok_index = lax.axis_index("tok")
    group_index = section_index * head_count + head_index
    patch_len = hidden.shape[1]
    width = hidden.shape[2]
    head_dim = qk_gain.shape[-1]
    own_rows = patch_len // group_count
    layer_count = w_qkv.shape[0]
    request_of, offsets = slot_layout(request_patches, patch_order)
    slot_total = request_of.shape[0]
    my_request = request_of[tok_index]
    my_offset = offsets[tok_index]
    positions = (my_offset * patch_len + jnp.arange(patch_len, dtype=jnp.int32)).astype(jnp.float32)
    slot_ids = jnp.arange(slot_total, dtype=jnp.int32)
    allowed = (request_of == my_request) & (slot_ids != tok_index)
    marked = jnp.where(allowed, slot_ids, -1)
    running = lax.cummax(marked, axis=0)
    first_allowed = jnp.argmax(allowed).astype(jnp.int32)
    fetch = jnp.where(running >= 0, running, first_allowed).astype(jnp.int32)
    allow = allowed.astype(jnp.int32)
    stale_all = lax.all_gather(stale_kv, "tok", axis=2, tiled=True)
    current_full = hidden[0]
    own_input = lax.dynamic_slice_in_dim(current_full, group_index * own_rows, own_rows, 0)
    outputs = []
    for layer_idx in range(layer_count):
        queries, keys_fresh, values_fresh = project(
            current_full,
            modulation[layer_idx],
            w_qkv[layer_idx],
            qk_gain[layer_idx],
            positions,
            head_dim,
        )
        attended = attend(
            queries, keys_fresh, values_fresh, stale_all, layer_idx, fetch, allow, head_dim
        )
        partial = jnp.dot(attended, w_out[layer_idx], preferred_element_type=jnp.float32).astype(
            jnp.bfloat16
        )
        summed = lax.psum_scatter(
            partial, ("section", "head"), scatter_dimension=0, tiled=True
        ).astype(jnp.float32)
        gate = modulation[layer_idx, 2]
        own_out = (own_input.astype(jnp.float32) + gate * summed).astype(jnp.bfloat16)
        if layer_idx + 1 < layer_count:
            current_full = lax.all_gather(own_out, ("section", "head"), axis=0, tiled=True)
        own_input = own_out
        outputs.append(own_out)
    last_own = outputs[-1]
    layer_out = jnp.stack(outputs)[:, None]
    normed = layer_norm(last_own.astype(jnp.float32)).astype(jnp.bfloat16)
    velocity = jnp.dot(normed, w_final, preferred_element_type=jnp.float32)[None]
    level_now = noise_level(step_index[0])
    level_next = noise_level(step_index[0] + 1)
    return (layer_out, latent + (level_next - level_now) * velocity, latent - level_now * velocity)


def solution(mesh):
    placed = (
        P("tok", None, None),
        P("tok", ("section", "head"), None),
        P(None, None, None, ("section", "head")),
        P(None, ("section", "head"), None),
        P(),
        P(),
        P(),
        P(None, None, "tok", None, ("section", "head")),
        P(),
        P(),
        P(),
    )
    return jax.shard_map(
        shards,
        mesh=mesh,
        in_specs=placed,
        out_specs=(
            P(None, "tok", ("section", "head"), None),
            P("tok", ("section", "head"), None),
            P("tok", ("section", "head"), None),
        ),
        check_vma=False,
    )
```

```python
import functools
import math

import jax
import jax.numpy as jnp
from jax import lax
from jax.experimental import pallas as pl
from jax.experimental.pallas import tpu as pltpu
from jax.sharding import PartitionSpec as P

STEPS = 28


norm_eps = 1e-06
time_shift = 3.0
rope_base = 10000.0


def layer_norm(inputs):
    average = jnp.mean(inputs, axis=-1, keepdims=True)
    centred = inputs - average
    variance = jnp.mean(centred * centred, axis=-1, keepdims=True)
    return centred * lax.rsqrt(variance + norm_eps)


def rms_norm(inputs, gains):
    return inputs * lax.rsqrt(jnp.mean(inputs * inputs, axis=-1, keepdims=True) + norm_eps) * gains


def rotate(inputs, positions):
    half_dim = inputs.shape[-1] // 2
    frequency = rope_base ** (-2.0 * jnp.arange(half_dim, dtype=jnp.float32) / inputs.shape[-1])
    angles = positions[..., None, None] * frequency
    pairs = inputs.reshape(inputs.shape[:-1] + (half_dim, 2))
    even_lane = pairs[..., 0]
    odd_lane = pairs[..., 1]
    cosine = jnp.cos(angles)
    sine = jnp.sin(angles)
    turned = jnp.stack(
        [even_lane * cosine - odd_lane * sine, even_lane * sine + odd_lane * cosine], axis=-1
    )
    return turned.reshape(inputs.shape)


def slot_layout(request_patches, patch_order):
    request_ends = jnp.cumsum(request_patches)
    starts = request_ends - request_patches
    request_of = jnp.sum((request_ends[None, :] <= patch_order[:, None]).astype(jnp.int32), axis=1)
    chosen = request_of[:, None] == jnp.arange(request_patches.shape[0], dtype=jnp.int32)[None, :]
    first_patch = jnp.sum(jnp.where(chosen, starts[None, :], 0), axis=1)
    return (request_of, patch_order - first_patch)


def project(inputs, layer_mod, weight, gains, positions, head_dim):
    normed = (layer_norm(inputs.astype(jnp.float32)) * (1.0 + layer_mod[1]) + layer_mod[0]).astype(
        jnp.bfloat16
    )
    rows = inputs.shape[0]
    column_count = weight.shape[2]
    heads = column_count // head_dim
    pieces = [
        jnp.dot(normed, weight[:, part, :], preferred_element_type=jnp.float32).reshape(
            rows, heads, head_dim
        )
        for part in range(3)
    ]
    queries = rotate(rms_norm(pieces[0], gains[0]), positions).astype(jnp.bfloat16)
    keys_fresh = rotate(rms_norm(pieces[1], gains[1]), positions).astype(jnp.bfloat16)
    values_fresh = pieces[2].astype(jnp.bfloat16)
    return (
        queries.reshape(rows, column_count),
        keys_fresh.reshape(rows, column_count),
        values_fresh.reshape(rows, column_count),
    )


def attention_kernel(
    head_dim, fetch_ref, allow_ref, q_ref, kf_ref, vf_ref, ks_ref, vs_ref, o_ref, m_sc, l_sc, acc_sc
):
    slot = pl.program_id(0)
    heads = q_ref.shape[1] // head_dim
    scaling = 1.0 / math.sqrt(head_dim)
    contract = (((1,), (1,)), ((), ()))

    @pl.when(slot == 0)
    def _fresh():
        for h in range(heads):
            lanes = slice(h * head_dim, (h + 1) * head_dim)
            scores = (
                lax.dot_general(
                    q_ref[:, lanes], kf_ref[:, lanes], contract, preferred_element_type=jnp.float32
                )
                * scaling
            )
            row_max = jnp.max(scores, axis=1, keepdims=True)
            weights = jnp.exp(scores - row_max)
            m_sc[h] = row_max
            l_sc[h] = jnp.sum(weights, axis=1, keepdims=True)
            acc_sc[h] = jnp.dot(
                weights.astype(jnp.bfloat16), vf_ref[:, lanes], preferred_element_type=jnp.float32
            )

    @pl.when(allow_ref[slot] != 0)
    def _stale():
        for h in range(heads):
            lanes = slice(h * head_dim, (h + 1) * head_dim)
            scores = (
                lax.dot_general(
                    q_ref[:, lanes], ks_ref[:, lanes], contract, preferred_element_type=jnp.float32
                )
                * scaling
            )
            old_max = m_sc[h]
            new_max = jnp.maximum(old_max, jnp.max(scores, axis=1, keepdims=True))
            factor = jnp.exp(old_max - new_max)
            weights = jnp.exp(scores - new_max)
            l_sc[h] = l_sc[h] * factor + jnp.sum(weights, axis=1, keepdims=True)
            acc_sc[h] = acc_sc[h] * factor + jnp.dot(
                weights.astype(jnp.bfloat16), vs_ref[:, lanes], preferred_element_type=jnp.float32
            )
            m_sc[h] = new_max

    @pl.when(slot == pl.num_programs(0) - 1)
    def _finish():
        for h in range(heads):
            lanes = slice(h * head_dim, (h + 1) * head_dim)
            o_ref[:, lanes] = (acc_sc[h] / l_sc[h]).astype(o_ref.dtype)


def attend(queries, keys_fresh, values_fresh, stale, fetch, allow, head_dim):
    rows, features = queries.shape
    slot_total = stale.shape[1]
    heads = features // head_dim
    whole = pl.BlockSpec((rows, features), lambda j, f, a: (0, 0))
    key_spec = pl.BlockSpec(
        (None, None, rows, features), lambda j, f, a: (0, f[j], 0, 0)
    )
    value_spec = pl.BlockSpec(
        (None, None, rows, features), lambda j, f, a: (1, f[j], 0, 0)
    )
    return pl.pallas_call(
        functools.partial(attention_kernel, head_dim),
        out_shape=jax.ShapeDtypeStruct((rows, features), jnp.bfloat16),
        grid_spec=pltpu.PrefetchScalarGridSpec(
            num_scalar_prefetch=2,
            grid=(slot_total,),
            in_specs=[whole, whole, whole, key_spec, value_spec],
            out_specs=whole,
            scratch_shapes=[
                pltpu.VMEM((heads, rows, 1), jnp.float32),
                pltpu.VMEM((heads, rows, 1), jnp.float32),
                pltpu.VMEM((heads, rows, head_dim), jnp.float32),
            ],
        ),
        compiler_params=pltpu.CompilerParams(dimension_semantics=("arbitrary",)),
    )(fetch, allow, queries, keys_fresh, values_fresh, stale, stale)


def exchange_kernel(head_count, own_rows, gather, part_ref, own_ref, gate_ref, *rest):
    if gather:
        (out_ref, full_ref, near, far, mid, acc, far_in, spread,
         s1_send, s1_recv, s2_send, s2_recv, g1_send, g1_recv, g2_send, g2_recv) = rest
    else:
        (out_ref, near, far, mid, acc, s1_send, s1_recv, s2_send, s2_recv) = rest
    mesh_ids = pl.DeviceIdType.MESH
    section = lax.axis_index("section")
    head = lax.axis_index("head")
    tok = lax.axis_index("tok")
    other = 1 - section
    half = head_count * own_rows

    barrier = pltpu.get_barrier_semaphore()
    pl.semaphore_signal(barrier, inc=1, device_id=(other, head, tok), device_id_type=mesh_ids)
    for h in range(head_count):
        @pl.when(h != head)
        def _greet():
            pl.semaphore_signal(barrier, inc=1, device_id=(section, h, tok), device_id_type=mesh_ids)
    pl.semaphore_wait(barrier, head_count)

    first = pltpu.make_async_remote_copy(
        src_ref=part_ref.at[pl.ds(pl.multiple_of(other * half, own_rows), half)],
        dst_ref=near,
        send_sem=s1_send,
        recv_sem=s1_recv,
        device_id=(other, head, tok),
        device_id_type=mesh_ids,
    )
    first.start()
    first.wait()
    base = pl.multiple_of(section * half, own_rows)
    for h in range(head_count):
        rows = pl.ds(pl.multiple_of(base + h * own_rows, own_rows), own_rows)
        mid[h] = (
            part_ref[rows, :].astype(jnp.float32)
            + near[h * own_rows:(h + 1) * own_rows, :].astype(jnp.float32)
        ).astype(mid.dtype)

    def far_copy(h, slot):
        return pltpu.make_async_remote_copy(
            src_ref=mid.at[h],
            dst_ref=far.at[slot],
            send_sem=s2_send.at[h],
            recv_sem=s2_recv.at[slot],
            device_id=(section, h, tok),
            device_id_type=mesh_ids,
        )

    for h in range(head_count):
        @pl.when(h != head)
        def _send():
            far_copy(h, head).start()
    mine = pl.ds(pl.multiple_of(base + head * own_rows, own_rows), own_rows)
    near_mine = pl.ds(pl.multiple_of(head * own_rows, own_rows), own_rows)
    acc[...] = part_ref[mine, :].astype(jnp.float32) + near[near_mine, :].astype(jnp.float32)
    for h in range(head_count):
        @pl.when(h != head)
        def _wait():
            far_copy(h, h).wait()
            acc[...] += far[h].astype(jnp.float32)
    if not gather:
        out_ref[...] = acc[...]
        return
    spread[head] = (own_ref[...].astype(jnp.float32) + gate_ref[...] * acc[...]).astype(spread.dtype)
    out_ref[...] = spread[head]

    def share_copy(h, slot):
        return pltpu.make_async_remote_copy(
            src_ref=spread.at[head],
            dst_ref=far_in.at[slot],
            send_sem=g1_send.at[h],
            recv_sem=g1_recv.at[slot],
            device_id=(section, h, tok),
            device_id_type=mesh_ids,
        )

    for h in range(head_count):
        @pl.when(h != head)
        def _share():
            share_copy(h, head).start()
    for h in range(head_count):
        @pl.when(h != head)
        def _collect():
            share_copy(h, h).wait()
            spread[h] = far_in[h]
    last = pltpu.make_async_remote_copy(
        src_ref=spread,
        dst_ref=full_ref.at[section],
        send_sem=g2_send,
        recv_sem=g2_recv,
        device_id=(other, head, tok),
        device_id_type=mesh_ids,
    )
    last.start()
    full_ref[section] = spread[...]
    last.wait()


def exchange(partial, own_input, gate, layer_idx, gather, head_count, own_rows):
    rows, width = partial.shape
    half = head_count * own_rows
    vmem = pl.BlockSpec(memory_space=pltpu.VMEM)
    scratch = [
        pltpu.VMEM((half, width), partial.dtype),
        pltpu.VMEM((head_count, own_rows, width), partial.dtype),
        pltpu.VMEM((head_count, own_rows, width), partial.dtype),
        pltpu.VMEM((own_rows, width), jnp.float32),
    ]
    if gather:
        out_shape = (
            jax.ShapeDtypeStruct((own_rows, width), jnp.bfloat16),
            jax.ShapeDtypeStruct((rows // half, head_count, own_rows, width), jnp.bfloat16),
        )
        out_specs = (vmem, vmem)
        scratch += [
            pltpu.VMEM((head_count, own_rows, width), jnp.bfloat16),
            pltpu.VMEM((head_count, own_rows, width), jnp.bfloat16),
        ]
    else:
        out_shape = jax.ShapeDtypeStruct((own_rows, width), jnp.float32)
        out_specs = vmem
    scratch += [
        pltpu.SemaphoreType.DMA(()),
        pltpu.SemaphoreType.DMA(()),
        pltpu.SemaphoreType.DMA((head_count,)),
        pltpu.SemaphoreType.DMA((head_count,)),
    ]
    if gather:
        scratch += [
            pltpu.SemaphoreType.DMA((head_count,)),
            pltpu.SemaphoreType.DMA((head_count,)),
            pltpu.SemaphoreType.DMA(()),
            pltpu.SemaphoreType.DMA(()),
        ]
    return pl.pallas_call(
        functools.partial(exchange_kernel, head_count, own_rows, gather),
        out_shape=out_shape,
        in_specs=[vmem, vmem, vmem],
        out_specs=out_specs,
        scratch_shapes=scratch,
        compiler_params=pltpu.CompilerParams(
            collective_id=layer_idx, has_side_effects=True, vmem_limit_bytes=48 * 1024 * 1024
        ),
    )(partial, own_input, gate.reshape(1, width))


def noise_level(position):
    time_left = 1.0 - position.astype(jnp.float32) / STEPS
    return time_shift * time_left / (1.0 + (time_shift - 1.0) * time_left)


def shards(
    hidden,
    latent,
    w_qkv,
    w_out,
    w_final,
    qk_gain,
    modulation,
    stale_kv,
    request_patches,
    patch_order,
    step_index,
):
    section_count = lax.axis_size("section")
    head_count = lax.axis_size("head")
    group_count = section_count * head_count
    section_index = lax.axis_index("section")
    head_index = lax.axis_index("head")
    tok_index = lax.axis_index("tok")
    group_index = section_index * head_count + head_index
    patch_len = hidden.shape[1]
    width = hidden.shape[2]
    head_dim = qk_gain.shape[-1]
    own_rows = patch_len // group_count
    layer_count = w_qkv.shape[0]
    request_of, offsets = slot_layout(request_patches, patch_order)
    slot_total = request_of.shape[0]
    my_request = request_of[tok_index]
    my_offset = offsets[tok_index]
    positions = (my_offset * patch_len + jnp.arange(patch_len, dtype=jnp.int32)).astype(jnp.float32)
    slot_ids = jnp.arange(slot_total, dtype=jnp.int32)
    allowed = (request_of == my_request) & (slot_ids != tok_index)
    marked = jnp.where(allowed, slot_ids, -1)
    running = lax.cummax(marked, axis=0)
    first_allowed = jnp.argmax(allowed).astype(jnp.int32)
    fetch = jnp.where(running >= 0, running, first_allowed).astype(jnp.int32)
    allow = allowed.astype(jnp.int32)
    stale_layers = [
        lax.all_gather(stale_kv[layer], "tok", axis=1, tiled=True) for layer in range(layer_count)
    ]
    current_full = hidden[0]
    own_input = lax.dynamic_slice_in_dim(current_full, group_index * own_rows, own_rows, 0)
    outputs = []
    for layer_idx in range(layer_count):
        queries, keys_fresh, values_fresh = project(
            current_full,
            modulation[layer_idx],
            w_qkv[layer_idx],
            qk_gain[layer_idx],
            positions,
            head_dim,
        )
        attended = attend(
            queries, keys_fresh, values_fresh, stale_layers[layer_idx], fetch, allow, head_dim
        )
        partial = jnp.dot(attended, w_out[layer_idx], preferred_element_type=jnp.float32).astype(
            jnp.bfloat16
        )
        gate = modulation[layer_idx, 2]
        if layer_idx + 1 < layer_count:
            own_out, gathered = exchange(
                partial, own_input, gate, layer_idx, True, head_count, own_rows
            )
            current_full = gathered.reshape(patch_len, width)
        else:
            summed = exchange(partial, own_input, gate, layer_idx, False, head_count, own_rows)
            own_out = (own_input.astype(jnp.float32) + gate * summed).astype(jnp.bfloat16)
        own_input = own_out
        outputs.append(own_out)
    last_own = outputs[-1]
    layer_out = jnp.stack(outputs)[:, None]
    normed = layer_norm(last_own.astype(jnp.float32)).astype(jnp.bfloat16)
    velocity = jnp.dot(normed, w_final, preferred_element_type=jnp.float32)[None]
    level_now = noise_level(step_index[0])
    level_next = noise_level(step_index[0] + 1)
    return (layer_out, latent + (level_next - level_now) * velocity, latent - level_now * velocity)


def solution(mesh):
    placed = (
        P("tok", None, None),
        P("tok", ("section", "head"), None),
        P(None, None, None, ("section", "head")),
        P(None, ("section", "head"), None),
        P(),
        P(),
        P(),
        P(None, None, "tok", None, ("section", "head")),
        P(),
        P(),
        P(),
    )
    return jax.shard_map(
        shards,
        mesh=mesh,
        in_specs=placed,
        out_specs=(
            P(None, "tok", ("section", "head"), None),
            P("tok", ("section", "head"), None),
            P("tok", ("section", "head"), None),
        ),
        check_vma=False,
    )
```

```python
import functools
import math

import jax
import jax.numpy as jnp
from jax import lax
from jax.experimental import pallas as pl
from jax.experimental.pallas import tpu as pltpu
from jax.sharding import PartitionSpec as P

STEPS = 28


norm_eps = 1e-06
time_shift = 3.0
rope_base = 10000.0


def layer_norm(inputs):
    average = jnp.mean(inputs, axis=-1, keepdims=True)
    centred = inputs - average
    variance = jnp.mean(centred * centred, axis=-1, keepdims=True)
    return centred * lax.rsqrt(variance + norm_eps)


def rms_norm(inputs, gains):
    return inputs * lax.rsqrt(jnp.mean(inputs * inputs, axis=-1, keepdims=True) + norm_eps) * gains


def rotate(inputs, positions):
    half_dim = inputs.shape[-1] // 2
    frequency = rope_base ** (-2.0 * jnp.arange(half_dim, dtype=jnp.float32) / inputs.shape[-1])
    angles = positions[..., None, None] * frequency
    pairs = inputs.reshape(inputs.shape[:-1] + (half_dim, 2))
    even_lane = pairs[..., 0]
    odd_lane = pairs[..., 1]
    cosine = jnp.cos(angles)
    sine = jnp.sin(angles)
    turned = jnp.stack(
        [even_lane * cosine - odd_lane * sine, even_lane * sine + odd_lane * cosine], axis=-1
    )
    return turned.reshape(inputs.shape)


def slot_layout(request_patches, patch_order):
    request_ends = jnp.cumsum(request_patches)
    starts = request_ends - request_patches
    request_of = jnp.sum((request_ends[None, :] <= patch_order[:, None]).astype(jnp.int32), axis=1)
    chosen = request_of[:, None] == jnp.arange(request_patches.shape[0], dtype=jnp.int32)[None, :]
    first_patch = jnp.sum(jnp.where(chosen, starts[None, :], 0), axis=1)
    return (request_of, patch_order - first_patch)


def project(inputs, layer_mod, weight, gains, positions, head_dim):
    normed = (layer_norm(inputs.astype(jnp.float32)) * (1.0 + layer_mod[1]) + layer_mod[0]).astype(
        jnp.bfloat16
    )
    rows = inputs.shape[0]
    column_count = weight.shape[2]
    heads = column_count // head_dim
    pieces = [
        jnp.dot(normed, weight[:, part, :], preferred_element_type=jnp.float32).reshape(
            rows, heads, head_dim
        )
        for part in range(3)
    ]
    queries = rotate(rms_norm(pieces[0], gains[0]), positions).astype(jnp.bfloat16)
    keys_fresh = rotate(rms_norm(pieces[1], gains[1]), positions).astype(jnp.bfloat16)
    values_fresh = pieces[2].astype(jnp.bfloat16)
    return (
        queries.reshape(rows, column_count),
        keys_fresh.reshape(rows, column_count),
        values_fresh.reshape(rows, column_count),
    )


def attention_kernel(
    head_dim, fetch_ref, allow_ref, q_ref, kf_ref, vf_ref, ks_ref, vs_ref, o_ref, m_sc, l_sc, acc_sc
):
    slot = pl.program_id(0)
    heads = q_ref.shape[1] // head_dim
    scaling = 1.0 / math.sqrt(head_dim)
    contract = (((1,), (1,)), ((), ()))

    @pl.when(slot == 0)
    def _fresh():
        for h in range(heads):
            lanes = slice(h * head_dim, (h + 1) * head_dim)
            scores = (
                lax.dot_general(
                    q_ref[:, lanes], kf_ref[:, lanes], contract, preferred_element_type=jnp.float32
                )
                * scaling
            )
            row_max = jnp.max(scores, axis=1, keepdims=True)
            weights = jnp.exp(scores - row_max)
            m_sc[h] = row_max
            l_sc[h] = jnp.sum(weights, axis=1, keepdims=True)
            acc_sc[h] = jnp.dot(
                weights.astype(jnp.bfloat16), vf_ref[:, lanes], preferred_element_type=jnp.float32
            )

    @pl.when(allow_ref[slot] != 0)
    def _stale():
        for h in range(heads):
            lanes = slice(h * head_dim, (h + 1) * head_dim)
            scores = (
                lax.dot_general(
                    q_ref[:, lanes], ks_ref[:, lanes], contract, preferred_element_type=jnp.float32
                )
                * scaling
            )
            old_max = m_sc[h]
            new_max = jnp.maximum(old_max, jnp.max(scores, axis=1, keepdims=True))
            factor = jnp.exp(old_max - new_max)
            weights = jnp.exp(scores - new_max)
            l_sc[h] = l_sc[h] * factor + jnp.sum(weights, axis=1, keepdims=True)
            acc_sc[h] = acc_sc[h] * factor + jnp.dot(
                weights.astype(jnp.bfloat16), vs_ref[:, lanes], preferred_element_type=jnp.float32
            )
            m_sc[h] = new_max

    @pl.when(slot == pl.num_programs(0) - 1)
    def _finish():
        for h in range(heads):
            lanes = slice(h * head_dim, (h + 1) * head_dim)
            o_ref[:, lanes] = (acc_sc[h] / l_sc[h]).astype(o_ref.dtype)


def attend(queries, keys_fresh, values_fresh, stale, fetch, allow, head_dim):
    rows, features = queries.shape
    slot_total = stale.shape[0]
    heads = features // head_dim
    whole = pl.BlockSpec((rows, features), lambda j, f, a: (0, 0))
    key_spec = pl.BlockSpec(
        (None, None, rows, features), lambda j, f, a: (f[j], 0, 0, 0)
    )
    value_spec = pl.BlockSpec(
        (None, None, rows, features), lambda j, f, a: (f[j], 1, 0, 0)
    )
    return pl.pallas_call(
        functools.partial(attention_kernel, head_dim),
        out_shape=jax.ShapeDtypeStruct((rows, features), jnp.bfloat16),
        grid_spec=pltpu.PrefetchScalarGridSpec(
            num_scalar_prefetch=2,
            grid=(slot_total,),
            in_specs=[whole, whole, whole, key_spec, value_spec],
            out_specs=whole,
            scratch_shapes=[
                pltpu.VMEM((heads, rows, 1), jnp.float32),
                pltpu.VMEM((heads, rows, 1), jnp.float32),
                pltpu.VMEM((heads, rows, head_dim), jnp.float32),
            ],
        ),
        compiler_params=pltpu.CompilerParams(dimension_semantics=("arbitrary",)),
    )(fetch, allow, queries, keys_fresh, values_fresh, stale, stale)


def exchange_kernel(head_count, own_rows, gather, part_ref, own_ref, gate_ref, *rest):
    if gather:
        (out_ref, full_ref, near, far, mid, acc, far_in, spread,
         s1_send, s1_recv, s2_send, s2_recv, g1_send, g1_recv, g2_send, g2_recv) = rest
    else:
        (out_ref, near, far, mid, acc, s1_send, s1_recv, s2_send, s2_recv) = rest
    mesh_ids = pl.DeviceIdType.MESH
    section = lax.axis_index("section")
    head = lax.axis_index("head")
    tok = lax.axis_index("tok")
    other = 1 - section
    half = head_count * own_rows

    barrier = pltpu.get_barrier_semaphore()
    pl.semaphore_signal(barrier, inc=1, device_id=(other, head, tok), device_id_type=mesh_ids)
    for h in range(head_count):
        @pl.when(h != head)
        def _greet():
            pl.semaphore_signal(barrier, inc=1, device_id=(section, h, tok), device_id_type=mesh_ids)
    pl.semaphore_wait(barrier, head_count)

    first = pltpu.make_async_remote_copy(
        src_ref=part_ref.at[pl.ds(pl.multiple_of(other * half, own_rows), half)],
        dst_ref=near,
        send_sem=s1_send,
        recv_sem=s1_recv,
        device_id=(other, head, tok),
        device_id_type=mesh_ids,
    )
    first.start()
    first.wait()
    base = pl.multiple_of(section * half, own_rows)
    for h in range(head_count):
        rows = pl.ds(pl.multiple_of(base + h * own_rows, own_rows), own_rows)
        mid[h] = (
            part_ref[rows, :].astype(jnp.float32)
            + near[h * own_rows:(h + 1) * own_rows, :].astype(jnp.float32)
        ).astype(mid.dtype)

    def far_copy(h, slot):
        return pltpu.make_async_remote_copy(
            src_ref=mid.at[h],
            dst_ref=far.at[slot],
            send_sem=s2_send.at[h],
            recv_sem=s2_recv.at[slot],
            device_id=(section, h, tok),
            device_id_type=mesh_ids,
        )

    for h in range(head_count):
        @pl.when(h != head)
        def _send():
            far_copy(h, head).start()
    mine = pl.ds(pl.multiple_of(base + head * own_rows, own_rows), own_rows)
    near_mine = pl.ds(pl.multiple_of(head * own_rows, own_rows), own_rows)
    acc[...] = part_ref[mine, :].astype(jnp.float32) + near[near_mine, :].astype(jnp.float32)
    for h in range(head_count):
        @pl.when(h != head)
        def _wait():
            far_copy(h, h).wait()
            acc[...] += far[h].astype(jnp.float32)
    if not gather:
        out_ref[...] = acc[...]
        return
    spread[head] = (own_ref[...].astype(jnp.float32) + gate_ref[...] * acc[...]).astype(spread.dtype)
    out_ref[...] = spread[head]

    def share_copy(h, slot):
        return pltpu.make_async_remote_copy(
            src_ref=spread.at[head],
            dst_ref=far_in.at[slot],
            send_sem=g1_send.at[h],
            recv_sem=g1_recv.at[slot],
            device_id=(section, h, tok),
            device_id_type=mesh_ids,
        )

    for h in range(head_count):
        @pl.when(h != head)
        def _share():
            share_copy(h, head).start()
    for h in range(head_count):
        @pl.when(h != head)
        def _collect():
            share_copy(h, h).wait()
            spread[h] = far_in[h]
    last = pltpu.make_async_remote_copy(
        src_ref=spread,
        dst_ref=full_ref.at[section],
        send_sem=g2_send,
        recv_sem=g2_recv,
        device_id=(other, head, tok),
        device_id_type=mesh_ids,
    )
    last.start()
    full_ref[section] = spread[...]
    last.wait()


def exchange(partial, own_input, gate, layer_idx, gather, head_count, own_rows):
    rows, width = partial.shape
    half = head_count * own_rows
    vmem = pl.BlockSpec(memory_space=pltpu.VMEM)
    scratch = [
        pltpu.VMEM((half, width), partial.dtype),
        pltpu.VMEM((head_count, own_rows, width), partial.dtype),
        pltpu.VMEM((head_count, own_rows, width), partial.dtype),
        pltpu.VMEM((own_rows, width), jnp.float32),
    ]
    if gather:
        out_shape = (
            jax.ShapeDtypeStruct((own_rows, width), jnp.bfloat16),
            jax.ShapeDtypeStruct((rows // half, head_count, own_rows, width), jnp.bfloat16),
        )
        out_specs = (vmem, vmem)
        scratch += [
            pltpu.VMEM((head_count, own_rows, width), jnp.bfloat16),
            pltpu.VMEM((head_count, own_rows, width), jnp.bfloat16),
        ]
    else:
        out_shape = jax.ShapeDtypeStruct((own_rows, width), jnp.float32)
        out_specs = vmem
    scratch += [
        pltpu.SemaphoreType.DMA(()),
        pltpu.SemaphoreType.DMA(()),
        pltpu.SemaphoreType.DMA((head_count,)),
        pltpu.SemaphoreType.DMA((head_count,)),
    ]
    if gather:
        scratch += [
            pltpu.SemaphoreType.DMA((head_count,)),
            pltpu.SemaphoreType.DMA((head_count,)),
            pltpu.SemaphoreType.DMA(()),
            pltpu.SemaphoreType.DMA(()),
        ]
    return pl.pallas_call(
        functools.partial(exchange_kernel, head_count, own_rows, gather),
        out_shape=out_shape,
        in_specs=[vmem, vmem, vmem],
        out_specs=out_specs,
        scratch_shapes=scratch,
        compiler_params=pltpu.CompilerParams(
            collective_id=layer_idx, has_side_effects=True, vmem_limit_bytes=48 * 1024 * 1024
        ),
    )(partial, own_input, gate.reshape(1, width))


def noise_level(position):
    time_left = 1.0 - position.astype(jnp.float32) / STEPS
    return time_shift * time_left / (1.0 + (time_shift - 1.0) * time_left)


def shards(
    hidden,
    latent,
    w_qkv,
    w_out,
    w_final,
    qk_gain,
    modulation,
    stale_kv,
    request_patches,
    patch_order,
    step_index,
):
    section_count = lax.axis_size("section")
    head_count = lax.axis_size("head")
    group_count = section_count * head_count
    section_index = lax.axis_index("section")
    head_index = lax.axis_index("head")
    tok_index = lax.axis_index("tok")
    group_index = section_index * head_count + head_index
    patch_len = hidden.shape[1]
    width = hidden.shape[2]
    head_dim = qk_gain.shape[-1]
    own_rows = patch_len // group_count
    layer_count = w_qkv.shape[0]
    request_of, offsets = slot_layout(request_patches, patch_order)
    slot_total = request_of.shape[0]
    my_request = request_of[tok_index]
    my_offset = offsets[tok_index]
    positions = (my_offset * patch_len + jnp.arange(patch_len, dtype=jnp.int32)).astype(jnp.float32)
    slot_ids = jnp.arange(slot_total, dtype=jnp.int32)
    allowed = (request_of == my_request) & (slot_ids != tok_index)
    marked = jnp.where(allowed, slot_ids, -1)
    running = lax.cummax(marked, axis=0)
    first_allowed = jnp.argmax(allowed).astype(jnp.int32)
    fetch = jnp.where(running >= 0, running, first_allowed).astype(jnp.int32)
    allow = allowed.astype(jnp.int32)
    stale_layers = [
        lax.all_gather(jnp.swapaxes(stale_kv[layer], 0, 1), "tok", axis=0, tiled=True)
        for layer in range(layer_count)
    ]
    current_full = hidden[0]
    own_input = lax.dynamic_slice_in_dim(current_full, group_index * own_rows, own_rows, 0)
    outputs = []
    for layer_idx in range(layer_count):
        queries, keys_fresh, values_fresh = project(
            current_full,
            modulation[layer_idx],
            w_qkv[layer_idx],
            qk_gain[layer_idx],
            positions,
            head_dim,
        )
        attended = attend(
            queries, keys_fresh, values_fresh, stale_layers[layer_idx], fetch, allow, head_dim
        )
        partial = jnp.dot(attended, w_out[layer_idx], preferred_element_type=jnp.float32).astype(
            jnp.bfloat16
        )
        gate = modulation[layer_idx, 2]
        if layer_idx + 1 < layer_count:
            own_out, gathered = exchange(
                partial, own_input, gate, layer_idx, True, head_count, own_rows
            )
            current_full = gathered.reshape(patch_len, width)
        else:
            summed = exchange(partial, own_input, gate, layer_idx, False, head_count, own_rows)
            own_out = (own_input.astype(jnp.float32) + gate * summed).astype(jnp.bfloat16)
        own_input = own_out
        outputs.append(own_out)
    last_own = outputs[-1]
    layer_out = jnp.stack(outputs)[:, None]
    normed = layer_norm(last_own.astype(jnp.float32)).astype(jnp.bfloat16)
    velocity = jnp.dot(normed, w_final, preferred_element_type=jnp.float32)[None]
    level_now = noise_level(step_index[0])
    level_next = noise_level(step_index[0] + 1)
    return (layer_out, latent + (level_next - level_now) * velocity, latent - level_now * velocity)


def solution(mesh):
    placed = (
        P("tok", None, None),
        P("tok", ("section", "head"), None),
        P(None, None, None, ("section", "head")),
        P(None, ("section", "head"), None),
        P(),
        P(),
        P(),
        P(None, None, "tok", None, ("section", "head")),
        P(),
        P(),
        P(),
    )
    return jax.shard_map(
        shards,
        mesh=mesh,
        in_specs=placed,
        out_specs=(
            P(None, "tok", ("section", "head"), None),
            P("tok", ("section", "head"), None),
            P("tok", ("section", "head"), None),
        ),
        check_vma=False,
    )
```

```python
import functools
import math

import jax
import jax.numpy as jnp
from jax import lax
from jax.experimental import pallas as pl
from jax.experimental.pallas import tpu as pltpu
from jax.sharding import PartitionSpec as P

STEPS = 28


norm_eps = 1e-06
time_shift = 3.0
rope_base = 10000.0


def layer_norm(inputs):
    average = jnp.mean(inputs, axis=-1, keepdims=True)
    centred = inputs - average
    variance = jnp.mean(centred * centred, axis=-1, keepdims=True)
    return centred * lax.rsqrt(variance + norm_eps)


def rms_norm(inputs, gains):
    return inputs * lax.rsqrt(jnp.mean(inputs * inputs, axis=-1, keepdims=True) + norm_eps) * gains


def rotate(inputs, positions):
    half_dim = inputs.shape[-1] // 2
    frequency = rope_base ** (-2.0 * jnp.arange(half_dim, dtype=jnp.float32) / inputs.shape[-1])
    angles = positions[..., None, None] * frequency
    pairs = inputs.reshape(inputs.shape[:-1] + (half_dim, 2))
    even_lane = pairs[..., 0]
    odd_lane = pairs[..., 1]
    cosine = jnp.cos(angles)
    sine = jnp.sin(angles)
    turned = jnp.stack(
        [even_lane * cosine - odd_lane * sine, even_lane * sine + odd_lane * cosine], axis=-1
    )
    return turned.reshape(inputs.shape)


def slot_layout(request_patches, patch_order):
    request_ends = jnp.cumsum(request_patches)
    starts = request_ends - request_patches
    request_of = jnp.sum((request_ends[None, :] <= patch_order[:, None]).astype(jnp.int32), axis=1)
    chosen = request_of[:, None] == jnp.arange(request_patches.shape[0], dtype=jnp.int32)[None, :]
    first_patch = jnp.sum(jnp.where(chosen, starts[None, :], 0), axis=1)
    return (request_of, patch_order - first_patch)


def project(inputs, layer_mod, weight, gains, positions, head_dim):
    normed = (layer_norm(inputs.astype(jnp.float32)) * (1.0 + layer_mod[1]) + layer_mod[0]).astype(
        jnp.bfloat16
    )
    rows = inputs.shape[0]
    column_count = weight.shape[2]
    heads = column_count // head_dim
    pieces = [
        jnp.dot(normed, weight[:, part, :], preferred_element_type=jnp.float32).reshape(
            rows, heads, head_dim
        )
        for part in range(3)
    ]
    queries = rotate(rms_norm(pieces[0], gains[0]), positions).astype(jnp.bfloat16)
    keys_fresh = rotate(rms_norm(pieces[1], gains[1]), positions).astype(jnp.bfloat16)
    values_fresh = pieces[2].astype(jnp.bfloat16)
    return (
        queries.reshape(rows, column_count),
        keys_fresh.reshape(rows, column_count),
        values_fresh.reshape(rows, column_count),
    )


def attention_kernel(
    head_dim, fetch_ref, allow_ref, q_ref, kf_ref, vf_ref, ks_ref, vs_ref, o_ref, m_sc, l_sc, acc_sc
):
    slot = pl.program_id(0)
    heads = q_ref.shape[1] // head_dim
    scaling = 1.0 / math.sqrt(head_dim)
    contract = (((1,), (1,)), ((), ()))

    def lanes_of(h):
        return pl.ds(pl.multiple_of(h * head_dim, head_dim), head_dim)

    @pl.when(slot == 0)
    def _fresh():
        @pl.loop(0, heads)
        def _head(h):
            lanes = lanes_of(h)
            scores = (
                lax.dot_general(
                    q_ref[:, lanes], kf_ref[:, lanes], contract, preferred_element_type=jnp.float32
                )
                * scaling
            )
            row_max = jnp.max(scores, axis=1, keepdims=True)
            weights = jnp.exp(scores - row_max)
            m_sc[h] = row_max
            l_sc[h] = jnp.sum(weights, axis=1, keepdims=True)
            acc_sc[h] = jnp.dot(
                weights.astype(jnp.bfloat16), vf_ref[:, lanes], preferred_element_type=jnp.float32
            )

    @pl.when(allow_ref[slot] != 0)
    def _stale():
        @pl.loop(0, heads)
        def _head(h):
            lanes = lanes_of(h)
            scores = (
                lax.dot_general(
                    q_ref[:, lanes], ks_ref[:, lanes], contract, preferred_element_type=jnp.float32
                )
                * scaling
            )
            old_max = m_sc[h]
            new_max = jnp.maximum(old_max, jnp.max(scores, axis=1, keepdims=True))
            factor = jnp.exp(old_max - new_max)
            weights = jnp.exp(scores - new_max)
            l_sc[h] = l_sc[h] * factor + jnp.sum(weights, axis=1, keepdims=True)
            acc_sc[h] = acc_sc[h] * factor + jnp.dot(
                weights.astype(jnp.bfloat16), vs_ref[:, lanes], preferred_element_type=jnp.float32
            )
            m_sc[h] = new_max

    @pl.when(slot == pl.num_programs(0) - 1)
    def _finish():
        @pl.loop(0, heads)
        def _head(h):
            o_ref[:, lanes_of(h)] = (acc_sc[h] / l_sc[h]).astype(o_ref.dtype)


def attend(queries, keys_fresh, values_fresh, stale, fetch, allow, head_dim):
    rows, features = queries.shape
    slot_total = stale.shape[0]
    heads = features // head_dim
    whole = pl.BlockSpec((rows, features), lambda j, f, a: (0, 0))
    key_spec = pl.BlockSpec(
        (None, None, rows, features), lambda j, f, a: (f[j], 0, 0, 0)
    )
    value_spec = pl.BlockSpec(
        (None, None, rows, features), lambda j, f, a: (f[j], 1, 0, 0)
    )
    return pl.pallas_call(
        functools.partial(attention_kernel, head_dim),
        out_shape=jax.ShapeDtypeStruct((rows, features), jnp.bfloat16),
        grid_spec=pltpu.PrefetchScalarGridSpec(
            num_scalar_prefetch=2,
            grid=(slot_total,),
            in_specs=[whole, whole, whole, key_spec, value_spec],
            out_specs=whole,
            scratch_shapes=[
                pltpu.VMEM((heads, rows, 1), jnp.float32),
                pltpu.VMEM((heads, rows, 1), jnp.float32),
                pltpu.VMEM((heads, rows, head_dim), jnp.float32),
            ],
        ),
        compiler_params=pltpu.CompilerParams(dimension_semantics=("arbitrary",)),
    )(fetch, allow, queries, keys_fresh, values_fresh, stale, stale)


def exchange_kernel(head_count, own_rows, gather, part_ref, own_ref, gate_ref, *rest):
    if gather:
        (out_ref, full_ref, near, far, mid, acc, far_in, spread,
         s1_send, s1_recv, s2_send, s2_recv, g1_send, g1_recv, g2_send, g2_recv) = rest
    else:
        (out_ref, near, far, mid, acc, s1_send, s1_recv, s2_send, s2_recv) = rest
    mesh_ids = pl.DeviceIdType.MESH
    section = lax.axis_index("section")
    head = lax.axis_index("head")
    tok = lax.axis_index("tok")
    other = 1 - section
    half = head_count * own_rows

    barrier = pltpu.get_barrier_semaphore()
    pl.semaphore_signal(barrier, inc=1, device_id=(other, head, tok), device_id_type=mesh_ids)
    for h in range(head_count):
        @pl.when(h != head)
        def _greet():
            pl.semaphore_signal(barrier, inc=1, device_id=(section, h, tok), device_id_type=mesh_ids)
    pl.semaphore_wait(barrier, head_count)

    first = pltpu.make_async_remote_copy(
        src_ref=part_ref.at[pl.ds(pl.multiple_of(other * half, own_rows), half)],
        dst_ref=near,
        send_sem=s1_send,
        recv_sem=s1_recv,
        device_id=(other, head, tok),
        device_id_type=mesh_ids,
    )
    first.start()
    first.wait()
    base = pl.multiple_of(section * half, own_rows)
    for h in range(head_count):
        rows = pl.ds(pl.multiple_of(base + h * own_rows, own_rows), own_rows)
        mid[h] = (
            part_ref[rows, :].astype(jnp.float32)
            + near[h * own_rows:(h + 1) * own_rows, :].astype(jnp.float32)
        ).astype(mid.dtype)

    def far_copy(h, slot):
        return pltpu.make_async_remote_copy(
            src_ref=mid.at[h],
            dst_ref=far.at[slot],
            send_sem=s2_send.at[h],
            recv_sem=s2_recv.at[slot],
            device_id=(section, h, tok),
            device_id_type=mesh_ids,
        )

    for h in range(head_count):
        @pl.when(h != head)
        def _send():
            far_copy(h, head).start()
    mine = pl.ds(pl.multiple_of(base + head * own_rows, own_rows), own_rows)
    near_mine = pl.ds(pl.multiple_of(head * own_rows, own_rows), own_rows)
    acc[...] = part_ref[mine, :].astype(jnp.float32) + near[near_mine, :].astype(jnp.float32)
    for h in range(head_count):
        @pl.when(h != head)
        def _wait():
            far_copy(h, h).wait()
            acc[...] += far[h].astype(jnp.float32)
    if not gather:
        out_ref[...] = acc[...]
        return
    spread[head] = (own_ref[...].astype(jnp.float32) + gate_ref[...] * acc[...]).astype(spread.dtype)
    out_ref[...] = spread[head]

    def share_copy(h, slot):
        return pltpu.make_async_remote_copy(
            src_ref=spread.at[head],
            dst_ref=far_in.at[slot],
            send_sem=g1_send.at[h],
            recv_sem=g1_recv.at[slot],
            device_id=(section, h, tok),
            device_id_type=mesh_ids,
        )

    for h in range(head_count):
        @pl.when(h != head)
        def _share():
            share_copy(h, head).start()
    for h in range(head_count):
        @pl.when(h != head)
        def _collect():
            share_copy(h, h).wait()
            spread[h] = far_in[h]
    last = pltpu.make_async_remote_copy(
        src_ref=spread,
        dst_ref=full_ref.at[section],
        send_sem=g2_send,
        recv_sem=g2_recv,
        device_id=(other, head, tok),
        device_id_type=mesh_ids,
    )
    last.start()
    full_ref[section] = spread[...]
    last.wait()


def exchange(partial, own_input, gate, layer_idx, gather, head_count, own_rows):
    rows, width = partial.shape
    half = head_count * own_rows
    vmem = pl.BlockSpec(memory_space=pltpu.VMEM)
    scratch = [
        pltpu.VMEM((half, width), partial.dtype),
        pltpu.VMEM((head_count, own_rows, width), partial.dtype),
        pltpu.VMEM((head_count, own_rows, width), partial.dtype),
        pltpu.VMEM((own_rows, width), jnp.float32),
    ]
    if gather:
        out_shape = (
            jax.ShapeDtypeStruct((own_rows, width), jnp.bfloat16),
            jax.ShapeDtypeStruct((rows // half, head_count, own_rows, width), jnp.bfloat16),
        )
        out_specs = (vmem, vmem)
        scratch += [
            pltpu.VMEM((head_count, own_rows, width), jnp.bfloat16),
            pltpu.VMEM((head_count, own_rows, width), jnp.bfloat16),
        ]
    else:
        out_shape = jax.ShapeDtypeStruct((own_rows, width), jnp.float32)
        out_specs = vmem
    scratch += [
        pltpu.SemaphoreType.DMA(()),
        pltpu.SemaphoreType.DMA(()),
        pltpu.SemaphoreType.DMA((head_count,)),
        pltpu.SemaphoreType.DMA((head_count,)),
    ]
    if gather:
        scratch += [
            pltpu.SemaphoreType.DMA((head_count,)),
            pltpu.SemaphoreType.DMA((head_count,)),
            pltpu.SemaphoreType.DMA(()),
            pltpu.SemaphoreType.DMA(()),
        ]
    return pl.pallas_call(
        functools.partial(exchange_kernel, head_count, own_rows, gather),
        out_shape=out_shape,
        in_specs=[vmem, vmem, vmem],
        out_specs=out_specs,
        scratch_shapes=scratch,
        compiler_params=pltpu.CompilerParams(
            collective_id=layer_idx, has_side_effects=True, vmem_limit_bytes=48 * 1024 * 1024
        ),
    )(partial, own_input, gate.reshape(1, width))


def noise_level(position):
    time_left = 1.0 - position.astype(jnp.float32) / STEPS
    return time_shift * time_left / (1.0 + (time_shift - 1.0) * time_left)


def shards(
    hidden,
    latent,
    w_qkv,
    w_out,
    w_final,
    qk_gain,
    modulation,
    stale_kv,
    request_patches,
    patch_order,
    step_index,
):
    section_count = lax.axis_size("section")
    head_count = lax.axis_size("head")
    group_count = section_count * head_count
    section_index = lax.axis_index("section")
    head_index = lax.axis_index("head")
    tok_index = lax.axis_index("tok")
    group_index = section_index * head_count + head_index
    patch_len = hidden.shape[1]
    width = hidden.shape[2]
    head_dim = qk_gain.shape[-1]
    own_rows = patch_len // group_count
    layer_count = w_qkv.shape[0]
    request_of, offsets = slot_layout(request_patches, patch_order)
    slot_total = request_of.shape[0]
    my_request = request_of[tok_index]
    my_offset = offsets[tok_index]
    positions = (my_offset * patch_len + jnp.arange(patch_len, dtype=jnp.int32)).astype(jnp.float32)
    slot_ids = jnp.arange(slot_total, dtype=jnp.int32)
    allowed = (request_of == my_request) & (slot_ids != tok_index)
    marked = jnp.where(allowed, slot_ids, -1)
    running = lax.cummax(marked, axis=0)
    first_allowed = jnp.argmax(allowed).astype(jnp.int32)
    fetch = jnp.where(running >= 0, running, first_allowed).astype(jnp.int32)
    allow = allowed.astype(jnp.int32)
    stale_layers = [
        lax.all_gather(jnp.swapaxes(stale_kv[layer], 0, 1), "tok", axis=0, tiled=True)
        for layer in range(layer_count)
    ]
    current_full = hidden[0]
    own_input = lax.dynamic_slice_in_dim(current_full, group_index * own_rows, own_rows, 0)
    outputs = []
    for layer_idx in range(layer_count):
        queries, keys_fresh, values_fresh = project(
            current_full,
            modulation[layer_idx],
            w_qkv[layer_idx],
            qk_gain[layer_idx],
            positions,
            head_dim,
        )
        attended = attend(
            queries, keys_fresh, values_fresh, stale_layers[layer_idx], fetch, allow, head_dim
        )
        partial = jnp.dot(attended, w_out[layer_idx], preferred_element_type=jnp.float32).astype(
            jnp.bfloat16
        )
        gate = modulation[layer_idx, 2]
        if layer_idx + 1 < layer_count:
            own_out, gathered = exchange(
                partial, own_input, gate, layer_idx, True, head_count, own_rows
            )
            current_full = gathered.reshape(patch_len, width)
        else:
            summed = exchange(partial, own_input, gate, layer_idx, False, head_count, own_rows)
            own_out = (own_input.astype(jnp.float32) + gate * summed).astype(jnp.bfloat16)
        own_input = own_out
        outputs.append(own_out)
    last_own = outputs[-1]
    layer_out = jnp.stack(outputs)[:, None]
    normed = layer_norm(last_own.astype(jnp.float32)).astype(jnp.bfloat16)
    velocity = jnp.dot(normed, w_final, preferred_element_type=jnp.float32)[None]
    level_now = noise_level(step_index[0])
    level_next = noise_level(step_index[0] + 1)
    return (layer_out, latent + (level_next - level_now) * velocity, latent - level_now * velocity)


def solution(mesh):
    placed = (
        P("tok", None, None),
        P("tok", ("section", "head"), None),
        P(None, None, None, ("section", "head")),
        P(None, ("section", "head"), None),
        P(),
        P(),
        P(),
        P(None, None, "tok", None, ("section", "head")),
        P(),
        P(),
        P(),
    )
    return jax.shard_map(
        shards,
        mesh=mesh,
        in_specs=placed,
        out_specs=(
            P(None, "tok", ("section", "head"), None),
            P("tok", ("section", "head"), None),
            P("tok", ("section", "head"), None),
        ),
        check_vma=False,
    )
```

```python
import functools
import math

import jax
import jax.numpy as jnp
from jax import lax
from jax.experimental import pallas as pl
from jax.experimental.pallas import tpu as pltpu
from jax.sharding import PartitionSpec as P

STEPS = 28


norm_eps = 1e-06
time_shift = 3.0
rope_base = 10000.0


def layer_norm(inputs):
    average = jnp.mean(inputs, axis=-1, keepdims=True)
    centred = inputs - average
    variance = jnp.mean(centred * centred, axis=-1, keepdims=True)
    return centred * lax.rsqrt(variance + norm_eps)


def rms_norm(inputs, gains):
    return inputs * lax.rsqrt(jnp.mean(inputs * inputs, axis=-1, keepdims=True) + norm_eps) * gains


def rotate(inputs, positions):
    half_dim = inputs.shape[-1] // 2
    frequency = rope_base ** (-2.0 * jnp.arange(half_dim, dtype=jnp.float32) / inputs.shape[-1])
    angles = positions[..., None, None] * frequency
    pairs = inputs.reshape(inputs.shape[:-1] + (half_dim, 2))
    even_lane = pairs[..., 0]
    odd_lane = pairs[..., 1]
    cosine = jnp.cos(angles)
    sine = jnp.sin(angles)
    turned = jnp.stack(
        [even_lane * cosine - odd_lane * sine, even_lane * sine + odd_lane * cosine], axis=-1
    )
    return turned.reshape(inputs.shape)


def slot_layout(request_patches, patch_order):
    request_ends = jnp.cumsum(request_patches)
    starts = request_ends - request_patches
    request_of = jnp.sum((request_ends[None, :] <= patch_order[:, None]).astype(jnp.int32), axis=1)
    chosen = request_of[:, None] == jnp.arange(request_patches.shape[0], dtype=jnp.int32)[None, :]
    first_patch = jnp.sum(jnp.where(chosen, starts[None, :], 0), axis=1)
    return (request_of, patch_order - first_patch)


def project(inputs, layer_mod, weight, gains, positions, head_dim):
    normed = (layer_norm(inputs.astype(jnp.float32)) * (1.0 + layer_mod[1]) + layer_mod[0]).astype(
        jnp.bfloat16
    )
    rows = inputs.shape[0]
    column_count = weight.shape[2]
    heads = column_count // head_dim
    pieces = [
        jnp.dot(normed, weight[:, part, :], preferred_element_type=jnp.float32).reshape(
            rows, heads, head_dim
        )
        for part in range(3)
    ]
    queries = rotate(rms_norm(pieces[0], gains[0]), positions).astype(jnp.bfloat16)
    keys_fresh = rotate(rms_norm(pieces[1], gains[1]), positions).astype(jnp.bfloat16)
    values_fresh = pieces[2].astype(jnp.bfloat16)
    return (
        queries.reshape(rows, column_count),
        keys_fresh.reshape(rows, column_count),
        values_fresh.reshape(rows, column_count),
    )


def attention_kernel(
    head_dim, fetch_ref, allow_ref, q_ref, kf_ref, vf_ref, ks_ref, vs_ref, o_ref, m_sc, l_sc, acc_sc
):
    slot = pl.program_id(0)
    heads = q_ref.shape[1] // head_dim
    scaling = 1.0 / math.sqrt(head_dim)
    contract = (((1,), (1,)), ((), ()))

    @pl.when(slot == 0)
    def _fresh():
        for h in range(heads):
            lanes = slice(h * head_dim, (h + 1) * head_dim)
            scores = (
                lax.dot_general(
                    q_ref[:, lanes], kf_ref[:, lanes], contract, preferred_element_type=jnp.float32
                )
                * scaling
            )
            row_max = jnp.max(scores, axis=1, keepdims=True)
            weights = jnp.exp(scores - row_max)
            m_sc[h] = row_max
            l_sc[h] = jnp.sum(weights, axis=1, keepdims=True)
            acc_sc[h] = jnp.dot(
                weights.astype(jnp.bfloat16), vf_ref[:, lanes], preferred_element_type=jnp.float32
            )

    @pl.when(allow_ref[slot] != 0)
    def _stale():
        for h in range(heads):
            lanes = slice(h * head_dim, (h + 1) * head_dim)
            scores = (
                lax.dot_general(
                    q_ref[:, lanes], ks_ref[:, lanes], contract, preferred_element_type=jnp.float32
                )
                * scaling
            )
            old_max = m_sc[h]
            new_max = jnp.maximum(old_max, jnp.max(scores, axis=1, keepdims=True))
            factor = jnp.exp(old_max - new_max)
            weights = jnp.exp(scores - new_max)
            l_sc[h] = l_sc[h] * factor + jnp.sum(weights, axis=1, keepdims=True)
            acc_sc[h] = acc_sc[h] * factor + jnp.dot(
                weights.astype(jnp.bfloat16), vs_ref[:, lanes], preferred_element_type=jnp.float32
            )
            m_sc[h] = new_max

    @pl.when(slot == pl.num_programs(0) - 1)
    def _finish():
        for h in range(heads):
            lanes = slice(h * head_dim, (h + 1) * head_dim)
            o_ref[:, lanes] = (acc_sc[h] / l_sc[h]).astype(o_ref.dtype)


def attend(queries, keys_fresh, values_fresh, stale, fetch, allow, head_dim):
    rows, features = queries.shape
    slot_total = stale.shape[0]
    heads = features // head_dim
    whole = pl.BlockSpec((rows, features), lambda j, f, a: (0, 0))
    key_spec = pl.BlockSpec(
        (None, None, rows, features), lambda j, f, a: (f[j], 0, 0, 0)
    )
    value_spec = pl.BlockSpec(
        (None, None, rows, features), lambda j, f, a: (f[j], 1, 0, 0)
    )
    return pl.pallas_call(
        functools.partial(attention_kernel, head_dim),
        out_shape=jax.ShapeDtypeStruct((rows, features), jnp.bfloat16),
        grid_spec=pltpu.PrefetchScalarGridSpec(
            num_scalar_prefetch=2,
            grid=(slot_total,),
            in_specs=[whole, whole, whole, key_spec, value_spec],
            out_specs=whole,
            scratch_shapes=[
                pltpu.VMEM((heads, rows, 1), jnp.float32),
                pltpu.VMEM((heads, rows, 1), jnp.float32),
                pltpu.VMEM((heads, rows, head_dim), jnp.float32),
            ],
        ),
        compiler_params=pltpu.CompilerParams(dimension_semantics=("arbitrary",)),
    )(fetch, allow, queries, keys_fresh, values_fresh, stale, stale)


def exchange_kernel(head_count, own_rows, gather, part_ref, own_ref, gate_ref, *rest):
    if gather:
        (out_ref, full_ref, near, far, mid, acc,
         s1_send, s1_recv, s2_send, s2_recv, g1_send, g1_recv, g2_send, g2_recv) = rest
    else:
        (out_ref, near, far, mid, acc, s1_send, s1_recv, s2_send, s2_recv) = rest
    mesh_ids = pl.DeviceIdType.MESH
    section = lax.axis_index("section")
    head = lax.axis_index("head")
    tok = lax.axis_index("tok")
    other = 1 - section
    half = head_count * own_rows

    barrier = pltpu.get_barrier_semaphore()
    pl.semaphore_signal(barrier, inc=1, device_id=(other, head, tok), device_id_type=mesh_ids)
    for h in range(head_count):
        @pl.when(h != head)
        def _greet():
            pl.semaphore_signal(barrier, inc=1, device_id=(section, h, tok), device_id_type=mesh_ids)
    pl.semaphore_wait(barrier, head_count)

    def near_copy(h):
        return pltpu.make_async_remote_copy(
            src_ref=part_ref.at[pl.ds(pl.multiple_of(other * half + h * own_rows, own_rows), own_rows)],
            dst_ref=near.at[h],
            send_sem=s1_send.at[h],
            recv_sem=s1_recv.at[h],
            device_id=(other, head, tok),
            device_id_type=mesh_ids,
        )

    def far_copy(h, slot):
        return pltpu.make_async_remote_copy(
            src_ref=mid.at[h],
            dst_ref=far.at[slot],
            send_sem=s2_send.at[h],
            recv_sem=s2_recv.at[slot],
            device_id=(section, h, tok),
            device_id_type=mesh_ids,
        )

    for h in range(head_count):
        near_copy(h).start()
    base = pl.multiple_of(section * half, own_rows)
    for h in range(head_count):
        near_copy(h).wait()

        @pl.when(h != head)
        def _send():
            rows = pl.ds(pl.multiple_of(base + h * own_rows, own_rows), own_rows)
            mid[h] = (part_ref[rows, :].astype(jnp.float32) + near[h].astype(jnp.float32)).astype(
                mid.dtype
            )
            far_copy(h, head).start()

    mine = pl.ds(pl.multiple_of(base + head * own_rows, own_rows), own_rows)
    acc[...] = part_ref[mine, :].astype(jnp.float32) + near[head].astype(jnp.float32)
    for h in range(head_count):
        @pl.when(h != head)
        def _wait():
            far_copy(h, h).wait()
            acc[...] += far[h].astype(jnp.float32)
    if not gather:
        out_ref[...] = acc[...]
        return
    result = (own_ref[...].astype(jnp.float32) + gate_ref[...] * acc[...]).astype(full_ref.dtype)
    full_ref[section, head] = result
    out_ref[...] = result

    def share_copy(h, slot):
        return pltpu.make_async_remote_copy(
            src_ref=full_ref.at[section, head],
            dst_ref=full_ref.at[section, slot],
            send_sem=g1_send.at[h],
            recv_sem=g1_recv.at[slot],
            device_id=(section, h, tok),
            device_id_type=mesh_ids,
        )

    def pass_copy(h):
        return pltpu.make_async_remote_copy(
            src_ref=full_ref.at[section, h],
            dst_ref=full_ref.at[section, h],
            send_sem=g2_send.at[h],
            recv_sem=g2_recv.at[h],
            device_id=(other, head, tok),
            device_id_type=mesh_ids,
        )

    for h in range(head_count):
        @pl.when(h != head)
        def _share():
            share_copy(h, head).start()
    for h in range(head_count):
        @pl.when(h == head)
        def _own():
            pass_copy(h).start()
    for h in range(head_count):
        @pl.when(h != head)
        def _collect():
            share_copy(h, h).wait()
            pass_copy(h).start()
    for h in range(head_count):
        pass_copy(h).wait()


def exchange(partial, own_input, gate, layer_idx, gather, head_count, own_rows):
    rows, width = partial.shape
    half = head_count * own_rows
    vmem = pl.BlockSpec(memory_space=pltpu.VMEM)
    scratch = [
        pltpu.VMEM((head_count, own_rows, width), partial.dtype),
        pltpu.VMEM((head_count, own_rows, width), partial.dtype),
        pltpu.VMEM((head_count, own_rows, width), partial.dtype),
        pltpu.VMEM((own_rows, width), jnp.float32),
    ]
    if gather:
        out_shape = (
            jax.ShapeDtypeStruct((own_rows, width), jnp.bfloat16),
            jax.ShapeDtypeStruct((rows // half, head_count, own_rows, width), jnp.bfloat16),
        )
        out_specs = (vmem, vmem)
    else:
        out_shape = jax.ShapeDtypeStruct((own_rows, width), jnp.float32)
        out_specs = vmem
    semaphore_sets = 4 if gather else 2
    scratch += [pltpu.SemaphoreType.DMA((head_count,))] * (2 * semaphore_sets)
    return pl.pallas_call(
        functools.partial(exchange_kernel, head_count, own_rows, gather),
        out_shape=out_shape,
        in_specs=[vmem, vmem, vmem],
        out_specs=out_specs,
        scratch_shapes=scratch,
        compiler_params=pltpu.CompilerParams(
            collective_id=layer_idx, has_side_effects=True, vmem_limit_bytes=48 * 1024 * 1024
        ),
    )(partial, own_input, gate.reshape(1, width))


def noise_level(position):
    time_left = 1.0 - position.astype(jnp.float32) / STEPS
    return time_shift * time_left / (1.0 + (time_shift - 1.0) * time_left)


def shards(
    hidden,
    latent,
    w_qkv,
    w_out,
    w_final,
    qk_gain,
    modulation,
    stale_kv,
    request_patches,
    patch_order,
    step_index,
):
    section_count = lax.axis_size("section")
    head_count = lax.axis_size("head")
    group_count = section_count * head_count
    section_index = lax.axis_index("section")
    head_index = lax.axis_index("head")
    tok_index = lax.axis_index("tok")
    group_index = section_index * head_count + head_index
    patch_len = hidden.shape[1]
    width = hidden.shape[2]
    head_dim = qk_gain.shape[-1]
    own_rows = patch_len // group_count
    layer_count = w_qkv.shape[0]
    request_of, offsets = slot_layout(request_patches, patch_order)
    slot_total = request_of.shape[0]
    my_request = request_of[tok_index]
    my_offset = offsets[tok_index]
    positions = (my_offset * patch_len + jnp.arange(patch_len, dtype=jnp.int32)).astype(jnp.float32)
    slot_ids = jnp.arange(slot_total, dtype=jnp.int32)
    allowed = (request_of == my_request) & (slot_ids != tok_index)
    marked = jnp.where(allowed, slot_ids, -1)
    running = lax.cummax(marked, axis=0)
    first_allowed = jnp.argmax(allowed).astype(jnp.int32)
    fetch = jnp.where(running >= 0, running, first_allowed).astype(jnp.int32)
    allow = allowed.astype(jnp.int32)
    stale_layers = [
        lax.all_gather(jnp.swapaxes(stale_kv[layer], 0, 1), "tok", axis=0, tiled=True)
        for layer in range(layer_count)
    ]
    current_full = hidden[0]
    own_input = lax.dynamic_slice_in_dim(current_full, group_index * own_rows, own_rows, 0)
    outputs = []
    for layer_idx in range(layer_count):
        queries, keys_fresh, values_fresh = project(
            current_full,
            modulation[layer_idx],
            w_qkv[layer_idx],
            qk_gain[layer_idx],
            positions,
            head_dim,
        )
        attended = attend(
            queries, keys_fresh, values_fresh, stale_layers[layer_idx], fetch, allow, head_dim
        )
        partial = jnp.dot(attended, w_out[layer_idx], preferred_element_type=jnp.float32).astype(
            jnp.bfloat16
        )
        gate = modulation[layer_idx, 2]
        if layer_idx + 1 < layer_count:
            own_out, gathered = exchange(
                partial, own_input, gate, layer_idx, True, head_count, own_rows
            )
            current_full = gathered.reshape(patch_len, width)
        else:
            summed = exchange(partial, own_input, gate, layer_idx, False, head_count, own_rows)
            own_out = (own_input.astype(jnp.float32) + gate * summed).astype(jnp.bfloat16)
        own_input = own_out
        outputs.append(own_out)
    last_own = outputs[-1]
    layer_out = jnp.stack(outputs)[:, None]
    normed = layer_norm(last_own.astype(jnp.float32)).astype(jnp.bfloat16)
    velocity = jnp.dot(normed, w_final, preferred_element_type=jnp.float32)[None]
    level_now = noise_level(step_index[0])
    level_next = noise_level(step_index[0] + 1)
    return (layer_out, latent + (level_next - level_now) * velocity, latent - level_now * velocity)


def solution(mesh):
    placed = (
        P("tok", None, None),
        P("tok", ("section", "head"), None),
        P(None, None, None, ("section", "head")),
        P(None, ("section", "head"), None),
        P(),
        P(),
        P(),
        P(None, None, "tok", None, ("section", "head")),
        P(),
        P(),
        P(),
    )
    return jax.shard_map(
        shards,
        mesh=mesh,
        in_specs=placed,
        out_specs=(
            P(None, "tok", ("section", "head"), None),
            P("tok", ("section", "head"), None),
            P("tok", ("section", "head"), None),
        ),
        check_vma=False,
    )
```

```python
import functools
import math

import jax
import jax.numpy as jnp
from jax import lax
from jax.experimental import pallas as pl
from jax.experimental.pallas import tpu as pltpu
from jax.sharding import PartitionSpec as P

STEPS = 28


norm_eps = 1e-06
time_shift = 3.0
rope_base = 10000.0


def layer_norm(inputs):
    average = jnp.mean(inputs, axis=-1, keepdims=True)
    centred = inputs - average
    variance = jnp.mean(centred * centred, axis=-1, keepdims=True)
    return centred * lax.rsqrt(variance + norm_eps)


def rms_norm(inputs, gains):
    return inputs * lax.rsqrt(jnp.mean(inputs * inputs, axis=-1, keepdims=True) + norm_eps) * gains


def rotate(inputs, positions):
    half_dim = inputs.shape[-1] // 2
    frequency = rope_base ** (-2.0 * jnp.arange(half_dim, dtype=jnp.float32) / inputs.shape[-1])
    angles = positions[..., None, None] * frequency
    pairs = inputs.reshape(inputs.shape[:-1] + (half_dim, 2))
    even_lane = pairs[..., 0]
    odd_lane = pairs[..., 1]
    cosine = jnp.cos(angles)
    sine = jnp.sin(angles)
    turned = jnp.stack(
        [even_lane * cosine - odd_lane * sine, even_lane * sine + odd_lane * cosine], axis=-1
    )
    return turned.reshape(inputs.shape)


def slot_layout(request_patches, patch_order):
    request_ends = jnp.cumsum(request_patches)
    starts = request_ends - request_patches
    request_of = jnp.sum((request_ends[None, :] <= patch_order[:, None]).astype(jnp.int32), axis=1)
    chosen = request_of[:, None] == jnp.arange(request_patches.shape[0], dtype=jnp.int32)[None, :]
    first_patch = jnp.sum(jnp.where(chosen, starts[None, :], 0), axis=1)
    return (request_of, patch_order - first_patch)


def project(inputs, layer_mod, weight, gains, positions, head_dim):
    normed = (layer_norm(inputs.astype(jnp.float32)) * (1.0 + layer_mod[1]) + layer_mod[0]).astype(
        jnp.bfloat16
    )
    rows = inputs.shape[0]
    column_count = weight.shape[2]
    heads = column_count // head_dim
    pieces = [
        jnp.dot(normed, weight[:, part, :], preferred_element_type=jnp.float32).reshape(
            rows, heads, head_dim
        )
        for part in range(3)
    ]
    queries = rotate(rms_norm(pieces[0], gains[0]), positions).astype(jnp.bfloat16)
    keys_fresh = rotate(rms_norm(pieces[1], gains[1]), positions).astype(jnp.bfloat16)
    values_fresh = pieces[2].astype(jnp.bfloat16)
    return (
        queries.reshape(rows, column_count),
        keys_fresh.reshape(rows, column_count),
        values_fresh.reshape(rows, column_count),
    )


def attention_kernel(
    head_dim, fetch_ref, allow_ref, q_ref, kf_ref, vf_ref, ks_ref, vs_ref, o_ref, m_sc, l_sc, acc_sc
):
    slot = pl.program_id(0)
    heads = q_ref.shape[1] // head_dim
    scaling = 1.0 / math.sqrt(head_dim)
    contract = (((1,), (1,)), ((), ()))

    @pl.when(slot == 0)
    def _fresh():
        for h in range(heads):
            lanes = slice(h * head_dim, (h + 1) * head_dim)
            scores = (
                lax.dot_general(
                    q_ref[:, lanes], kf_ref[:, lanes], contract, preferred_element_type=jnp.float32
                )
                * scaling
            )
            row_max = jnp.max(scores, axis=1, keepdims=True)
            weights = jnp.exp(scores - row_max)
            m_sc[h] = row_max
            l_sc[h] = jnp.sum(weights, axis=1, keepdims=True)
            acc_sc[h] = jnp.dot(
                weights.astype(jnp.bfloat16), vf_ref[:, lanes], preferred_element_type=jnp.float32
            )

    @pl.when(allow_ref[slot] != 0)
    def _stale():
        for h in range(heads):
            lanes = slice(h * head_dim, (h + 1) * head_dim)
            scores = (
                lax.dot_general(
                    q_ref[:, lanes], ks_ref[:, lanes], contract, preferred_element_type=jnp.float32
                )
                * scaling
            )
            old_max = m_sc[h]
            new_max = jnp.maximum(old_max, jnp.max(scores, axis=1, keepdims=True))
            factor = jnp.exp(old_max - new_max)
            weights = jnp.exp(scores - new_max)
            l_sc[h] = l_sc[h] * factor + jnp.sum(weights, axis=1, keepdims=True)
            acc_sc[h] = acc_sc[h] * factor + jnp.dot(
                weights.astype(jnp.bfloat16), vs_ref[:, lanes], preferred_element_type=jnp.float32
            )
            m_sc[h] = new_max

    @pl.when(slot == pl.num_programs(0) - 1)
    def _finish():
        for h in range(heads):
            lanes = slice(h * head_dim, (h + 1) * head_dim)
            o_ref[:, lanes] = (acc_sc[h] / l_sc[h]).astype(o_ref.dtype)


def attend(queries, keys_fresh, values_fresh, stale, fetch, allow, head_dim):
    rows, features = queries.shape
    slot_total = stale.shape[0]
    heads = features // head_dim
    whole = pl.BlockSpec((rows, features), lambda j, f, a: (0, 0))
    key_spec = pl.BlockSpec(
        (None, None, rows, features), lambda j, f, a: (f[j], 0, 0, 0)
    )
    value_spec = pl.BlockSpec(
        (None, None, rows, features), lambda j, f, a: (f[j], 1, 0, 0)
    )
    return pl.pallas_call(
        functools.partial(attention_kernel, head_dim),
        out_shape=jax.ShapeDtypeStruct((rows, features), jnp.bfloat16),
        grid_spec=pltpu.PrefetchScalarGridSpec(
            num_scalar_prefetch=2,
            grid=(slot_total,),
            in_specs=[whole, whole, whole, key_spec, value_spec],
            out_specs=whole,
            scratch_shapes=[
                pltpu.VMEM((heads, rows, 1), jnp.float32),
                pltpu.VMEM((heads, rows, 1), jnp.float32),
                pltpu.VMEM((heads, rows, head_dim), jnp.float32),
            ],
        ),
        compiler_params=pltpu.CompilerParams(dimension_semantics=("arbitrary",)),
    )(fetch, allow, queries, keys_fresh, values_fresh, stale, stale)


def exchange_kernel(head_count, own_rows, split, gather, part_ref, own_ref, gate_ref, *rest):
    if gather:
        (out_ref, full_ref, near, mid, land_a, land_b, sums_a, sums_b, acc,
         s1_send, s1_recv, r_send, r_recv, a_send, a_recv, g2_send, g2_recv) = rest
    else:
        (out_ref, near, mid, land_a, land_b, sums_a, sums_b, acc,
         s1_send, s1_recv, r_send, r_recv) = rest
    mesh_ids = pl.DeviceIdType.MESH
    section = lax.axis_index("section")
    head = lax.axis_index("head")
    tok = lax.axis_index("tok")
    other = 1 - section
    half = head_count * own_rows
    up = lax.rem(head + 1, head_count)
    down = lax.rem(head + head_count - 1, head_count)
    opposite = lax.rem(head + 2, head_count)
    low = pl.ds(0, split)
    high = pl.ds(split, own_rows - split)

    barrier = pltpu.get_barrier_semaphore()
    pl.semaphore_signal(barrier, inc=1, device_id=(other, head, tok), device_id_type=mesh_ids)
    for h in range(head_count):
        @pl.when(h != head)
        def _greet():
            pl.semaphore_signal(barrier, inc=1, device_id=(section, h, tok), device_id_type=mesh_ids)
    pl.semaphore_wait(barrier, head_count)

    def near_copy(h):
        return pltpu.make_async_remote_copy(
            src_ref=part_ref.at[pl.ds(pl.multiple_of(other * half + h * own_rows, own_rows), own_rows)],
            dst_ref=near.at[h],
            send_sem=s1_send.at[h],
            recv_sem=s1_recv.at[h],
            device_id=(other, head, tok),
            device_id_type=mesh_ids,
        )

    def ring(kind, src, dst, target, send_sem, recv_sem):
        return pltpu.make_async_remote_copy(
            src_ref=src,
            dst_ref=dst,
            send_sem=send_sem.at[kind],
            recv_sem=recv_sem.at[kind],
            device_id=(section, target, tok),
            device_id_type=mesh_ids,
        )

    for h in range(head_count):
        near_copy(h).start()
    base = pl.multiple_of(section * half, own_rows)
    for h in range(head_count):
        near_copy(h).wait()

        @pl.when(h != head)
        def _pair():
            rows = pl.ds(pl.multiple_of(base + h * own_rows, own_rows), own_rows)
            mid[h] = (part_ref[rows, :].astype(jnp.float32) + near[h].astype(jnp.float32)).astype(
                mid.dtype
            )

    pass_a = ring(0, mid.at[opposite, low], land_a.at[0], up, r_send, r_recv)
    pass_b = ring(1, mid.at[opposite, high], land_b.at[0], down, r_send, r_recv)
    direct_a = ring(2, mid.at[down, low], land_a.at[1], down, r_send, r_recv)
    direct_b = ring(3, mid.at[up, high], land_b.at[1], up, r_send, r_recv)
    pass_a.start()
    pass_b.start()
    direct_a.start()
    direct_b.start()
    mine = pl.ds(pl.multiple_of(base + head * own_rows, own_rows), own_rows)
    acc[...] = part_ref[mine, :].astype(jnp.float32) + near[head].astype(jnp.float32)
    pass_a.wait()
    sums_a[...] = (mid[up, low].astype(jnp.float32) + land_a[0].astype(jnp.float32)).astype(
        sums_a.dtype
    )
    joined_a = ring(4, sums_a, land_a.at[2], up, r_send, r_recv)
    joined_a.start()
    pass_b.wait()
    sums_b[...] = (mid[down, high].astype(jnp.float32) + land_b[0].astype(jnp.float32)).astype(
        sums_b.dtype
    )
    joined_b = ring(5, sums_b, land_b.at[2], down, r_send, r_recv)
    joined_b.start()
    direct_a.wait()
    direct_b.wait()
    joined_a.wait()
    joined_b.wait()
    acc[low, :] += (
        land_a[1].astype(jnp.float32) + land_a[2].astype(jnp.float32)
    )
    acc[high, :] += (
        land_b[1].astype(jnp.float32) + land_b[2].astype(jnp.float32)
    )
    if not gather:
        out_ref[...] = acc[...]
        return
    result = (own_ref[...].astype(jnp.float32) + gate_ref[...] * acc[...]).astype(full_ref.dtype)
    full_ref[section, head] = result
    out_ref[...] = result

    def pass_copy(h):
        return pltpu.make_async_remote_copy(
            src_ref=full_ref.at[section, h],
            dst_ref=full_ref.at[section, h],
            send_sem=g2_send.at[h],
            recv_sem=g2_recv.at[h],
            device_id=(other, head, tok),
            device_id_type=mesh_ids,
        )

    to_up = ring(0, full_ref.at[section, head], full_ref.at[section, head], up, a_send, a_recv)
    to_down = ring(1, full_ref.at[section, head], full_ref.at[section, head], down, a_send, a_recv)
    to_up.start()
    to_down.start()
    pass_copy(head).start()
    to_up.wait()
    onward_a = ring(
        2, full_ref.at[section, down, low], full_ref.at[section, down, low], up, a_send, a_recv
    )
    onward_a.start()
    pass_copy(down).start()
    to_down.wait()
    onward_b = ring(
        3, full_ref.at[section, up, high], full_ref.at[section, up, high], down, a_send, a_recv
    )
    onward_b.start()
    pass_copy(up).start()
    onward_a.wait()
    onward_b.wait()
    pass_copy(opposite).start()
    pass_copy(head).wait()
    pass_copy(down).wait()
    pass_copy(up).wait()
    pass_copy(opposite).wait()


def exchange(partial, own_input, gate, layer_idx, gather, head_count, own_rows):
    rows, width = partial.shape
    half = head_count * own_rows
    split = (own_rows * 2 // 3) // 16 * 16
    vmem = pl.BlockSpec(memory_space=pltpu.VMEM)
    scratch = [
        pltpu.VMEM((head_count, own_rows, width), partial.dtype),
        pltpu.VMEM((head_count, own_rows, width), partial.dtype),
        pltpu.VMEM((3, split, width), partial.dtype),
        pltpu.VMEM((3, own_rows - split, width), partial.dtype),
        pltpu.VMEM((split, width), partial.dtype),
        pltpu.VMEM((own_rows - split, width), partial.dtype),
        pltpu.VMEM((own_rows, width), jnp.float32),
        pltpu.SemaphoreType.DMA((head_count,)),
        pltpu.SemaphoreType.DMA((head_count,)),
        pltpu.SemaphoreType.DMA((6,)),
        pltpu.SemaphoreType.DMA((6,)),
    ]
    if gather:
        out_shape = (
            jax.ShapeDtypeStruct((own_rows, width), jnp.bfloat16),
            jax.ShapeDtypeStruct((rows // half, head_count, own_rows, width), jnp.bfloat16),
        )
        out_specs = (vmem, vmem)
        scratch += [pltpu.SemaphoreType.DMA((head_count,))] * 4
    else:
        out_shape = jax.ShapeDtypeStruct((own_rows, width), jnp.float32)
        out_specs = vmem
    return pl.pallas_call(
        functools.partial(exchange_kernel, head_count, own_rows, split, gather),
        out_shape=out_shape,
        in_specs=[vmem, vmem, vmem],
        out_specs=out_specs,
        scratch_shapes=scratch,
        compiler_params=pltpu.CompilerParams(
            collective_id=layer_idx, has_side_effects=True, vmem_limit_bytes=48 * 1024 * 1024
        ),
    )(partial, own_input, gate.reshape(1, width))


def noise_level(position):
    time_left = 1.0 - position.astype(jnp.float32) / STEPS
    return time_shift * time_left / (1.0 + (time_shift - 1.0) * time_left)


def shards(
    hidden,
    latent,
    w_qkv,
    w_out,
    w_final,
    qk_gain,
    modulation,
    stale_kv,
    request_patches,
    patch_order,
    step_index,
):
    section_count = lax.axis_size("section")
    head_count = lax.axis_size("head")
    group_count = section_count * head_count
    section_index = lax.axis_index("section")
    head_index = lax.axis_index("head")
    tok_index = lax.axis_index("tok")
    group_index = section_index * head_count + head_index
    patch_len = hidden.shape[1]
    width = hidden.shape[2]
    head_dim = qk_gain.shape[-1]
    own_rows = patch_len // group_count
    layer_count = w_qkv.shape[0]
    request_of, offsets = slot_layout(request_patches, patch_order)
    slot_total = request_of.shape[0]
    my_request = request_of[tok_index]
    my_offset = offsets[tok_index]
    positions = (my_offset * patch_len + jnp.arange(patch_len, dtype=jnp.int32)).astype(jnp.float32)
    slot_ids = jnp.arange(slot_total, dtype=jnp.int32)
    allowed = (request_of == my_request) & (slot_ids != tok_index)
    marked = jnp.where(allowed, slot_ids, -1)
    running = lax.cummax(marked, axis=0)
    first_allowed = jnp.argmax(allowed).astype(jnp.int32)
    fetch = jnp.where(running >= 0, running, first_allowed).astype(jnp.int32)
    allow = allowed.astype(jnp.int32)
    stale_layers = [
        lax.all_gather(jnp.swapaxes(stale_kv[layer], 0, 1), "tok", axis=0, tiled=True)
        for layer in range(layer_count)
    ]
    current_full = hidden[0]
    own_input = lax.dynamic_slice_in_dim(current_full, group_index * own_rows, own_rows, 0)
    outputs = []
    for layer_idx in range(layer_count):
        queries, keys_fresh, values_fresh = project(
            current_full,
            modulation[layer_idx],
            w_qkv[layer_idx],
            qk_gain[layer_idx],
            positions,
            head_dim,
        )
        attended = attend(
            queries, keys_fresh, values_fresh, stale_layers[layer_idx], fetch, allow, head_dim
        )
        partial = jnp.dot(attended, w_out[layer_idx], preferred_element_type=jnp.float32).astype(
            jnp.bfloat16
        )
        gate = modulation[layer_idx, 2]
        if layer_idx + 1 < layer_count:
            own_out, gathered = exchange(
                partial, own_input, gate, layer_idx, True, head_count, own_rows
            )
            current_full = gathered.reshape(patch_len, width)
        else:
            summed = exchange(partial, own_input, gate, layer_idx, False, head_count, own_rows)
            own_out = (own_input.astype(jnp.float32) + gate * summed).astype(jnp.bfloat16)
        own_input = own_out
        outputs.append(own_out)
    last_own = outputs[-1]
    layer_out = jnp.stack(outputs)[:, None]
    normed = layer_norm(last_own.astype(jnp.float32)).astype(jnp.bfloat16)
    velocity = jnp.dot(normed, w_final, preferred_element_type=jnp.float32)[None]
    level_now = noise_level(step_index[0])
    level_next = noise_level(step_index[0] + 1)
    return (layer_out, latent + (level_next - level_now) * velocity, latent - level_now * velocity)


def solution(mesh):
    placed = (
        P("tok", None, None),
        P("tok", ("section", "head"), None),
        P(None, None, None, ("section", "head")),
        P(None, ("section", "head"), None),
        P(),
        P(),
        P(),
        P(None, None, "tok", None, ("section", "head")),
        P(),
        P(),
        P(),
    )
    return jax.shard_map(
        shards,
        mesh=mesh,
        in_specs=placed,
        out_specs=(
            P(None, "tok", ("section", "head"), None),
            P("tok", ("section", "head"), None),
            P("tok", ("section", "head"), None),
        ),
        check_vma=False,
    )
```

```python
import functools
import math

import jax
import jax.numpy as jnp
from jax import lax
from jax.experimental import pallas as pl
from jax.experimental.pallas import tpu as pltpu
from jax.sharding import PartitionSpec as P

STEPS = 28


norm_eps = 1e-06
time_shift = 3.0
rope_base = 10000.0


def layer_norm(inputs):
    average = jnp.mean(inputs, axis=-1, keepdims=True)
    centred = inputs - average
    variance = jnp.mean(centred * centred, axis=-1, keepdims=True)
    return centred * lax.rsqrt(variance + norm_eps)


def rms_norm(inputs, gains):
    return inputs * lax.rsqrt(jnp.mean(inputs * inputs, axis=-1, keepdims=True) + norm_eps) * gains


def rotate(inputs, positions):
    half_dim = inputs.shape[-1] // 2
    frequency = rope_base ** (-2.0 * jnp.arange(half_dim, dtype=jnp.float32) / inputs.shape[-1])
    angles = positions[..., None, None] * frequency
    pairs = inputs.reshape(inputs.shape[:-1] + (half_dim, 2))
    even_lane = pairs[..., 0]
    odd_lane = pairs[..., 1]
    cosine = jnp.cos(angles)
    sine = jnp.sin(angles)
    turned = jnp.stack(
        [even_lane * cosine - odd_lane * sine, even_lane * sine + odd_lane * cosine], axis=-1
    )
    return turned.reshape(inputs.shape)


def slot_layout(request_patches, patch_order):
    request_ends = jnp.cumsum(request_patches)
    starts = request_ends - request_patches
    request_of = jnp.sum((request_ends[None, :] <= patch_order[:, None]).astype(jnp.int32), axis=1)
    chosen = request_of[:, None] == jnp.arange(request_patches.shape[0], dtype=jnp.int32)[None, :]
    first_patch = jnp.sum(jnp.where(chosen, starts[None, :], 0), axis=1)
    return (request_of, patch_order - first_patch)


def project(inputs, layer_mod, weight, gains, positions, head_dim):
    normed = (layer_norm(inputs.astype(jnp.float32)) * (1.0 + layer_mod[1]) + layer_mod[0]).astype(
        jnp.bfloat16
    )
    rows = inputs.shape[0]
    column_count = weight.shape[2]
    heads = column_count // head_dim
    pieces = [
        jnp.dot(normed, weight[:, part, :], preferred_element_type=jnp.float32).reshape(
            rows, heads, head_dim
        )
        for part in range(3)
    ]
    queries = rotate(rms_norm(pieces[0], gains[0]), positions).astype(jnp.bfloat16)
    keys_fresh = rotate(rms_norm(pieces[1], gains[1]), positions).astype(jnp.bfloat16)
    values_fresh = pieces[2].astype(jnp.bfloat16)
    return (
        queries.reshape(rows, column_count),
        keys_fresh.reshape(rows, column_count),
        values_fresh.reshape(rows, column_count),
    )


def attention_kernel(
    head_dim, fetch_ref, allow_ref, q_ref, kf_ref, vf_ref, ks_ref, vs_ref, o_ref, qt_sc, m_sc, l_sc, acc_sc
):
    slot = pl.program_id(0)
    heads = q_ref.shape[1] // head_dim
    scaling = 1.0 / math.sqrt(head_dim)
    by_key = (((0,), (0,)), ((), ()))

    @pl.when(slot == 0)
    def _fresh():
        for h in range(heads):
            lanes = slice(h * head_dim, (h + 1) * head_dim)
            qt_sc[h] = q_ref[:, lanes].T
            scores = (
                jnp.dot(kf_ref[:, lanes], qt_sc[h], preferred_element_type=jnp.float32) * scaling
            )
            col_max = jnp.max(scores, axis=0, keepdims=True)
            weights = jnp.exp(scores - col_max)
            m_sc[h] = col_max
            l_sc[h] = jnp.sum(weights, axis=0, keepdims=True)
            acc_sc[h] = lax.dot_general(
                vf_ref[:, lanes], weights.astype(jnp.bfloat16), by_key,
                preferred_element_type=jnp.float32,
            )

    @pl.when(allow_ref[slot] != 0)
    def _stale():
        for h in range(heads):
            lanes = slice(h * head_dim, (h + 1) * head_dim)
            scores = (
                jnp.dot(ks_ref[:, lanes], qt_sc[h], preferred_element_type=jnp.float32) * scaling
            )
            old_max = m_sc[h]
            new_max = jnp.maximum(old_max, jnp.max(scores, axis=0, keepdims=True))
            factor = jnp.exp(old_max - new_max)
            weights = jnp.exp(scores - new_max)
            l_sc[h] = l_sc[h] * factor + jnp.sum(weights, axis=0, keepdims=True)
            acc_sc[h] = acc_sc[h] * factor + lax.dot_general(
                vs_ref[:, lanes], weights.astype(jnp.bfloat16), by_key,
                preferred_element_type=jnp.float32,
            )
            m_sc[h] = new_max

    @pl.when(slot == pl.num_programs(0) - 1)
    def _finish():
        for h in range(heads):
            lanes = slice(h * head_dim, (h + 1) * head_dim)
            o_ref[:, lanes] = (acc_sc[h] / l_sc[h]).T.astype(o_ref.dtype)


def attend(queries, keys_fresh, values_fresh, stale, fetch, allow, head_dim):
    rows, features = queries.shape
    slot_total = stale.shape[0]
    heads = features // head_dim
    whole = pl.BlockSpec((rows, features), lambda j, f, a: (0, 0))
    key_spec = pl.BlockSpec(
        (None, None, rows, features), lambda j, f, a: (f[j], 0, 0, 0)
    )
    value_spec = pl.BlockSpec(
        (None, None, rows, features), lambda j, f, a: (f[j], 1, 0, 0)
    )
    return pl.pallas_call(
        functools.partial(attention_kernel, head_dim),
        out_shape=jax.ShapeDtypeStruct((rows, features), jnp.bfloat16),
        grid_spec=pltpu.PrefetchScalarGridSpec(
            num_scalar_prefetch=2,
            grid=(slot_total,),
            in_specs=[whole, whole, whole, key_spec, value_spec],
            out_specs=whole,
            scratch_shapes=[
                pltpu.VMEM((heads, head_dim, rows), jnp.bfloat16),
                pltpu.VMEM((heads, 1, rows), jnp.float32),
                pltpu.VMEM((heads, 1, rows), jnp.float32),
                pltpu.VMEM((heads, head_dim, rows), jnp.float32),
            ],
        ),
        compiler_params=pltpu.CompilerParams(dimension_semantics=("arbitrary",)),
    )(fetch, allow, queries, keys_fresh, values_fresh, stale, stale)


def exchange_kernel(head_count, own_rows, split, gather, part_ref, own_ref, gate_ref, *rest):
    if gather:
        (out_ref, full_ref, near, mid, land_a, land_b, sums_a, sums_b, acc,
         s1_send, s1_recv, r_send, r_recv, a_send, a_recv, g2_send, g2_recv) = rest
    else:
        (out_ref, near, mid, land_a, land_b, sums_a, sums_b, acc,
         s1_send, s1_recv, r_send, r_recv) = rest
    mesh_ids = pl.DeviceIdType.MESH
    section = lax.axis_index("section")
    head = lax.axis_index("head")
    tok = lax.axis_index("tok")
    other = 1 - section
    half = head_count * own_rows
    up = lax.rem(head + 1, head_count)
    down = lax.rem(head + head_count - 1, head_count)
    opposite = lax.rem(head + 2, head_count)
    low = pl.ds(0, split)
    high = pl.ds(split, own_rows - split)

    barrier = pltpu.get_barrier_semaphore()
    pl.semaphore_signal(barrier, inc=1, device_id=(other, head, tok), device_id_type=mesh_ids)
    for h in range(head_count):
        @pl.when(h != head)
        def _greet():
            pl.semaphore_signal(barrier, inc=1, device_id=(section, h, tok), device_id_type=mesh_ids)
    pl.semaphore_wait(barrier, head_count)

    def near_copy(h):
        return pltpu.make_async_remote_copy(
            src_ref=part_ref.at[pl.ds(pl.multiple_of(other * half + h * own_rows, own_rows), own_rows)],
            dst_ref=near.at[h],
            send_sem=s1_send.at[h],
            recv_sem=s1_recv.at[h],
            device_id=(other, head, tok),
            device_id_type=mesh_ids,
        )

    def ring(kind, src, dst, target, send_sem, recv_sem):
        return pltpu.make_async_remote_copy(
            src_ref=src,
            dst_ref=dst,
            send_sem=send_sem.at[kind],
            recv_sem=recv_sem.at[kind],
            device_id=(section, target, tok),
            device_id_type=mesh_ids,
        )

    for h in range(head_count):
        near_copy(h).start()
    base = pl.multiple_of(section * half, own_rows)
    for h in range(head_count):
        near_copy(h).wait()

        @pl.when(h != head)
        def _pair():
            rows = pl.ds(pl.multiple_of(base + h * own_rows, own_rows), own_rows)
            mid[h] = (part_ref[rows, :].astype(jnp.float32) + near[h].astype(jnp.float32)).astype(
                mid.dtype
            )

    pass_a = ring(0, mid.at[opposite, low], land_a.at[0], up, r_send, r_recv)
    pass_b = ring(1, mid.at[opposite, high], land_b.at[0], down, r_send, r_recv)
    direct_a = ring(2, mid.at[down, low], land_a.at[1], down, r_send, r_recv)
    direct_b = ring(3, mid.at[up, high], land_b.at[1], up, r_send, r_recv)
    pass_a.start()
    pass_b.start()
    direct_a.start()
    direct_b.start()
    mine = pl.ds(pl.multiple_of(base + head * own_rows, own_rows), own_rows)
    acc[...] = part_ref[mine, :].astype(jnp.float32) + near[head].astype(jnp.float32)
    pass_a.wait()
    sums_a[...] = (mid[up, low].astype(jnp.float32) + land_a[0].astype(jnp.float32)).astype(
        sums_a.dtype
    )
    joined_a = ring(4, sums_a, land_a.at[2], up, r_send, r_recv)
    joined_a.start()
    pass_b.wait()
    sums_b[...] = (mid[down, high].astype(jnp.float32) + land_b[0].astype(jnp.float32)).astype(
        sums_b.dtype
    )
    joined_b = ring(5, sums_b, land_b.at[2], down, r_send, r_recv)
    joined_b.start()
    direct_a.wait()
    direct_b.wait()
    joined_a.wait()
    joined_b.wait()
    acc[low, :] += (
        land_a[1].astype(jnp.float32) + land_a[2].astype(jnp.float32)
    )
    acc[high, :] += (
        land_b[1].astype(jnp.float32) + land_b[2].astype(jnp.float32)
    )
    if not gather:
        out_ref[...] = acc[...]
        return
    result = (own_ref[...].astype(jnp.float32) + gate_ref[...] * acc[...]).astype(full_ref.dtype)
    full_ref[section, head] = result
    out_ref[...] = result

    def pass_copy(h):
        return pltpu.make_async_remote_copy(
            src_ref=full_ref.at[section, h],
            dst_ref=full_ref.at[section, h],
            send_sem=g2_send.at[h],
            recv_sem=g2_recv.at[h],
            device_id=(other, head, tok),
            device_id_type=mesh_ids,
        )

    to_up = ring(0, full_ref.at[section, head], full_ref.at[section, head], up, a_send, a_recv)
    to_down = ring(1, full_ref.at[section, head], full_ref.at[section, head], down, a_send, a_recv)
    to_up.start()
    to_down.start()
    pass_copy(head).start()
    to_up.wait()
    onward_a = ring(
        2, full_ref.at[section, down, low], full_ref.at[section, down, low], up, a_send, a_recv
    )
    onward_a.start()
    pass_copy(down).start()
    to_down.wait()
    onward_b = ring(
        3, full_ref.at[section, up, high], full_ref.at[section, up, high], down, a_send, a_recv
    )
    onward_b.start()
    pass_copy(up).start()
    onward_a.wait()
    onward_b.wait()
    pass_copy(opposite).start()
    pass_copy(head).wait()
    pass_copy(down).wait()
    pass_copy(up).wait()
    pass_copy(opposite).wait()


def exchange(partial, own_input, gate, layer_idx, gather, head_count, own_rows):
    rows, width = partial.shape
    half = head_count * own_rows
    split = (own_rows * 2 // 3) // 16 * 16
    vmem = pl.BlockSpec(memory_space=pltpu.VMEM)
    scratch = [
        pltpu.VMEM((head_count, own_rows, width), partial.dtype),
        pltpu.VMEM((head_count, own_rows, width), partial.dtype),
        pltpu.VMEM((3, split, width), partial.dtype),
        pltpu.VMEM((3, own_rows - split, width), partial.dtype),
        pltpu.VMEM((split, width), partial.dtype),
        pltpu.VMEM((own_rows - split, width), partial.dtype),
        pltpu.VMEM((own_rows, width), jnp.float32),
        pltpu.SemaphoreType.DMA((head_count,)),
        pltpu.SemaphoreType.DMA((head_count,)),
        pltpu.SemaphoreType.DMA((6,)),
        pltpu.SemaphoreType.DMA((6,)),
    ]
    if gather:
        out_shape = (
            jax.ShapeDtypeStruct((own_rows, width), jnp.bfloat16),
            jax.ShapeDtypeStruct((rows // half, head_count, own_rows, width), jnp.bfloat16),
        )
        out_specs = (vmem, vmem)
        scratch += [pltpu.SemaphoreType.DMA((head_count,))] * 4
    else:
        out_shape = jax.ShapeDtypeStruct((own_rows, width), jnp.float32)
        out_specs = vmem
    return pl.pallas_call(
        functools.partial(exchange_kernel, head_count, own_rows, split, gather),
        out_shape=out_shape,
        in_specs=[vmem, vmem, vmem],
        out_specs=out_specs,
        scratch_shapes=scratch,
        compiler_params=pltpu.CompilerParams(
            collective_id=layer_idx, has_side_effects=True, vmem_limit_bytes=48 * 1024 * 1024
        ),
    )(partial, own_input, gate.reshape(1, width))


def noise_level(position):
    time_left = 1.0 - position.astype(jnp.float32) / STEPS
    return time_shift * time_left / (1.0 + (time_shift - 1.0) * time_left)


def shards(
    hidden,
    latent,
    w_qkv,
    w_out,
    w_final,
    qk_gain,
    modulation,
    stale_kv,
    request_patches,
    patch_order,
    step_index,
):
    section_count = lax.axis_size("section")
    head_count = lax.axis_size("head")
    group_count = section_count * head_count
    section_index = lax.axis_index("section")
    head_index = lax.axis_index("head")
    tok_index = lax.axis_index("tok")
    group_index = section_index * head_count + head_index
    patch_len = hidden.shape[1]
    width = hidden.shape[2]
    head_dim = qk_gain.shape[-1]
    own_rows = patch_len // group_count
    layer_count = w_qkv.shape[0]
    request_of, offsets = slot_layout(request_patches, patch_order)
    slot_total = request_of.shape[0]
    my_request = request_of[tok_index]
    my_offset = offsets[tok_index]
    positions = (my_offset * patch_len + jnp.arange(patch_len, dtype=jnp.int32)).astype(jnp.float32)
    slot_ids = jnp.arange(slot_total, dtype=jnp.int32)
    allowed = (request_of == my_request) & (slot_ids != tok_index)
    marked = jnp.where(allowed, slot_ids, -1)
    running = lax.cummax(marked, axis=0)
    first_allowed = jnp.argmax(allowed).astype(jnp.int32)
    fetch = jnp.where(running >= 0, running, first_allowed).astype(jnp.int32)
    allow = allowed.astype(jnp.int32)
    stale_layers = [
        lax.all_gather(jnp.swapaxes(stale_kv[layer], 0, 1), "tok", axis=0, tiled=True)
        for layer in range(layer_count)
    ]
    current_full = hidden[0]
    own_input = lax.dynamic_slice_in_dim(current_full, group_index * own_rows, own_rows, 0)
    outputs = []
    for layer_idx in range(layer_count):
        queries, keys_fresh, values_fresh = project(
            current_full,
            modulation[layer_idx],
            w_qkv[layer_idx],
            qk_gain[layer_idx],
            positions,
            head_dim,
        )
        attended = attend(
            queries, keys_fresh, values_fresh, stale_layers[layer_idx], fetch, allow, head_dim
        )
        partial = jnp.dot(attended, w_out[layer_idx], preferred_element_type=jnp.float32).astype(
            jnp.bfloat16
        )
        gate = modulation[layer_idx, 2]
        if layer_idx + 1 < layer_count:
            own_out, gathered = exchange(
                partial, own_input, gate, layer_idx, True, head_count, own_rows
            )
            current_full = gathered.reshape(patch_len, width)
        else:
            summed = exchange(partial, own_input, gate, layer_idx, False, head_count, own_rows)
            own_out = (own_input.astype(jnp.float32) + gate * summed).astype(jnp.bfloat16)
        own_input = own_out
        outputs.append(own_out)
    last_own = outputs[-1]
    layer_out = jnp.stack(outputs)[:, None]
    normed = layer_norm(last_own.astype(jnp.float32)).astype(jnp.bfloat16)
    velocity = jnp.dot(normed, w_final, preferred_element_type=jnp.float32)[None]
    level_now = noise_level(step_index[0])
    level_next = noise_level(step_index[0] + 1)
    return (layer_out, latent + (level_next - level_now) * velocity, latent - level_now * velocity)


def solution(mesh):
    placed = (
        P("tok", None, None),
        P("tok", ("section", "head"), None),
        P(None, None, None, ("section", "head")),
        P(None, ("section", "head"), None),
        P(),
        P(),
        P(),
        P(None, None, "tok", None, ("section", "head")),
        P(),
        P(),
        P(),
    )
    return jax.shard_map(
        shards,
        mesh=mesh,
        in_specs=placed,
        out_specs=(
            P(None, "tok", ("section", "head"), None),
            P("tok", ("section", "head"), None),
            P("tok", ("section", "head"), None),
        ),
        check_vma=False,
    )
```

```python
import functools
import math

import jax
import jax.numpy as jnp
from jax import lax
from jax.experimental import pallas as pl
from jax.experimental.pallas import tpu as pltpu
from jax.sharding import PartitionSpec as P

STEPS = 28


norm_eps = 1e-06
time_shift = 3.0
rope_base = 10000.0


def layer_norm(inputs):
    average = jnp.mean(inputs, axis=-1, keepdims=True)
    centred = inputs - average
    variance = jnp.mean(centred * centred, axis=-1, keepdims=True)
    return centred * lax.rsqrt(variance + norm_eps)


def rms_norm(inputs, gains):
    return inputs * lax.rsqrt(jnp.mean(inputs * inputs, axis=-1, keepdims=True) + norm_eps) * gains


def rotate(inputs, positions):
    half_dim = inputs.shape[-1] // 2
    frequency = rope_base ** (-2.0 * jnp.arange(half_dim, dtype=jnp.float32) / inputs.shape[-1])
    angles = positions[..., None, None] * frequency
    pairs = inputs.reshape(inputs.shape[:-1] + (half_dim, 2))
    even_lane = pairs[..., 0]
    odd_lane = pairs[..., 1]
    cosine = jnp.cos(angles)
    sine = jnp.sin(angles)
    turned = jnp.stack(
        [even_lane * cosine - odd_lane * sine, even_lane * sine + odd_lane * cosine], axis=-1
    )
    return turned.reshape(inputs.shape)


def slot_layout(request_patches, patch_order):
    request_ends = jnp.cumsum(request_patches)
    starts = request_ends - request_patches
    request_of = jnp.sum((request_ends[None, :] <= patch_order[:, None]).astype(jnp.int32), axis=1)
    chosen = request_of[:, None] == jnp.arange(request_patches.shape[0], dtype=jnp.int32)[None, :]
    first_patch = jnp.sum(jnp.where(chosen, starts[None, :], 0), axis=1)
    return (request_of, patch_order - first_patch)


def project(inputs, layer_mod, weight, gains, positions, head_dim):
    normed = (layer_norm(inputs.astype(jnp.float32)) * (1.0 + layer_mod[1]) + layer_mod[0]).astype(
        jnp.bfloat16
    )
    rows = inputs.shape[0]
    column_count = weight.shape[2]
    heads = column_count // head_dim
    pieces = [
        jnp.dot(normed, weight[:, part, :], preferred_element_type=jnp.float32).reshape(
            rows, heads, head_dim
        )
        for part in range(3)
    ]
    queries = rotate(rms_norm(pieces[0], gains[0]), positions).astype(jnp.bfloat16)
    keys_fresh = rotate(rms_norm(pieces[1], gains[1]), positions).astype(jnp.bfloat16)
    values_fresh = pieces[2].astype(jnp.bfloat16)
    return (
        queries.reshape(rows, column_count),
        keys_fresh.reshape(rows, column_count),
        values_fresh.reshape(rows, column_count),
    )


def attention_kernel(
    head_dim, fetch_ref, allow_ref, q_ref, kf_ref, vf_ref, ks_ref, vs_ref, o_ref, qt_sc, m_sc, l_sc, acc_sc
):
    slot = pl.program_id(0)
    heads = q_ref.shape[1] // head_dim
    scaling = 1.0 / math.sqrt(head_dim)
    by_key = (((0,), (0,)), ((), ()))

    @pl.when(slot == 0)
    def _fresh():
        for h in range(heads):
            lanes = slice(h * head_dim, (h + 1) * head_dim)
            qt_sc[h] = q_ref[:, lanes].T
            scores = (
                jnp.dot(kf_ref[:, lanes], qt_sc[h], preferred_element_type=jnp.float32) * scaling
            )
            col_max = jnp.max(scores, axis=0, keepdims=True)
            weights = jnp.exp(scores - col_max)
            m_sc[h] = col_max
            l_sc[h] = jnp.sum(weights, axis=0, keepdims=True)
            acc_sc[h] = lax.dot_general(
                vf_ref[:, lanes], weights.astype(jnp.bfloat16), by_key,
                preferred_element_type=jnp.float32,
            )

    @pl.when(allow_ref[slot] != 0)
    def _stale():
        for h in range(heads):
            lanes = slice(h * head_dim, (h + 1) * head_dim)
            scores = (
                jnp.dot(ks_ref[:, lanes], qt_sc[h], preferred_element_type=jnp.float32) * scaling
            )
            old_max = m_sc[h]
            new_max = jnp.maximum(old_max, jnp.max(scores, axis=0, keepdims=True))
            factor = jnp.exp(old_max - new_max)
            weights = jnp.exp(scores - new_max)
            l_sc[h] = l_sc[h] * factor + jnp.sum(weights, axis=0, keepdims=True)
            acc_sc[h] = acc_sc[h] * factor + lax.dot_general(
                vs_ref[:, lanes], weights.astype(jnp.bfloat16), by_key,
                preferred_element_type=jnp.float32,
            )
            m_sc[h] = new_max

    @pl.when(slot == pl.num_programs(0) - 1)
    def _finish():
        for h in range(heads):
            lanes = slice(h * head_dim, (h + 1) * head_dim)
            o_ref[:, lanes] = (acc_sc[h] / l_sc[h]).T.astype(o_ref.dtype)


def attend(queries, keys_fresh, values_fresh, stale, fetch, allow, head_dim):
    rows, features = queries.shape
    slot_total = stale.shape[0]
    heads = features // head_dim
    whole = pl.BlockSpec((rows, features), lambda j, f, a: (0, 0))
    key_spec = pl.BlockSpec(
        (None, None, rows, features), lambda j, f, a: (f[j], 0, 0, 0)
    )
    value_spec = pl.BlockSpec(
        (None, None, rows, features), lambda j, f, a: (f[j], 1, 0, 0)
    )
    return pl.pallas_call(
        functools.partial(attention_kernel, head_dim),
        out_shape=jax.ShapeDtypeStruct((rows, features), jnp.bfloat16),
        grid_spec=pltpu.PrefetchScalarGridSpec(
            num_scalar_prefetch=2,
            grid=(slot_total,),
            in_specs=[whole, whole, whole, key_spec, value_spec],
            out_specs=whole,
            scratch_shapes=[
                pltpu.VMEM((heads, head_dim, rows), jnp.bfloat16),
                pltpu.VMEM((heads, 1, rows), jnp.float32),
                pltpu.VMEM((heads, 1, rows), jnp.float32),
                pltpu.VMEM((heads, head_dim, rows), jnp.float32),
            ],
        ),
        compiler_params=pltpu.CompilerParams(dimension_semantics=("arbitrary",)),
    )(fetch, allow, queries, keys_fresh, values_fresh, stale, stale)


def exchange_kernel(head_count, own_rows, split, gather, part_ref, own_ref, gate_ref, *rest):
    if gather:
        (out_ref, full_ref, land_a, land_b, sums_a, sums_b, acc,
         r_send, r_recv, a_send, a_recv, g2_send, g2_recv) = rest
    else:
        (out_ref, land_a, land_b, sums_a, sums_b, acc, r_send, r_recv) = rest
    mesh_ids = pl.DeviceIdType.MESH
    section = lax.axis_index("section")
    head = lax.axis_index("head")
    tok = lax.axis_index("tok")
    other = 1 - section
    up = lax.rem(head + 1, head_count)
    down = lax.rem(head + head_count - 1, head_count)
    opposite = lax.rem(head + 2, head_count)
    low = pl.ds(0, split)
    high = pl.ds(split, own_rows - split)

    def rows_of(block, offset, count):
        return pl.ds(pl.multiple_of(block * own_rows + offset, 16), count)

    barrier = pltpu.get_barrier_semaphore()
    pl.semaphore_signal(barrier, inc=1, device_id=(other, head, tok), device_id_type=mesh_ids)
    for h in range(head_count):
        @pl.when(h != head)
        def _greet():
            pl.semaphore_signal(barrier, inc=1, device_id=(section, h, tok), device_id_type=mesh_ids)
    pl.semaphore_wait(barrier, head_count)

    def ring(kind, src, dst, target, send_sem, recv_sem):
        return pltpu.make_async_remote_copy(
            src_ref=src,
            dst_ref=dst,
            send_sem=send_sem.at[kind],
            recv_sem=recv_sem.at[kind],
            device_id=(section, target, tok),
            device_id_type=mesh_ids,
        )

    low_count = split
    high_count = own_rows - split
    pass_a = ring(0, part_ref.at[rows_of(opposite, 0, low_count)], land_a.at[0], up, r_send, r_recv)
    pass_b = ring(1, part_ref.at[rows_of(opposite, split, high_count)], land_b.at[0], down, r_send, r_recv)
    direct_a = ring(2, part_ref.at[rows_of(down, 0, low_count)], land_a.at[1], down, r_send, r_recv)
    direct_b = ring(3, part_ref.at[rows_of(up, split, high_count)], land_b.at[1], up, r_send, r_recv)
    pass_a.start()
    pass_b.start()
    direct_a.start()
    direct_b.start()
    acc[...] = part_ref[rows_of(head, 0, own_rows), :].astype(jnp.float32)
    pass_a.wait()
    sums_a[...] = (
        part_ref[rows_of(up, 0, low_count), :].astype(jnp.float32) + land_a[0].astype(jnp.float32)
    ).astype(sums_a.dtype)
    joined_a = ring(4, sums_a, land_a.at[2], up, r_send, r_recv)
    joined_a.start()
    pass_b.wait()
    sums_b[...] = (
        part_ref[rows_of(down, split, high_count), :].astype(jnp.float32)
        + land_b[0].astype(jnp.float32)
    ).astype(sums_b.dtype)
    joined_b = ring(5, sums_b, land_b.at[2], down, r_send, r_recv)
    joined_b.start()
    direct_a.wait()
    direct_b.wait()
    joined_a.wait()
    joined_b.wait()
    acc[low, :] += land_a[1].astype(jnp.float32) + land_a[2].astype(jnp.float32)
    acc[high, :] += land_b[1].astype(jnp.float32) + land_b[2].astype(jnp.float32)
    if not gather:
        out_ref[...] = acc[...]
        return
    result = (own_ref[...].astype(jnp.float32) + gate_ref[...] * acc[...]).astype(full_ref.dtype)
    full_ref[section, head] = result
    out_ref[...] = result

    def pass_copy(h):
        return pltpu.make_async_remote_copy(
            src_ref=full_ref.at[section, h],
            dst_ref=full_ref.at[section, h],
            send_sem=g2_send.at[h],
            recv_sem=g2_recv.at[h],
            device_id=(other, head, tok),
            device_id_type=mesh_ids,
        )

    to_up = ring(0, full_ref.at[section, head], full_ref.at[section, head], up, a_send, a_recv)
    to_down = ring(1, full_ref.at[section, head], full_ref.at[section, head], down, a_send, a_recv)
    to_up.start()
    to_down.start()
    pass_copy(head).start()
    to_up.wait()
    onward_a = ring(
        2, full_ref.at[section, down, low], full_ref.at[section, down, low], up, a_send, a_recv
    )
    onward_a.start()
    pass_copy(down).start()
    to_down.wait()
    onward_b = ring(
        3, full_ref.at[section, up, high], full_ref.at[section, up, high], down, a_send, a_recv
    )
    onward_b.start()
    pass_copy(up).start()
    onward_a.wait()
    onward_b.wait()
    pass_copy(opposite).start()
    pass_copy(head).wait()
    pass_copy(down).wait()
    pass_copy(up).wait()
    pass_copy(opposite).wait()


def exchange(partial, own_input, gate, layer_idx, gather, head_count, own_rows):
    rows, width = partial.shape
    split = (own_rows * 2 // 3) // 16 * 16
    vmem = pl.BlockSpec(memory_space=pltpu.VMEM)
    scratch = [
        pltpu.VMEM((3, split, width), partial.dtype),
        pltpu.VMEM((3, own_rows - split, width), partial.dtype),
        pltpu.VMEM((split, width), partial.dtype),
        pltpu.VMEM((own_rows - split, width), partial.dtype),
        pltpu.VMEM((own_rows, width), jnp.float32),
        pltpu.SemaphoreType.DMA((6,)),
        pltpu.SemaphoreType.DMA((6,)),
    ]
    if gather:
        out_shape = (
            jax.ShapeDtypeStruct((own_rows, width), jnp.bfloat16),
            jax.ShapeDtypeStruct((2, head_count, own_rows, width), jnp.bfloat16),
        )
        out_specs = (vmem, vmem)
        scratch += [pltpu.SemaphoreType.DMA((head_count,))] * 4
    else:
        out_shape = jax.ShapeDtypeStruct((own_rows, width), jnp.float32)
        out_specs = vmem
    return pl.pallas_call(
        functools.partial(exchange_kernel, head_count, own_rows, split, gather),
        out_shape=out_shape,
        in_specs=[vmem, vmem, vmem],
        out_specs=out_specs,
        scratch_shapes=scratch,
        compiler_params=pltpu.CompilerParams(
            collective_id=layer_idx, has_side_effects=True, vmem_limit_bytes=48 * 1024 * 1024
        ),
    )(partial, own_input, gate.reshape(1, width))


def noise_level(position):
    time_left = 1.0 - position.astype(jnp.float32) / STEPS
    return time_shift * time_left / (1.0 + (time_shift - 1.0) * time_left)


def shards(
    hidden,
    latent,
    w_qkv,
    w_out,
    w_final,
    qk_gain,
    modulation,
    stale_kv,
    request_patches,
    patch_order,
    step_index,
):
    section_count = lax.axis_size("section")
    head_count = lax.axis_size("head")
    group_count = section_count * head_count
    section_index = lax.axis_index("section")
    head_index = lax.axis_index("head")
    tok_index = lax.axis_index("tok")
    group_index = section_index * head_count + head_index
    patch_len = hidden.shape[1]
    width = hidden.shape[2]
    head_dim = qk_gain.shape[-1]
    own_rows = patch_len // group_count
    layer_count = w_qkv.shape[0]
    request_of, offsets = slot_layout(request_patches, patch_order)
    slot_total = request_of.shape[0]
    my_request = request_of[tok_index]
    my_offset = offsets[tok_index]
    positions = (my_offset * patch_len + jnp.arange(patch_len, dtype=jnp.int32)).astype(jnp.float32)
    slot_ids = jnp.arange(slot_total, dtype=jnp.int32)
    allowed = (request_of == my_request) & (slot_ids != tok_index)
    marked = jnp.where(allowed, slot_ids, -1)
    running = lax.cummax(marked, axis=0)
    first_allowed = jnp.argmax(allowed).astype(jnp.int32)
    fetch = jnp.where(running >= 0, running, first_allowed).astype(jnp.int32)
    allow = allowed.astype(jnp.int32)
    stale_layers = [
        lax.all_gather(jnp.swapaxes(stale_kv[layer], 0, 1), "tok", axis=0, tiled=True)
        for layer in range(layer_count)
    ]
    current_full = hidden[0]
    w_partner = lax.ppermute(w_out, "section", perm=[(0, 1), (1, 0)])
    own_input = lax.dynamic_slice_in_dim(current_full, group_index * own_rows, own_rows, 0)
    outputs = []
    for layer_idx in range(layer_count):
        queries, keys_fresh, values_fresh = project(
            current_full,
            modulation[layer_idx],
            w_qkv[layer_idx],
            qk_gain[layer_idx],
            positions,
            head_dim,
        )
        attended = attend(
            queries, keys_fresh, values_fresh, stale_layers[layer_idx], fetch, allow, head_dim
        )
        half_rows = patch_len // section_count
        mine = lax.dynamic_slice_in_dim(attended, section_index * half_rows, half_rows, 0)
        theirs = lax.dynamic_slice_in_dim(attended, (1 - section_index) * half_rows, half_rows, 0)
        swapped = lax.ppermute(theirs, "section", perm=[(0, 1), (1, 0)])
        partial = (
            jnp.dot(mine, w_out[layer_idx], preferred_element_type=jnp.float32)
            + jnp.dot(swapped, w_partner[layer_idx], preferred_element_type=jnp.float32)
        ).astype(jnp.bfloat16)
        gate = modulation[layer_idx, 2]
        if layer_idx + 1 < layer_count:
            own_out, gathered = exchange(
                partial, own_input, gate, layer_idx, True, head_count, own_rows
            )
            current_full = gathered.reshape(patch_len, width)
        else:
            summed = exchange(partial, own_input, gate, layer_idx, False, head_count, own_rows)
            own_out = (own_input.astype(jnp.float32) + gate * summed).astype(jnp.bfloat16)
        own_input = own_out
        outputs.append(own_out)
    last_own = outputs[-1]
    layer_out = jnp.stack(outputs)[:, None]
    normed = layer_norm(last_own.astype(jnp.float32)).astype(jnp.bfloat16)
    velocity = jnp.dot(normed, w_final, preferred_element_type=jnp.float32)[None]
    level_now = noise_level(step_index[0])
    level_next = noise_level(step_index[0] + 1)
    return (layer_out, latent + (level_next - level_now) * velocity, latent - level_now * velocity)


def solution(mesh):
    placed = (
        P("tok", None, None),
        P("tok", ("section", "head"), None),
        P(None, None, None, ("section", "head")),
        P(None, ("section", "head"), None),
        P(),
        P(),
        P(),
        P(None, None, "tok", None, ("section", "head")),
        P(),
        P(),
        P(),
    )
    return jax.shard_map(
        shards,
        mesh=mesh,
        in_specs=placed,
        out_specs=(
            P(None, "tok", ("section", "head"), None),
            P("tok", ("section", "head"), None),
            P("tok", ("section", "head"), None),
        ),
        check_vma=False,
    )
```

```python
import functools
import math

import jax
import jax.numpy as jnp
from jax import lax
from jax.experimental import pallas as pl
from jax.experimental.pallas import tpu as pltpu
from jax.sharding import PartitionSpec as P

STEPS = 28
MOST = 8


norm_eps = 1e-06
time_shift = 3.0
rope_base = 10000.0


def layer_norm(inputs):
    average = jnp.mean(inputs, axis=-1, keepdims=True)
    centred = inputs - average
    variance = jnp.mean(centred * centred, axis=-1, keepdims=True)
    return centred * lax.rsqrt(variance + norm_eps)


def rms_norm(inputs, gains):
    return inputs * lax.rsqrt(jnp.mean(inputs * inputs, axis=-1, keepdims=True) + norm_eps) * gains


def rotate(inputs, positions):
    half_dim = inputs.shape[-1] // 2
    frequency = rope_base ** (-2.0 * jnp.arange(half_dim, dtype=jnp.float32) / inputs.shape[-1])
    angles = positions[..., None, None] * frequency
    pairs = inputs.reshape(inputs.shape[:-1] + (half_dim, 2))
    even_lane = pairs[..., 0]
    odd_lane = pairs[..., 1]
    cosine = jnp.cos(angles)
    sine = jnp.sin(angles)
    turned = jnp.stack(
        [even_lane * cosine - odd_lane * sine, even_lane * sine + odd_lane * cosine], axis=-1
    )
    return turned.reshape(inputs.shape)


def slot_layout(request_patches, patch_order):
    request_ends = jnp.cumsum(request_patches)
    starts = request_ends - request_patches
    request_of = jnp.sum((request_ends[None, :] <= patch_order[:, None]).astype(jnp.int32), axis=1)
    chosen = request_of[:, None] == jnp.arange(request_patches.shape[0], dtype=jnp.int32)[None, :]
    first_patch = jnp.sum(jnp.where(chosen, starts[None, :], 0), axis=1)
    return (request_of, patch_order - first_patch)


def project(inputs, layer_mod, weight, gains, positions, head_dim):
    normed = (layer_norm(inputs.astype(jnp.float32)) * (1.0 + layer_mod[1]) + layer_mod[0]).astype(
        jnp.bfloat16
    )
    rows = inputs.shape[0]
    column_count = weight.shape[2]
    heads = column_count // head_dim
    pieces = [
        jnp.dot(normed, weight[:, part, :], preferred_element_type=jnp.float32).reshape(
            rows, heads, head_dim
        )
        for part in range(3)
    ]
    queries = rotate(rms_norm(pieces[0], gains[0]), positions).astype(jnp.bfloat16)
    keys_fresh = rotate(rms_norm(pieces[1], gains[1]), positions).astype(jnp.bfloat16)
    values_fresh = pieces[2].astype(jnp.bfloat16)
    return (
        queries.reshape(rows, column_count),
        keys_fresh.reshape(rows, column_count),
        values_fresh.reshape(rows, column_count),
    )


def attention_kernel(
    head_dim, fetch_ref, allow_ref, q_ref, kf_ref, vf_ref, ks_ref, vs_ref, o_ref, qt_sc, m_sc, l_sc, acc_sc
):
    slot = pl.program_id(0)
    heads = q_ref.shape[1] // head_dim
    scaling = 1.0 / math.sqrt(head_dim)
    by_key = (((0,), (0,)), ((), ()))

    @pl.when(slot == 0)
    def _fresh():
        for h in range(heads):
            lanes = slice(h * head_dim, (h + 1) * head_dim)
            qt_sc[h] = q_ref[:, lanes].T
            scores = (
                jnp.dot(kf_ref[:, lanes], qt_sc[h], preferred_element_type=jnp.float32) * scaling
            )
            col_max = jnp.max(scores, axis=0, keepdims=True)
            weights = jnp.exp(scores - col_max)
            m_sc[h] = col_max
            l_sc[h] = jnp.sum(weights, axis=0, keepdims=True)
            acc_sc[h] = lax.dot_general(
                vf_ref[:, lanes], weights.astype(jnp.bfloat16), by_key,
                preferred_element_type=jnp.float32,
            )

    @pl.when(allow_ref[slot] != 0)
    def _stale():
        for h in range(heads):
            lanes = slice(h * head_dim, (h + 1) * head_dim)
            scores = (
                jnp.dot(ks_ref[:, lanes], qt_sc[h], preferred_element_type=jnp.float32) * scaling
            )
            old_max = m_sc[h]
            new_max = jnp.maximum(old_max, jnp.max(scores, axis=0, keepdims=True))
            factor = jnp.exp(old_max - new_max)
            weights = jnp.exp(scores - new_max)
            l_sc[h] = l_sc[h] * factor + jnp.sum(weights, axis=0, keepdims=True)
            acc_sc[h] = acc_sc[h] * factor + lax.dot_general(
                vs_ref[:, lanes], weights.astype(jnp.bfloat16), by_key,
                preferred_element_type=jnp.float32,
            )
            m_sc[h] = new_max

    @pl.when(slot == pl.num_programs(0) - 1)
    def _finish():
        for h in range(heads):
            lanes = slice(h * head_dim, (h + 1) * head_dim)
            o_ref[:, lanes] = (acc_sc[h] / l_sc[h]).T.astype(o_ref.dtype)


def attend(queries, keys_fresh, values_fresh, stale, fetch, allow, head_dim):
    rows, features = queries.shape
    slot_total = fetch.shape[0]
    heads = features // head_dim
    whole = pl.BlockSpec((rows, features), lambda j, f, a: (0, 0))
    key_spec = pl.BlockSpec(
        (None, None, rows, features), lambda j, f, a: (f[j], 0, 0, 0)
    )
    value_spec = pl.BlockSpec(
        (None, None, rows, features), lambda j, f, a: (f[j], 1, 0, 0)
    )
    return pl.pallas_call(
        functools.partial(attention_kernel, head_dim),
        out_shape=jax.ShapeDtypeStruct((rows, features), jnp.bfloat16),
        grid_spec=pltpu.PrefetchScalarGridSpec(
            num_scalar_prefetch=2,
            grid=(slot_total,),
            in_specs=[whole, whole, whole, key_spec, value_spec],
            out_specs=whole,
            scratch_shapes=[
                pltpu.VMEM((heads, head_dim, rows), jnp.bfloat16),
                pltpu.VMEM((heads, 1, rows), jnp.float32),
                pltpu.VMEM((heads, 1, rows), jnp.float32),
                pltpu.VMEM((heads, head_dim, rows), jnp.float32),
            ],
        ),
        compiler_params=pltpu.CompilerParams(dimension_semantics=("arbitrary",)),
    )(fetch, allow, queries, keys_fresh, values_fresh, stale, stale)


def exchange_kernel(head_count, own_rows, split, gather, part_ref, own_ref, gate_ref, *rest):
    if gather:
        (out_ref, full_ref, land_a, land_b, sums_a, sums_b, acc,
         r_send, r_recv, a_send, a_recv, g2_send, g2_recv) = rest
    else:
        (out_ref, land_a, land_b, sums_a, sums_b, acc, r_send, r_recv) = rest
    mesh_ids = pl.DeviceIdType.MESH
    section = lax.axis_index("section")
    head = lax.axis_index("head")
    tok = lax.axis_index("tok")
    other = 1 - section
    up = lax.rem(head + 1, head_count)
    down = lax.rem(head + head_count - 1, head_count)
    opposite = lax.rem(head + 2, head_count)
    low = pl.ds(0, split)
    high = pl.ds(split, own_rows - split)

    def rows_of(block, offset, count):
        return pl.ds(pl.multiple_of(block * own_rows + offset, 16), count)

    barrier = pltpu.get_barrier_semaphore()
    pl.semaphore_signal(barrier, inc=1, device_id=(other, head, tok), device_id_type=mesh_ids)
    for h in range(head_count):
        @pl.when(h != head)
        def _greet():
            pl.semaphore_signal(barrier, inc=1, device_id=(section, h, tok), device_id_type=mesh_ids)
    pl.semaphore_wait(barrier, head_count)

    def ring(kind, src, dst, target, send_sem, recv_sem):
        return pltpu.make_async_remote_copy(
            src_ref=src,
            dst_ref=dst,
            send_sem=send_sem.at[kind],
            recv_sem=recv_sem.at[kind],
            device_id=(section, target, tok),
            device_id_type=mesh_ids,
        )

    low_count = split
    high_count = own_rows - split
    pass_a = ring(0, part_ref.at[rows_of(opposite, 0, low_count)], land_a.at[0], up, r_send, r_recv)
    pass_b = ring(1, part_ref.at[rows_of(opposite, split, high_count)], land_b.at[0], down, r_send, r_recv)
    direct_a = ring(2, part_ref.at[rows_of(down, 0, low_count)], land_a.at[1], down, r_send, r_recv)
    direct_b = ring(3, part_ref.at[rows_of(up, split, high_count)], land_b.at[1], up, r_send, r_recv)
    pass_a.start()
    pass_b.start()
    direct_a.start()
    direct_b.start()
    acc[...] = part_ref[rows_of(head, 0, own_rows), :].astype(jnp.float32)
    pass_a.wait()
    sums_a[...] = (
        part_ref[rows_of(up, 0, low_count), :].astype(jnp.float32) + land_a[0].astype(jnp.float32)
    ).astype(sums_a.dtype)
    joined_a = ring(4, sums_a, land_a.at[2], up, r_send, r_recv)
    joined_a.start()
    pass_b.wait()
    sums_b[...] = (
        part_ref[rows_of(down, split, high_count), :].astype(jnp.float32)
        + land_b[0].astype(jnp.float32)
    ).astype(sums_b.dtype)
    joined_b = ring(5, sums_b, land_b.at[2], down, r_send, r_recv)
    joined_b.start()
    direct_a.wait()
    direct_b.wait()
    joined_a.wait()
    joined_b.wait()
    acc[low, :] += land_a[1].astype(jnp.float32) + land_a[2].astype(jnp.float32)
    acc[high, :] += land_b[1].astype(jnp.float32) + land_b[2].astype(jnp.float32)
    if not gather:
        out_ref[...] = acc[...]
        return
    result = (own_ref[...].astype(jnp.float32) + gate_ref[...] * acc[...]).astype(full_ref.dtype)
    full_ref[section, head] = result
    out_ref[...] = result

    def pass_copy(h):
        return pltpu.make_async_remote_copy(
            src_ref=full_ref.at[section, h],
            dst_ref=full_ref.at[section, h],
            send_sem=g2_send.at[h],
            recv_sem=g2_recv.at[h],
            device_id=(other, head, tok),
            device_id_type=mesh_ids,
        )

    to_up = ring(0, full_ref.at[section, head], full_ref.at[section, head], up, a_send, a_recv)
    to_down = ring(1, full_ref.at[section, head], full_ref.at[section, head], down, a_send, a_recv)
    to_up.start()
    to_down.start()
    pass_copy(head).start()
    to_up.wait()
    onward_a = ring(
        2, full_ref.at[section, down, low], full_ref.at[section, down, low], up, a_send, a_recv
    )
    onward_a.start()
    pass_copy(down).start()
    to_down.wait()
    onward_b = ring(
        3, full_ref.at[section, up, high], full_ref.at[section, up, high], down, a_send, a_recv
    )
    onward_b.start()
    pass_copy(up).start()
    onward_a.wait()
    onward_b.wait()
    pass_copy(opposite).start()
    pass_copy(head).wait()
    pass_copy(down).wait()
    pass_copy(up).wait()
    pass_copy(opposite).wait()


def exchange(partial, own_input, gate, layer_idx, gather, head_count, own_rows):
    rows, width = partial.shape
    split = (own_rows * 2 // 3) // 16 * 16
    vmem = pl.BlockSpec(memory_space=pltpu.VMEM)
    scratch = [
        pltpu.VMEM((3, split, width), partial.dtype),
        pltpu.VMEM((3, own_rows - split, width), partial.dtype),
        pltpu.VMEM((split, width), partial.dtype),
        pltpu.VMEM((own_rows - split, width), partial.dtype),
        pltpu.VMEM((own_rows, width), jnp.float32),
        pltpu.SemaphoreType.DMA((6,)),
        pltpu.SemaphoreType.DMA((6,)),
    ]
    if gather:
        out_shape = (
            jax.ShapeDtypeStruct((own_rows, width), jnp.bfloat16),
            jax.ShapeDtypeStruct((2, head_count, own_rows, width), jnp.bfloat16),
        )
        out_specs = (vmem, vmem)
        scratch += [pltpu.SemaphoreType.DMA((head_count,))] * 4
    else:
        out_shape = jax.ShapeDtypeStruct((own_rows, width), jnp.float32)
        out_specs = vmem
    return pl.pallas_call(
        functools.partial(exchange_kernel, head_count, own_rows, split, gather),
        out_shape=out_shape,
        in_specs=[vmem, vmem, vmem],
        out_specs=out_specs,
        scratch_shapes=scratch,
        compiler_params=pltpu.CompilerParams(
            collective_id=layer_idx, has_side_effects=True, vmem_limit_bytes=48 * 1024 * 1024
        ),
    )(partial, own_input, gate.reshape(1, width))


def noise_level(position):
    time_left = 1.0 - position.astype(jnp.float32) / STEPS
    return time_shift * time_left / (1.0 + (time_shift - 1.0) * time_left)


def shards(
    hidden,
    latent,
    w_qkv,
    w_out,
    w_final,
    qk_gain,
    modulation,
    stale_kv,
    request_patches,
    patch_order,
    step_index,
):
    section_count = lax.axis_size("section")
    head_count = lax.axis_size("head")
    group_count = section_count * head_count
    section_index = lax.axis_index("section")
    head_index = lax.axis_index("head")
    tok_index = lax.axis_index("tok")
    group_index = section_index * head_count + head_index
    patch_len = hidden.shape[1]
    width = hidden.shape[2]
    head_dim = qk_gain.shape[-1]
    own_rows = patch_len // group_count
    layer_count = w_qkv.shape[0]
    request_of, offsets = slot_layout(request_patches, patch_order)
    slot_total = request_of.shape[0]
    my_request = request_of[tok_index]
    my_offset = offsets[tok_index]
    positions = (my_offset * patch_len + jnp.arange(patch_len, dtype=jnp.int32)).astype(jnp.float32)
    slot_ids = jnp.arange(slot_total, dtype=jnp.int32)
    allowed = (request_of == my_request) & (slot_ids != tok_index)
    rank = jnp.cumsum(allowed.astype(jnp.int32)) - 1
    count = jnp.sum(allowed.astype(jnp.int32))
    step_ids = jnp.arange(MOST - 1, dtype=jnp.int32)
    picked = allowed[None, :] & (rank[None, :] == step_ids[:, None])
    compact = jnp.sum(jnp.where(picked, slot_ids[None, :], 0), axis=1)
    last_pick = jnp.sum(jnp.where(allowed & (rank == count - 1), slot_ids, 0))
    fetch = jnp.where(step_ids < count, compact, last_pick).astype(jnp.int32)
    allow = (step_ids < count).astype(jnp.int32)
    stale_layers = [
        lax.all_gather(jnp.swapaxes(stale_kv[layer], 0, 1), "tok", axis=0, tiled=True)
        for layer in range(layer_count)
    ]
    current_full = hidden[0]
    w_partner = lax.ppermute(w_out, "section", perm=[(0, 1), (1, 0)])
    own_input = lax.dynamic_slice_in_dim(current_full, group_index * own_rows, own_rows, 0)
    outputs = []
    for layer_idx in range(layer_count):
        queries, keys_fresh, values_fresh = project(
            current_full,
            modulation[layer_idx],
            w_qkv[layer_idx],
            qk_gain[layer_idx],
            positions,
            head_dim,
        )
        attended = attend(
            queries, keys_fresh, values_fresh, stale_layers[layer_idx], fetch, allow, head_dim
        )
        half_rows = patch_len // section_count
        mine = lax.dynamic_slice_in_dim(attended, section_index * half_rows, half_rows, 0)
        theirs = lax.dynamic_slice_in_dim(attended, (1 - section_index) * half_rows, half_rows, 0)
        swapped = lax.ppermute(theirs, "section", perm=[(0, 1), (1, 0)])
        partial = (
            jnp.dot(mine, w_out[layer_idx], preferred_element_type=jnp.float32)
            + jnp.dot(swapped, w_partner[layer_idx], preferred_element_type=jnp.float32)
        ).astype(jnp.bfloat16)
        gate = modulation[layer_idx, 2]
        if layer_idx + 1 < layer_count:
            own_out, gathered = exchange(
                partial, own_input, gate, layer_idx, True, head_count, own_rows
            )
            current_full = gathered.reshape(patch_len, width)
        else:
            summed = exchange(partial, own_input, gate, layer_idx, False, head_count, own_rows)
            own_out = (own_input.astype(jnp.float32) + gate * summed).astype(jnp.bfloat16)
        own_input = own_out
        outputs.append(own_out)
    last_own = outputs[-1]
    layer_out = jnp.stack(outputs)[:, None]
    normed = layer_norm(last_own.astype(jnp.float32)).astype(jnp.bfloat16)
    velocity = jnp.dot(normed, w_final, preferred_element_type=jnp.float32)[None]
    level_now = noise_level(step_index[0])
    level_next = noise_level(step_index[0] + 1)
    return (layer_out, latent + (level_next - level_now) * velocity, latent - level_now * velocity)


def solution(mesh):
    placed = (
        P("tok", None, None),
        P("tok", ("section", "head"), None),
        P(None, None, None, ("section", "head")),
        P(None, ("section", "head"), None),
        P(),
        P(),
        P(),
        P(None, None, "tok", None, ("section", "head")),
        P(),
        P(),
        P(),
    )
    return jax.shard_map(
        shards,
        mesh=mesh,
        in_specs=placed,
        out_specs=(
            P(None, "tok", ("section", "head"), None),
            P("tok", ("section", "head"), None),
            P("tok", ("section", "head"), None),
        ),
        check_vma=False,
    )
```

```python
import functools
import math

import jax
import jax.numpy as jnp
from jax import lax
from jax.experimental import pallas as pl
from jax.experimental.pallas import tpu as pltpu
from jax.sharding import PartitionSpec as P

STEPS = 28
MOST = 8


norm_eps = 1e-06
time_shift = 3.0
rope_base = 10000.0


def layer_norm(inputs):
    average = jnp.mean(inputs, axis=-1, keepdims=True)
    centred = inputs - average
    variance = jnp.mean(centred * centred, axis=-1, keepdims=True)
    return centred * lax.rsqrt(variance + norm_eps)


def rms_norm(inputs, gains):
    return inputs * lax.rsqrt(jnp.mean(inputs * inputs, axis=-1, keepdims=True) + norm_eps) * gains


def rotate(inputs, positions):
    half_dim = inputs.shape[-1] // 2
    frequency = rope_base ** (-2.0 * jnp.arange(half_dim, dtype=jnp.float32) / inputs.shape[-1])
    angles = positions[..., None, None] * frequency
    pairs = inputs.reshape(inputs.shape[:-1] + (half_dim, 2))
    even_lane = pairs[..., 0]
    odd_lane = pairs[..., 1]
    cosine = jnp.cos(angles)
    sine = jnp.sin(angles)
    turned = jnp.stack(
        [even_lane * cosine - odd_lane * sine, even_lane * sine + odd_lane * cosine], axis=-1
    )
    return turned.reshape(inputs.shape)


def slot_layout(request_patches, patch_order):
    request_ends = jnp.cumsum(request_patches)
    starts = request_ends - request_patches
    request_of = jnp.sum((request_ends[None, :] <= patch_order[:, None]).astype(jnp.int32), axis=1)
    chosen = request_of[:, None] == jnp.arange(request_patches.shape[0], dtype=jnp.int32)[None, :]
    first_patch = jnp.sum(jnp.where(chosen, starts[None, :], 0), axis=1)
    return (request_of, patch_order - first_patch)


def project(inputs, layer_mod, weight, gains, positions, head_dim):
    normed = (layer_norm(inputs.astype(jnp.float32)) * (1.0 + layer_mod[1]) + layer_mod[0]).astype(
        jnp.bfloat16
    )
    rows = inputs.shape[0]
    column_count = weight.shape[2]
    heads = column_count // head_dim
    pieces = [
        jnp.dot(normed, weight[:, part, :], preferred_element_type=jnp.float32).reshape(
            rows, heads, head_dim
        )
        for part in range(3)
    ]
    queries = rotate(rms_norm(pieces[0], gains[0]), positions).astype(jnp.bfloat16)
    keys_fresh = rotate(rms_norm(pieces[1], gains[1]), positions).astype(jnp.bfloat16)
    values_fresh = pieces[2].astype(jnp.bfloat16)
    return (
        queries.reshape(rows, column_count),
        keys_fresh.reshape(rows, column_count),
        values_fresh.reshape(rows, column_count),
    )


def attention_kernel(
    head_dim, fetch_ref, allow_ref, q_ref, kf_ref, vf_ref, ks_ref, vs_ref, o_ref, qt_sc, m_sc, l_sc, acc_sc
):
    slot = pl.program_id(0)
    heads = q_ref.shape[1] // head_dim
    scaling = 1.0 / math.sqrt(head_dim)
    by_key = (((0,), (0,)), ((), ()))

    @pl.when(slot == 0)
    def _fresh():
        for h in range(heads):
            lanes = slice(h * head_dim, (h + 1) * head_dim)
            qt_sc[h] = q_ref[:, lanes].T
            scores = (
                jnp.dot(kf_ref[:, lanes], qt_sc[h], preferred_element_type=jnp.float32) * scaling
            )
            col_max = jnp.max(scores, axis=0, keepdims=True)
            weights = jnp.exp(scores - col_max)
            m_sc[h] = col_max
            l_sc[h] = jnp.sum(weights, axis=0, keepdims=True)
            acc_sc[h] = lax.dot_general(
                vf_ref[:, lanes], weights.astype(jnp.bfloat16), by_key,
                preferred_element_type=jnp.float32,
            )

    @pl.when(allow_ref[slot] != 0)
    def _stale():
        for h in range(heads):
            lanes = slice(h * head_dim, (h + 1) * head_dim)
            scores = (
                jnp.dot(ks_ref[:, lanes], qt_sc[h], preferred_element_type=jnp.float32) * scaling
            )
            old_max = m_sc[h]
            new_max = jnp.maximum(old_max, jnp.max(scores, axis=0, keepdims=True))
            factor = jnp.exp(old_max - new_max)
            weights = jnp.exp(scores - new_max)
            l_sc[h] = l_sc[h] * factor + jnp.sum(weights, axis=0, keepdims=True)
            acc_sc[h] = acc_sc[h] * factor + lax.dot_general(
                vs_ref[:, lanes], weights.astype(jnp.bfloat16), by_key,
                preferred_element_type=jnp.float32,
            )
            m_sc[h] = new_max

    @pl.when(slot == pl.num_programs(0) - 1)
    def _finish():
        for h in range(heads):
            lanes = slice(h * head_dim, (h + 1) * head_dim)
            o_ref[:, lanes] = (acc_sc[h] / l_sc[h]).T.astype(o_ref.dtype)


def attend(queries, keys_fresh, values_fresh, stale, fetch, allow, head_dim):
    rows, features = queries.shape
    slot_total = fetch.shape[0]
    heads = features // head_dim
    whole = pl.BlockSpec((rows, features), lambda j, f, a: (0, 0))
    key_spec = pl.BlockSpec(
        (None, None, rows, features), lambda j, f, a: (f[j], 0, 0, 0)
    )
    value_spec = pl.BlockSpec(
        (None, None, rows, features), lambda j, f, a: (f[j], 1, 0, 0)
    )
    return pl.pallas_call(
        functools.partial(attention_kernel, head_dim),
        out_shape=jax.ShapeDtypeStruct((rows, features), jnp.bfloat16),
        grid_spec=pltpu.PrefetchScalarGridSpec(
            num_scalar_prefetch=2,
            grid=(slot_total,),
            in_specs=[whole, whole, whole, key_spec, value_spec],
            out_specs=whole,
            scratch_shapes=[
                pltpu.VMEM((heads, head_dim, rows), jnp.bfloat16),
                pltpu.VMEM((heads, 1, rows), jnp.float32),
                pltpu.VMEM((heads, 1, rows), jnp.float32),
                pltpu.VMEM((heads, head_dim, rows), jnp.float32),
            ],
        ),
        compiler_params=pltpu.CompilerParams(dimension_semantics=("arbitrary",)),
    )(fetch, allow, queries, keys_fresh, values_fresh, stale, stale)


def exchange_kernel(
    head_count, own_rows, split, gather, mine_ref, theirs_ref, w_ref, wp_ref, own_ref, gate_ref, *rest
):
    if gather:
        (out_ref, full_ref, part_ref, land_a, land_b, sums_a, sums_b, acc,
         r_send, r_recv, a_send, a_recv, g2_send, g2_recv) = rest
    else:
        (out_ref, part_ref, land_a, land_b, sums_a, sums_b, acc, r_send, r_recv) = rest
    mesh_ids = pl.DeviceIdType.MESH
    section = lax.axis_index("section")
    head = lax.axis_index("head")
    tok = lax.axis_index("tok")
    other = 1 - section
    up = lax.rem(head + 1, head_count)
    down = lax.rem(head + head_count - 1, head_count)
    opposite = lax.rem(head + 2, head_count)
    low = pl.ds(0, split)
    high = pl.ds(split, own_rows - split)

    def rows_of(block, offset, count):
        return pl.ds(pl.multiple_of(block * own_rows + offset, 16), count)

    barrier = pltpu.get_barrier_semaphore()
    pl.semaphore_signal(barrier, inc=1, device_id=(other, head, tok), device_id_type=mesh_ids)
    for h in range(head_count):
        @pl.when(h != head)
        def _greet():
            pl.semaphore_signal(barrier, inc=1, device_id=(section, h, tok), device_id_type=mesh_ids)

    def project_block(block):
        rows = pl.ds(pl.multiple_of(block * own_rows, 16), own_rows)
        return jnp.dot(
            mine_ref[rows, :], w_ref[...], preferred_element_type=jnp.float32
        ) + jnp.dot(theirs_ref[rows, :], wp_ref[...], preferred_element_type=jnp.float32)

    part_ref[opposite] = project_block(opposite).astype(part_ref.dtype)
    pl.semaphore_wait(barrier, head_count)

    def ring(kind, src, dst, target, send_sem, recv_sem):
        return pltpu.make_async_remote_copy(
            src_ref=src,
            dst_ref=dst,
            send_sem=send_sem.at[kind],
            recv_sem=recv_sem.at[kind],
            device_id=(section, target, tok),
            device_id_type=mesh_ids,
        )

    low_count = split
    high_count = own_rows - split
    pass_a = ring(0, part_ref.at[opposite, low], land_a.at[0], up, r_send, r_recv)
    pass_b = ring(1, part_ref.at[opposite, high], land_b.at[0], down, r_send, r_recv)
    direct_a = ring(2, part_ref.at[down, low], land_a.at[1], down, r_send, r_recv)
    direct_b = ring(3, part_ref.at[up, high], land_b.at[1], up, r_send, r_recv)
    pass_a.start()
    pass_b.start()
    part_ref[down] = project_block(down).astype(part_ref.dtype)
    direct_a.start()
    part_ref[up] = project_block(up).astype(part_ref.dtype)
    direct_b.start()
    acc[...] = project_block(head)
    pass_a.wait()
    sums_a[...] = (
        part_ref[up, low].astype(jnp.float32) + land_a[0].astype(jnp.float32)
    ).astype(sums_a.dtype)
    joined_a = ring(4, sums_a, land_a.at[2], up, r_send, r_recv)
    joined_a.start()
    pass_b.wait()
    sums_b[...] = (
        part_ref[down, high].astype(jnp.float32) + land_b[0].astype(jnp.float32)
    ).astype(sums_b.dtype)
    joined_b = ring(5, sums_b, land_b.at[2], down, r_send, r_recv)
    joined_b.start()
    direct_a.wait()
    direct_b.wait()
    joined_a.wait()
    joined_b.wait()
    acc[low, :] += land_a[1].astype(jnp.float32) + land_a[2].astype(jnp.float32)
    acc[high, :] += land_b[1].astype(jnp.float32) + land_b[2].astype(jnp.float32)
    if not gather:
        out_ref[...] = acc[...]
        return
    result = (own_ref[...].astype(jnp.float32) + gate_ref[...] * acc[...]).astype(full_ref.dtype)
    full_ref[section, head] = result
    out_ref[...] = result

    def pass_copy(h):
        return pltpu.make_async_remote_copy(
            src_ref=full_ref.at[section, h],
            dst_ref=full_ref.at[section, h],
            send_sem=g2_send.at[h],
            recv_sem=g2_recv.at[h],
            device_id=(other, head, tok),
            device_id_type=mesh_ids,
        )

    to_up = ring(0, full_ref.at[section, head], full_ref.at[section, head], up, a_send, a_recv)
    to_down = ring(1, full_ref.at[section, head], full_ref.at[section, head], down, a_send, a_recv)
    to_up.start()
    to_down.start()
    pass_copy(head).start()
    to_up.wait()
    onward_a = ring(
        2, full_ref.at[section, down, low], full_ref.at[section, down, low], up, a_send, a_recv
    )
    onward_a.start()
    pass_copy(down).start()
    to_down.wait()
    onward_b = ring(
        3, full_ref.at[section, up, high], full_ref.at[section, up, high], down, a_send, a_recv
    )
    onward_b.start()
    pass_copy(up).start()
    onward_a.wait()
    onward_b.wait()
    pass_copy(opposite).start()
    pass_copy(head).wait()
    pass_copy(down).wait()
    pass_copy(up).wait()
    pass_copy(opposite).wait()


def exchange(mine, theirs, weight, partner_weight, own_input, gate, layer_idx, gather, head_count, own_rows):
    width = weight.shape[1]
    split = (own_rows * 2 // 3) // 16 * 16
    vmem = pl.BlockSpec(memory_space=pltpu.VMEM)
    scratch = [
        pltpu.VMEM((head_count, own_rows, width), jnp.bfloat16),
        pltpu.VMEM((3, split, width), jnp.bfloat16),
        pltpu.VMEM((3, own_rows - split, width), jnp.bfloat16),
        pltpu.VMEM((split, width), jnp.bfloat16),
        pltpu.VMEM((own_rows - split, width), jnp.bfloat16),
        pltpu.VMEM((own_rows, width), jnp.float32),
        pltpu.SemaphoreType.DMA((6,)),
        pltpu.SemaphoreType.DMA((6,)),
    ]
    if gather:
        out_shape = (
            jax.ShapeDtypeStruct((own_rows, width), jnp.bfloat16),
            jax.ShapeDtypeStruct((2, head_count, own_rows, width), jnp.bfloat16),
        )
        out_specs = (vmem, vmem)
        scratch += [pltpu.SemaphoreType.DMA((head_count,))] * 4
    else:
        out_shape = jax.ShapeDtypeStruct((own_rows, width), jnp.float32)
        out_specs = vmem
    return pl.pallas_call(
        functools.partial(exchange_kernel, head_count, own_rows, split, gather),
        out_shape=out_shape,
        in_specs=[vmem] * 6,
        out_specs=out_specs,
        scratch_shapes=scratch,
        compiler_params=pltpu.CompilerParams(
            collective_id=layer_idx, has_side_effects=True, vmem_limit_bytes=56 * 1024 * 1024
        ),
    )(mine, theirs, weight, partner_weight, own_input, gate.reshape(1, width))


def noise_level(position):
    time_left = 1.0 - position.astype(jnp.float32) / STEPS
    return time_shift * time_left / (1.0 + (time_shift - 1.0) * time_left)


def shards(
    hidden,
    latent,
    w_qkv,
    w_out,
    w_final,
    qk_gain,
    modulation,
    stale_kv,
    request_patches,
    patch_order,
    step_index,
):
    section_count = lax.axis_size("section")
    head_count = lax.axis_size("head")
    group_count = section_count * head_count
    section_index = lax.axis_index("section")
    head_index = lax.axis_index("head")
    tok_index = lax.axis_index("tok")
    group_index = section_index * head_count + head_index
    patch_len = hidden.shape[1]
    width = hidden.shape[2]
    head_dim = qk_gain.shape[-1]
    own_rows = patch_len // group_count
    layer_count = w_qkv.shape[0]
    request_of, offsets = slot_layout(request_patches, patch_order)
    slot_total = request_of.shape[0]
    my_request = request_of[tok_index]
    my_offset = offsets[tok_index]
    positions = (my_offset * patch_len + jnp.arange(patch_len, dtype=jnp.int32)).astype(jnp.float32)
    slot_ids = jnp.arange(slot_total, dtype=jnp.int32)
    allowed = (request_of == my_request) & (slot_ids != tok_index)
    rank = jnp.cumsum(allowed.astype(jnp.int32)) - 1
    count = jnp.sum(allowed.astype(jnp.int32))
    step_ids = jnp.arange(MOST - 1, dtype=jnp.int32)
    picked = allowed[None, :] & (rank[None, :] == step_ids[:, None])
    compact = jnp.sum(jnp.where(picked, slot_ids[None, :], 0), axis=1)
    last_pick = jnp.sum(jnp.where(allowed & (rank == count - 1), slot_ids, 0))
    fetch = jnp.where(step_ids < count, compact, last_pick).astype(jnp.int32)
    allow = (step_ids < count).astype(jnp.int32)
    stale_layers = [
        lax.all_gather(jnp.swapaxes(stale_kv[layer], 0, 1), "tok", axis=0, tiled=True)
        for layer in range(layer_count)
    ]
    current_full = hidden[0]
    w_partner = lax.ppermute(w_out, "section", perm=[(0, 1), (1, 0)])
    own_input = lax.dynamic_slice_in_dim(current_full, group_index * own_rows, own_rows, 0)
    outputs = []
    for layer_idx in range(layer_count):
        queries, keys_fresh, values_fresh = project(
            current_full,
            modulation[layer_idx],
            w_qkv[layer_idx],
            qk_gain[layer_idx],
            positions,
            head_dim,
        )
        attended = attend(
            queries, keys_fresh, values_fresh, stale_layers[layer_idx], fetch, allow, head_dim
        )
        half_rows = patch_len // section_count
        mine = lax.dynamic_slice_in_dim(attended, section_index * half_rows, half_rows, 0)
        theirs = lax.dynamic_slice_in_dim(attended, (1 - section_index) * half_rows, half_rows, 0)
        swapped = lax.ppermute(theirs, "section", perm=[(0, 1), (1, 0)])
        gate = modulation[layer_idx, 2]
        if layer_idx + 1 < layer_count:
            own_out, gathered = exchange(
                mine, swapped, w_out[layer_idx], w_partner[layer_idx], own_input, gate,
                layer_idx, True, head_count, own_rows,
            )
            current_full = gathered.reshape(patch_len, width)
        else:
            summed = exchange(
                mine, swapped, w_out[layer_idx], w_partner[layer_idx], own_input, gate,
                layer_idx, False, head_count, own_rows,
            )
            own_out = (own_input.astype(jnp.float32) + gate * summed).astype(jnp.bfloat16)
        own_input = own_out
        outputs.append(own_out)
    last_own = outputs[-1]
    layer_out = jnp.stack(outputs)[:, None]
    normed = layer_norm(last_own.astype(jnp.float32)).astype(jnp.bfloat16)
    velocity = jnp.dot(normed, w_final, preferred_element_type=jnp.float32)[None]
    level_now = noise_level(step_index[0])
    level_next = noise_level(step_index[0] + 1)
    return (layer_out, latent + (level_next - level_now) * velocity, latent - level_now * velocity)


def solution(mesh):
    placed = (
        P("tok", None, None),
        P("tok", ("section", "head"), None),
        P(None, None, None, ("section", "head")),
        P(None, ("section", "head"), None),
        P(),
        P(),
        P(),
        P(None, None, "tok", None, ("section", "head")),
        P(),
        P(),
        P(),
    )
    return jax.shard_map(
        shards,
        mesh=mesh,
        in_specs=placed,
        out_specs=(
            P(None, "tok", ("section", "head"), None),
            P("tok", ("section", "head"), None),
            P("tok", ("section", "head"), None),
        ),
        check_vma=False,
    )
```

```python
import functools
import math

import jax
import jax.numpy as jnp
from jax import lax
from jax.experimental import pallas as pl
from jax.experimental.pallas import tpu as pltpu
from jax.sharding import PartitionSpec as P

STEPS = 28
MOST = 8


norm_eps = 1e-06
time_shift = 3.0
rope_base = 10000.0


def layer_norm(inputs):
    average = jnp.mean(inputs, axis=-1, keepdims=True)
    centred = inputs - average
    variance = jnp.mean(centred * centred, axis=-1, keepdims=True)
    return centred * lax.rsqrt(variance + norm_eps)


def rms_norm(inputs, gains):
    return inputs * lax.rsqrt(jnp.mean(inputs * inputs, axis=-1, keepdims=True) + norm_eps) * gains


def rotate(inputs, positions):
    half_dim = inputs.shape[-1] // 2
    frequency = rope_base ** (-2.0 * jnp.arange(half_dim, dtype=jnp.float32) / inputs.shape[-1])
    angles = positions[..., None, None] * frequency
    cosine = jnp.repeat(jnp.cos(angles), 2, axis=-1)
    sign = jnp.tile(jnp.array([-1.0, 1.0], dtype=jnp.float32), half_dim)
    sine = jnp.repeat(jnp.sin(angles), 2, axis=-1) * sign
    pairs = inputs.reshape(inputs.shape[:-1] + (half_dim, 2))
    swapped = pairs[..., ::-1].reshape(inputs.shape)
    return inputs * cosine + swapped * sine


def slot_layout(request_patches, patch_order):
    request_ends = jnp.cumsum(request_patches)
    starts = request_ends - request_patches
    request_of = jnp.sum((request_ends[None, :] <= patch_order[:, None]).astype(jnp.int32), axis=1)
    chosen = request_of[:, None] == jnp.arange(request_patches.shape[0], dtype=jnp.int32)[None, :]
    first_patch = jnp.sum(jnp.where(chosen, starts[None, :], 0), axis=1)
    return (request_of, patch_order - first_patch)


def project(inputs, layer_mod, weight, gains, positions, head_dim):
    normed = (layer_norm(inputs.astype(jnp.float32)) * (1.0 + layer_mod[1]) + layer_mod[0]).astype(
        jnp.bfloat16
    )
    rows = inputs.shape[0]
    column_count = weight.shape[2]
    heads = column_count // head_dim
    pieces = [
        jnp.dot(normed, weight[:, part, :], preferred_element_type=jnp.float32).reshape(
            rows, heads, head_dim
        )
        for part in range(3)
    ]
    queries = rotate(rms_norm(pieces[0], gains[0]), positions).astype(jnp.bfloat16)
    keys_fresh = rotate(rms_norm(pieces[1], gains[1]), positions).astype(jnp.bfloat16)
    values_fresh = pieces[2].astype(jnp.bfloat16)
    return (
        queries.reshape(rows, column_count),
        keys_fresh.reshape(rows, column_count),
        values_fresh.reshape(rows, column_count),
    )


def attention_kernel(
    head_dim, fetch_ref, allow_ref, q_ref, kf_ref, vf_ref, ks_ref, vs_ref, o_ref, qt_sc, m_sc, l_sc, acc_sc
):
    slot = pl.program_id(0)
    heads = q_ref.shape[1] // head_dim
    scaling = 1.0 / math.sqrt(head_dim)
    by_key = (((0,), (0,)), ((), ()))

    @pl.when(slot == 0)
    def _fresh():
        for h in range(heads):
            lanes = slice(h * head_dim, (h + 1) * head_dim)
            qt_sc[h] = q_ref[:, lanes].T
            scores = (
                jnp.dot(kf_ref[:, lanes], qt_sc[h], preferred_element_type=jnp.float32) * scaling
            )
            col_max = jnp.max(scores, axis=0, keepdims=True)
            weights = jnp.exp(scores - col_max)
            m_sc[h] = col_max
            l_sc[h] = jnp.sum(weights, axis=0, keepdims=True)
            acc_sc[h] = lax.dot_general(
                vf_ref[:, lanes], weights.astype(jnp.bfloat16), by_key,
                preferred_element_type=jnp.float32,
            )

    @pl.when(allow_ref[slot] != 0)
    def _stale():
        for h in range(heads):
            lanes = slice(h * head_dim, (h + 1) * head_dim)
            scores = (
                jnp.dot(ks_ref[:, lanes], qt_sc[h], preferred_element_type=jnp.float32) * scaling
            )
            old_max = m_sc[h]
            new_max = jnp.maximum(old_max, jnp.max(scores, axis=0, keepdims=True))
            factor = jnp.exp(old_max - new_max)
            weights = jnp.exp(scores - new_max)
            l_sc[h] = l_sc[h] * factor + jnp.sum(weights, axis=0, keepdims=True)
            acc_sc[h] = acc_sc[h] * factor + lax.dot_general(
                vs_ref[:, lanes], weights.astype(jnp.bfloat16), by_key,
                preferred_element_type=jnp.float32,
            )
            m_sc[h] = new_max

    @pl.when(slot == pl.num_programs(0) - 1)
    def _finish():
        for h in range(heads):
            lanes = slice(h * head_dim, (h + 1) * head_dim)
            o_ref[:, lanes] = (acc_sc[h] / l_sc[h]).T.astype(o_ref.dtype)


def attend(queries, keys_fresh, values_fresh, stale, fetch, allow, head_dim):
    rows, features = queries.shape
    slot_total = fetch.shape[0]
    heads = features // head_dim
    whole = pl.BlockSpec((rows, features), lambda j, f, a: (0, 0))
    key_spec = pl.BlockSpec(
        (None, None, rows, features), lambda j, f, a: (f[j], 0, 0, 0)
    )
    value_spec = pl.BlockSpec(
        (None, None, rows, features), lambda j, f, a: (f[j], 1, 0, 0)
    )
    return pl.pallas_call(
        functools.partial(attention_kernel, head_dim),
        out_shape=jax.ShapeDtypeStruct((rows, features), jnp.bfloat16),
        grid_spec=pltpu.PrefetchScalarGridSpec(
            num_scalar_prefetch=2,
            grid=(slot_total,),
            in_specs=[whole, whole, whole, key_spec, value_spec],
            out_specs=whole,
            scratch_shapes=[
                pltpu.VMEM((heads, head_dim, rows), jnp.bfloat16),
                pltpu.VMEM((heads, 1, rows), jnp.float32),
                pltpu.VMEM((heads, 1, rows), jnp.float32),
                pltpu.VMEM((heads, head_dim, rows), jnp.float32),
            ],
        ),
        compiler_params=pltpu.CompilerParams(dimension_semantics=("arbitrary",)),
    )(fetch, allow, queries, keys_fresh, values_fresh, stale, stale)


def exchange_kernel(head_count, own_rows, split, gather, part_ref, own_ref, gate_ref, *rest):
    if gather:
        (out_ref, full_ref, land_a, land_b, sums_a, sums_b, acc,
         r_send, r_recv, a_send, a_recv, g2_send, g2_recv) = rest
    else:
        (out_ref, land_a, land_b, sums_a, sums_b, acc, r_send, r_recv) = rest
    mesh_ids = pl.DeviceIdType.MESH
    section = lax.axis_index("section")
    head = lax.axis_index("head")
    tok = lax.axis_index("tok")
    other = 1 - section
    up = lax.rem(head + 1, head_count)
    down = lax.rem(head + head_count - 1, head_count)
    opposite = lax.rem(head + 2, head_count)
    low = pl.ds(0, split)
    high = pl.ds(split, own_rows - split)

    def rows_of(block, offset, count):
        return pl.ds(pl.multiple_of(block * own_rows + offset, 16), count)

    barrier = pltpu.get_barrier_semaphore()
    pl.semaphore_signal(barrier, inc=1, device_id=(other, head, tok), device_id_type=mesh_ids)
    for h in range(head_count):
        @pl.when(h != head)
        def _greet():
            pl.semaphore_signal(barrier, inc=1, device_id=(section, h, tok), device_id_type=mesh_ids)
    pl.semaphore_wait(barrier, head_count)

    def ring(kind, src, dst, target, send_sem, recv_sem):
        return pltpu.make_async_remote_copy(
            src_ref=src,
            dst_ref=dst,
            send_sem=send_sem.at[kind],
            recv_sem=recv_sem.at[kind],
            device_id=(section, target, tok),
            device_id_type=mesh_ids,
        )

    low_count = split
    high_count = own_rows - split
    pass_a = ring(0, part_ref.at[rows_of(opposite, 0, low_count)], land_a.at[0], up, r_send, r_recv)
    pass_b = ring(1, part_ref.at[rows_of(opposite, split, high_count)], land_b.at[0], down, r_send, r_recv)
    direct_a = ring(2, part_ref.at[rows_of(down, 0, low_count)], land_a.at[1], down, r_send, r_recv)
    direct_b = ring(3, part_ref.at[rows_of(up, split, high_count)], land_b.at[1], up, r_send, r_recv)
    pass_a.start()
    pass_b.start()
    direct_a.start()
    direct_b.start()
    def by_chunks(count, body):
        @pl.loop(0, count // 16)
        def _chunk(c):
            body(pl.multiple_of(c * 16, 16))

    def own_rows_in(r):
        acc[pl.ds(r, 16), :] = part_ref[rows_of(head, r, 16), :].astype(jnp.float32)

    by_chunks(own_rows, own_rows_in)
    pass_a.wait()

    def sum_low(r):
        sums_a[pl.ds(r, 16), :] = (
            part_ref[rows_of(up, r, 16), :].astype(jnp.float32)
            + land_a[0, pl.ds(r, 16), :].astype(jnp.float32)
        ).astype(sums_a.dtype)

    by_chunks(low_count, sum_low)
    joined_a = ring(4, sums_a, land_a.at[2], up, r_send, r_recv)
    joined_a.start()
    pass_b.wait()
    def sum_high(r):
        sums_b[pl.ds(r, 16), :] = (
            part_ref[rows_of(down, split + r, 16), :].astype(jnp.float32)
            + land_b[0, pl.ds(r, 16), :].astype(jnp.float32)
        ).astype(sums_b.dtype)

    by_chunks(high_count, sum_high)
    joined_b = ring(5, sums_b, land_b.at[2], down, r_send, r_recv)
    joined_b.start()
    direct_a.wait()
    direct_b.wait()
    joined_a.wait()
    joined_b.wait()
    def add_low(r):
        acc[pl.ds(r, 16), :] += (
            land_a[1, pl.ds(r, 16), :].astype(jnp.float32) + land_a[2, pl.ds(r, 16), :].astype(jnp.float32)
        )

    def add_high(r):
        acc[pl.ds(split + r, 16), :] += (
            land_b[1, pl.ds(r, 16), :].astype(jnp.float32) + land_b[2, pl.ds(r, 16), :].astype(jnp.float32)
        )

    by_chunks(low_count, add_low)
    by_chunks(high_count, add_high)
    if not gather:
        out_ref[...] = acc[...]
        return

    def finish(r):
        result = (
            own_ref[pl.ds(r, 16), :].astype(jnp.float32) + gate_ref[...] * acc[pl.ds(r, 16), :]
        ).astype(full_ref.dtype)
        full_ref[section, head, pl.ds(r, 16), :] = result
        out_ref[pl.ds(r, 16), :] = result

    by_chunks(own_rows, finish)

    def pass_copy(h):
        return pltpu.make_async_remote_copy(
            src_ref=full_ref.at[section, h],
            dst_ref=full_ref.at[section, h],
            send_sem=g2_send.at[h],
            recv_sem=g2_recv.at[h],
            device_id=(other, head, tok),
            device_id_type=mesh_ids,
        )

    to_up = ring(0, full_ref.at[section, head], full_ref.at[section, head], up, a_send, a_recv)
    to_down = ring(1, full_ref.at[section, head], full_ref.at[section, head], down, a_send, a_recv)
    to_up.start()
    to_down.start()
    pass_copy(head).start()
    to_up.wait()
    onward_a = ring(
        2, full_ref.at[section, down, low], full_ref.at[section, down, low], up, a_send, a_recv
    )
    onward_a.start()
    pass_copy(down).start()
    to_down.wait()
    onward_b = ring(
        3, full_ref.at[section, up, high], full_ref.at[section, up, high], down, a_send, a_recv
    )
    onward_b.start()
    pass_copy(up).start()
    onward_a.wait()
    onward_b.wait()
    pass_copy(opposite).start()
    pass_copy(head).wait()
    pass_copy(down).wait()
    pass_copy(up).wait()
    pass_copy(opposite).wait()


def exchange(partial, own_input, gate, layer_idx, gather, head_count, own_rows):
    rows, width = partial.shape
    split = (own_rows * 2 // 3) // 16 * 16
    vmem = pl.BlockSpec(memory_space=pltpu.VMEM)
    scratch = [
        pltpu.VMEM((3, split, width), partial.dtype),
        pltpu.VMEM((3, own_rows - split, width), partial.dtype),
        pltpu.VMEM((split, width), partial.dtype),
        pltpu.VMEM((own_rows - split, width), partial.dtype),
        pltpu.VMEM((own_rows, width), jnp.float32),
        pltpu.SemaphoreType.DMA((6,)),
        pltpu.SemaphoreType.DMA((6,)),
    ]
    if gather:
        out_shape = (
            jax.ShapeDtypeStruct((own_rows, width), jnp.bfloat16),
            jax.ShapeDtypeStruct((2, head_count, own_rows, width), jnp.bfloat16),
        )
        out_specs = (vmem, vmem)
        scratch += [pltpu.SemaphoreType.DMA((head_count,))] * 4
    else:
        out_shape = jax.ShapeDtypeStruct((own_rows, width), jnp.float32)
        out_specs = vmem
    return pl.pallas_call(
        functools.partial(exchange_kernel, head_count, own_rows, split, gather),
        out_shape=out_shape,
        in_specs=[vmem, vmem, vmem],
        out_specs=out_specs,
        scratch_shapes=scratch,
        compiler_params=pltpu.CompilerParams(
            collective_id=layer_idx, has_side_effects=True, vmem_limit_bytes=48 * 1024 * 1024
        ),
    )(partial, own_input, gate.reshape(1, width))


def noise_level(position):
    time_left = 1.0 - position.astype(jnp.float32) / STEPS
    return time_shift * time_left / (1.0 + (time_shift - 1.0) * time_left)


def shards(
    hidden,
    latent,
    w_qkv,
    w_out,
    w_final,
    qk_gain,
    modulation,
    stale_kv,
    request_patches,
    patch_order,
    step_index,
):
    section_count = lax.axis_size("section")
    head_count = lax.axis_size("head")
    group_count = section_count * head_count
    section_index = lax.axis_index("section")
    head_index = lax.axis_index("head")
    tok_index = lax.axis_index("tok")
    group_index = section_index * head_count + head_index
    patch_len = hidden.shape[1]
    width = hidden.shape[2]
    head_dim = qk_gain.shape[-1]
    own_rows = patch_len // group_count
    layer_count = w_qkv.shape[0]
    request_of, offsets = slot_layout(request_patches, patch_order)
    slot_total = request_of.shape[0]
    my_request = request_of[tok_index]
    my_offset = offsets[tok_index]
    positions = (my_offset * patch_len + jnp.arange(patch_len, dtype=jnp.int32)).astype(jnp.float32)
    slot_ids = jnp.arange(slot_total, dtype=jnp.int32)
    allowed = (request_of == my_request) & (slot_ids != tok_index)
    rank = jnp.cumsum(allowed.astype(jnp.int32)) - 1
    count = jnp.sum(allowed.astype(jnp.int32))
    step_ids = jnp.arange(MOST - 1, dtype=jnp.int32)
    picked = allowed[None, :] & (rank[None, :] == step_ids[:, None])
    compact = jnp.sum(jnp.where(picked, slot_ids[None, :], 0), axis=1)
    last_pick = jnp.sum(jnp.where(allowed & (rank == count - 1), slot_ids, 0))
    fetch = jnp.where(step_ids < count, compact, last_pick).astype(jnp.int32)
    allow = (step_ids < count).astype(jnp.int32)
    stale_layers = [
        lax.all_gather(jnp.swapaxes(stale_kv[layer], 0, 1), "tok", axis=0, tiled=True)
        for layer in range(layer_count)
    ]
    current_full = hidden[0]
    w_partner = lax.ppermute(w_out, "section", perm=[(0, 1), (1, 0)])
    own_input = lax.dynamic_slice_in_dim(current_full, group_index * own_rows, own_rows, 0)
    outputs = []
    for layer_idx in range(layer_count):
        queries, keys_fresh, values_fresh = project(
            current_full,
            modulation[layer_idx],
            w_qkv[layer_idx],
            qk_gain[layer_idx],
            positions,
            head_dim,
        )
        attended = attend(
            queries, keys_fresh, values_fresh, stale_layers[layer_idx], fetch, allow, head_dim
        )
        half_rows = patch_len // section_count
        mine = lax.dynamic_slice_in_dim(attended, section_index * half_rows, half_rows, 0)
        theirs = lax.dynamic_slice_in_dim(attended, (1 - section_index) * half_rows, half_rows, 0)
        swapped = lax.ppermute(theirs, "section", perm=[(0, 1), (1, 0)])
        partial = (
            jnp.dot(mine, w_out[layer_idx], preferred_element_type=jnp.float32)
            + jnp.dot(swapped, w_partner[layer_idx], preferred_element_type=jnp.float32)
        ).astype(jnp.bfloat16)
        gate = modulation[layer_idx, 2]
        if layer_idx + 1 < layer_count:
            own_out, gathered = exchange(
                partial, own_input, gate, layer_idx, True, head_count, own_rows
            )
            current_full = gathered.reshape(patch_len, width)
        else:
            summed = exchange(partial, own_input, gate, layer_idx, False, head_count, own_rows)
            own_out = (own_input.astype(jnp.float32) + gate * summed).astype(jnp.bfloat16)
        own_input = own_out
        outputs.append(own_out)
    last_own = outputs[-1]
    layer_out = jnp.stack(outputs)[:, None]
    normed = layer_norm(last_own.astype(jnp.float32)).astype(jnp.bfloat16)
    velocity = jnp.dot(normed, w_final, preferred_element_type=jnp.float32)[None]
    level_now = noise_level(step_index[0])
    level_next = noise_level(step_index[0] + 1)
    return (layer_out, latent + (level_next - level_now) * velocity, latent - level_now * velocity)


def solution(mesh):
    placed = (
        P("tok", None, None),
        P("tok", ("section", "head"), None),
        P(None, None, None, ("section", "head")),
        P(None, ("section", "head"), None),
        P(),
        P(),
        P(),
        P(None, None, "tok", None, ("section", "head")),
        P(),
        P(),
        P(),
    )
    return jax.shard_map(
        shards,
        mesh=mesh,
        in_specs=placed,
        out_specs=(
            P(None, "tok", ("section", "head"), None),
            P("tok", ("section", "head"), None),
            P("tok", ("section", "head"), None),
        ),
        check_vma=False,
    )
```

```python
import functools
import math

import jax
import jax.numpy as jnp
from jax import lax
from jax.experimental import pallas as pl
from jax.experimental.pallas import tpu as pltpu
from jax.sharding import PartitionSpec as P

STEPS = 28
MOST = 8


norm_eps = 1e-06
time_shift = 3.0
rope_base = 10000.0


def layer_norm(inputs):
    average = jnp.mean(inputs, axis=-1, keepdims=True)
    centred = inputs - average
    variance = jnp.mean(centred * centred, axis=-1, keepdims=True)
    return centred * lax.rsqrt(variance + norm_eps)


def rms_norm(inputs, gains):
    return inputs * lax.rsqrt(jnp.mean(inputs * inputs, axis=-1, keepdims=True) + norm_eps) * gains


def rotate(inputs, positions):
    half_dim = inputs.shape[-1] // 2
    frequency = rope_base ** (-2.0 * jnp.arange(half_dim, dtype=jnp.float32) / inputs.shape[-1])
    angles = positions[..., None, None] * frequency
    pairs = inputs.reshape(inputs.shape[:-1] + (half_dim, 2))
    even_lane = pairs[..., 0]
    odd_lane = pairs[..., 1]
    cosine = jnp.cos(angles)
    sine = jnp.sin(angles)
    turned = jnp.stack(
        [even_lane * cosine - odd_lane * sine, even_lane * sine + odd_lane * cosine], axis=-1
    )
    return turned.reshape(inputs.shape)


def slot_layout(request_patches, patch_order):
    request_ends = jnp.cumsum(request_patches)
    starts = request_ends - request_patches
    request_of = jnp.sum((request_ends[None, :] <= patch_order[:, None]).astype(jnp.int32), axis=1)
    chosen = request_of[:, None] == jnp.arange(request_patches.shape[0], dtype=jnp.int32)[None, :]
    first_patch = jnp.sum(jnp.where(chosen, starts[None, :], 0), axis=1)
    return (request_of, patch_order - first_patch)


def project(inputs, layer_mod, weight, gains, positions, head_dim):
    normed = (layer_norm(inputs.astype(jnp.float32)) * (1.0 + layer_mod[1]) + layer_mod[0]).astype(
        jnp.bfloat16
    )
    rows = inputs.shape[0]
    column_count = weight.shape[2]
    heads = column_count // head_dim
    pieces = [
        jnp.dot(normed, weight[:, part, :], preferred_element_type=jnp.float32).reshape(
            rows, heads, head_dim
        )
        for part in range(3)
    ]
    queries = rotate(rms_norm(pieces[0], gains[0]), positions).astype(jnp.bfloat16)
    keys_fresh = rotate(rms_norm(pieces[1], gains[1]), positions).astype(jnp.bfloat16)
    values_fresh = pieces[2].astype(jnp.bfloat16)
    return (
        queries.reshape(rows, column_count),
        keys_fresh.reshape(rows, column_count),
        values_fresh.reshape(rows, column_count),
    )


def fresh_kernel(head_dim, q_ref, kf_ref, vf_ref, qt_ref, m_ref, l_ref, acc_ref):
    heads = q_ref.shape[1] // head_dim
    scaling = 1.0 / math.sqrt(head_dim)
    by_key = (((0,), (0,)), ((), ()))
    for h in range(heads):
        lanes = slice(h * head_dim, (h + 1) * head_dim)
        qt_ref[h] = q_ref[:, lanes].T
        scores = jnp.dot(kf_ref[:, lanes], qt_ref[h], preferred_element_type=jnp.float32) * scaling
        col_max = jnp.max(scores, axis=0, keepdims=True)
        weights = jnp.exp(scores - col_max)
        m_ref[h] = col_max
        l_ref[h] = jnp.sum(weights, axis=0, keepdims=True)
        acc_ref[h] = lax.dot_general(
            vf_ref[:, lanes], weights.astype(jnp.bfloat16), by_key,
            preferred_element_type=jnp.float32,
        )


def attention_kernel(
    head_dim, fetch_ref, allow_ref, qt_ref, m0_ref, l0_ref, acc0_ref, ks_ref, vs_ref, o_ref,
    m_sc, l_sc, acc_sc
):
    slot = pl.program_id(0)
    heads = qt_ref.shape[0]
    scaling = 1.0 / math.sqrt(head_dim)
    by_key = (((0,), (0,)), ((), ()))

    @pl.when(slot == 0)
    def _start():
        m_sc[...] = m0_ref[...]
        l_sc[...] = l0_ref[...]
        acc_sc[...] = acc0_ref[...]

    @pl.when(allow_ref[slot] != 0)
    def _stale():
        for h in range(heads):
            lanes = slice(h * head_dim, (h + 1) * head_dim)
            scores = (
                jnp.dot(ks_ref[:, lanes], qt_ref[h], preferred_element_type=jnp.float32) * scaling
            )
            old_max = m_sc[h]
            new_max = jnp.maximum(old_max, jnp.max(scores, axis=0, keepdims=True))
            factor = jnp.exp(old_max - new_max)
            weights = jnp.exp(scores - new_max)
            l_sc[h] = l_sc[h] * factor + jnp.sum(weights, axis=0, keepdims=True)
            acc_sc[h] = acc_sc[h] * factor + lax.dot_general(
                vs_ref[:, lanes], weights.astype(jnp.bfloat16), by_key,
                preferred_element_type=jnp.float32,
            )
            m_sc[h] = new_max

    @pl.when(slot == pl.num_programs(0) - 1)
    def _finish():
        for h in range(heads):
            lanes = slice(h * head_dim, (h + 1) * head_dim)
            o_ref[:, lanes] = (acc_sc[h] / l_sc[h]).T.astype(o_ref.dtype)


def attend(queries, keys_fresh, values_fresh, stale, fetch, allow, head_dim):
    rows, features = queries.shape
    slot_total = fetch.shape[0]
    heads = features // head_dim
    vmem = pl.BlockSpec(memory_space=pltpu.VMEM)
    state = pl.pallas_call(
        functools.partial(fresh_kernel, head_dim),
        out_shape=(
            jax.ShapeDtypeStruct((heads, head_dim, rows), jnp.bfloat16),
            jax.ShapeDtypeStruct((heads, 1, rows), jnp.float32),
            jax.ShapeDtypeStruct((heads, 1, rows), jnp.float32),
            jax.ShapeDtypeStruct((heads, head_dim, rows), jnp.float32),
        ),
        in_specs=[vmem] * 3,
        out_specs=(vmem,) * 4,
    )(queries, keys_fresh, values_fresh)
    whole = pl.BlockSpec((rows, features), lambda j, f, a: (0, 0))
    qt_spec = pl.BlockSpec((heads, head_dim, rows), lambda j, f, a: (0, 0, 0))
    stat_spec = pl.BlockSpec((heads, 1, rows), lambda j, f, a: (0, 0, 0))
    key_spec = pl.BlockSpec(
        (None, None, rows, features), lambda j, f, a: (f[j], 0, 0, 0)
    )
    value_spec = pl.BlockSpec(
        (None, None, rows, features), lambda j, f, a: (f[j], 1, 0, 0)
    )
    return pl.pallas_call(
        functools.partial(attention_kernel, head_dim),
        out_shape=jax.ShapeDtypeStruct((rows, features), jnp.bfloat16),
        grid_spec=pltpu.PrefetchScalarGridSpec(
            num_scalar_prefetch=2,
            grid=(slot_total,),
            in_specs=[qt_spec, stat_spec, stat_spec, qt_spec, key_spec, value_spec],
            out_specs=whole,
            scratch_shapes=[
                pltpu.VMEM((heads, 1, rows), jnp.float32),
                pltpu.VMEM((heads, 1, rows), jnp.float32),
                pltpu.VMEM((heads, head_dim, rows), jnp.float32),
            ],
        ),
        compiler_params=pltpu.CompilerParams(dimension_semantics=("arbitrary",)),
    )(fetch, allow, *state, stale, stale)


def exchange_kernel(head_count, own_rows, split, gather, part_ref, own_ref, gate_ref, *rest):
    if gather:
        (out_ref, full_ref, land_a, land_b, sums_a, sums_b, acc,
         r_send, r_recv, a_send, a_recv, g2_send, g2_recv) = rest
    else:
        (out_ref, land_a, land_b, sums_a, sums_b, acc, r_send, r_recv) = rest
    mesh_ids = pl.DeviceIdType.MESH
    section = lax.axis_index("section")
    head = lax.axis_index("head")
    tok = lax.axis_index("tok")
    other = 1 - section
    up = lax.rem(head + 1, head_count)
    down = lax.rem(head + head_count - 1, head_count)
    opposite = lax.rem(head + 2, head_count)
    low = pl.ds(0, split)
    high = pl.ds(split, own_rows - split)

    def rows_of(block, offset, count):
        return pl.ds(pl.multiple_of(block * own_rows + offset, 16), count)

    barrier = pltpu.get_barrier_semaphore()
    pl.semaphore_signal(barrier, inc=1, device_id=(other, head, tok), device_id_type=mesh_ids)
    for h in range(head_count):
        @pl.when(h != head)
        def _greet():
            pl.semaphore_signal(barrier, inc=1, device_id=(section, h, tok), device_id_type=mesh_ids)
    pl.semaphore_wait(barrier, head_count)

    def ring(kind, src, dst, target, send_sem, recv_sem):
        return pltpu.make_async_remote_copy(
            src_ref=src,
            dst_ref=dst,
            send_sem=send_sem.at[kind],
            recv_sem=recv_sem.at[kind],
            device_id=(section, target, tok),
            device_id_type=mesh_ids,
        )

    low_count = split
    high_count = own_rows - split
    pass_a = ring(0, part_ref.at[rows_of(opposite, 0, low_count)], land_a.at[0], up, r_send, r_recv)
    pass_b = ring(1, part_ref.at[rows_of(opposite, split, high_count)], land_b.at[0], down, r_send, r_recv)
    direct_a = ring(2, part_ref.at[rows_of(down, 0, low_count)], land_a.at[1], down, r_send, r_recv)
    direct_b = ring(3, part_ref.at[rows_of(up, split, high_count)], land_b.at[1], up, r_send, r_recv)
    pass_a.start()
    pass_b.start()
    direct_a.start()
    direct_b.start()
    acc[...] = part_ref[rows_of(head, 0, own_rows), :].astype(jnp.float32)
    pass_a.wait()
    sums_a[...] = (
        part_ref[rows_of(up, 0, low_count), :].astype(jnp.float32) + land_a[0].astype(jnp.float32)
    ).astype(sums_a.dtype)
    joined_a = ring(4, sums_a, land_a.at[2], up, r_send, r_recv)
    joined_a.start()
    pass_b.wait()
    sums_b[...] = (
        part_ref[rows_of(down, split, high_count), :].astype(jnp.float32)
        + land_b[0].astype(jnp.float32)
    ).astype(sums_b.dtype)
    joined_b = ring(5, sums_b, land_b.at[2], down, r_send, r_recv)
    joined_b.start()
    direct_a.wait()
    direct_b.wait()
    joined_a.wait()
    joined_b.wait()
    acc[low, :] += land_a[1].astype(jnp.float32) + land_a[2].astype(jnp.float32)
    acc[high, :] += land_b[1].astype(jnp.float32) + land_b[2].astype(jnp.float32)
    if not gather:
        out_ref[...] = acc[...]
        return
    result = (own_ref[...].astype(jnp.float32) + gate_ref[...] * acc[...]).astype(full_ref.dtype)
    full_ref[section, head] = result
    out_ref[...] = result

    def pass_copy(h):
        return pltpu.make_async_remote_copy(
            src_ref=full_ref.at[section, h],
            dst_ref=full_ref.at[section, h],
            send_sem=g2_send.at[h],
            recv_sem=g2_recv.at[h],
            device_id=(other, head, tok),
            device_id_type=mesh_ids,
        )

    to_up = ring(0, full_ref.at[section, head], full_ref.at[section, head], up, a_send, a_recv)
    to_down = ring(1, full_ref.at[section, head], full_ref.at[section, head], down, a_send, a_recv)
    to_up.start()
    to_down.start()
    pass_copy(head).start()
    to_up.wait()
    onward_a = ring(
        2, full_ref.at[section, down, low], full_ref.at[section, down, low], up, a_send, a_recv
    )
    onward_a.start()
    pass_copy(down).start()
    to_down.wait()
    onward_b = ring(
        3, full_ref.at[section, up, high], full_ref.at[section, up, high], down, a_send, a_recv
    )
    onward_b.start()
    pass_copy(up).start()
    onward_a.wait()
    onward_b.wait()
    pass_copy(opposite).start()
    pass_copy(head).wait()
    pass_copy(down).wait()
    pass_copy(up).wait()
    pass_copy(opposite).wait()


def exchange(partial, own_input, gate, layer_idx, gather, head_count, own_rows):
    rows, width = partial.shape
    split = (own_rows * 2 // 3) // 16 * 16
    vmem = pl.BlockSpec(memory_space=pltpu.VMEM)
    scratch = [
        pltpu.VMEM((3, split, width), partial.dtype),
        pltpu.VMEM((3, own_rows - split, width), partial.dtype),
        pltpu.VMEM((split, width), partial.dtype),
        pltpu.VMEM((own_rows - split, width), partial.dtype),
        pltpu.VMEM((own_rows, width), jnp.float32),
        pltpu.SemaphoreType.DMA((6,)),
        pltpu.SemaphoreType.DMA((6,)),
    ]
    if gather:
        out_shape = (
            jax.ShapeDtypeStruct((own_rows, width), jnp.bfloat16),
            jax.ShapeDtypeStruct((2, head_count, own_rows, width), jnp.bfloat16),
        )
        out_specs = (vmem, vmem)
        scratch += [pltpu.SemaphoreType.DMA((head_count,))] * 4
    else:
        out_shape = jax.ShapeDtypeStruct((own_rows, width), jnp.float32)
        out_specs = vmem
    return pl.pallas_call(
        functools.partial(exchange_kernel, head_count, own_rows, split, gather),
        out_shape=out_shape,
        in_specs=[vmem, vmem, vmem],
        out_specs=out_specs,
        scratch_shapes=scratch,
        compiler_params=pltpu.CompilerParams(
            collective_id=layer_idx, has_side_effects=True, vmem_limit_bytes=48 * 1024 * 1024
        ),
    )(partial, own_input, gate.reshape(1, width))


def noise_level(position):
    time_left = 1.0 - position.astype(jnp.float32) / STEPS
    return time_shift * time_left / (1.0 + (time_shift - 1.0) * time_left)


def shards(
    hidden,
    latent,
    w_qkv,
    w_out,
    w_final,
    qk_gain,
    modulation,
    stale_kv,
    request_patches,
    patch_order,
    step_index,
):
    section_count = lax.axis_size("section")
    head_count = lax.axis_size("head")
    group_count = section_count * head_count
    section_index = lax.axis_index("section")
    head_index = lax.axis_index("head")
    tok_index = lax.axis_index("tok")
    group_index = section_index * head_count + head_index
    patch_len = hidden.shape[1]
    width = hidden.shape[2]
    head_dim = qk_gain.shape[-1]
    own_rows = patch_len // group_count
    layer_count = w_qkv.shape[0]
    request_of, offsets = slot_layout(request_patches, patch_order)
    slot_total = request_of.shape[0]
    my_request = request_of[tok_index]
    my_offset = offsets[tok_index]
    positions = (my_offset * patch_len + jnp.arange(patch_len, dtype=jnp.int32)).astype(jnp.float32)
    slot_ids = jnp.arange(slot_total, dtype=jnp.int32)
    allowed = (request_of == my_request) & (slot_ids != tok_index)
    rank = jnp.cumsum(allowed.astype(jnp.int32)) - 1
    count = jnp.sum(allowed.astype(jnp.int32))
    step_ids = jnp.arange(MOST - 1, dtype=jnp.int32)
    picked = allowed[None, :] & (rank[None, :] == step_ids[:, None])
    compact = jnp.sum(jnp.where(picked, slot_ids[None, :], 0), axis=1)
    last_pick = jnp.sum(jnp.where(allowed & (rank == count - 1), slot_ids, 0))
    fetch = jnp.where(step_ids < count, compact, last_pick).astype(jnp.int32)
    allow = (step_ids < count).astype(jnp.int32)
    stale_layers = [
        lax.all_gather(jnp.swapaxes(stale_kv[layer], 0, 1), "tok", axis=0, tiled=True)
        for layer in range(layer_count)
    ]
    current_full = hidden[0]
    w_partner = lax.ppermute(w_out, "section", perm=[(0, 1), (1, 0)])
    own_input = lax.dynamic_slice_in_dim(current_full, group_index * own_rows, own_rows, 0)
    outputs = []
    for layer_idx in range(layer_count):
        queries, keys_fresh, values_fresh = project(
            current_full,
            modulation[layer_idx],
            w_qkv[layer_idx],
            qk_gain[layer_idx],
            positions,
            head_dim,
        )
        attended = attend(
            queries, keys_fresh, values_fresh, stale_layers[layer_idx], fetch, allow, head_dim
        )
        half_rows = patch_len // section_count
        mine = lax.dynamic_slice_in_dim(attended, section_index * half_rows, half_rows, 0)
        theirs = lax.dynamic_slice_in_dim(attended, (1 - section_index) * half_rows, half_rows, 0)
        swapped = lax.ppermute(theirs, "section", perm=[(0, 1), (1, 0)])
        partial = (
            jnp.dot(mine, w_out[layer_idx], preferred_element_type=jnp.float32)
            + jnp.dot(swapped, w_partner[layer_idx], preferred_element_type=jnp.float32)
        ).astype(jnp.bfloat16)
        gate = modulation[layer_idx, 2]
        if layer_idx + 1 < layer_count:
            own_out, gathered = exchange(
                partial, own_input, gate, layer_idx, True, head_count, own_rows
            )
            current_full = gathered.reshape(patch_len, width)
        else:
            summed = exchange(partial, own_input, gate, layer_idx, False, head_count, own_rows)
            own_out = (own_input.astype(jnp.float32) + gate * summed).astype(jnp.bfloat16)
        own_input = own_out
        outputs.append(own_out)
    last_own = outputs[-1]
    layer_out = jnp.stack(outputs)[:, None]
    normed = layer_norm(last_own.astype(jnp.float32)).astype(jnp.bfloat16)
    velocity = jnp.dot(normed, w_final, preferred_element_type=jnp.float32)[None]
    level_now = noise_level(step_index[0])
    level_next = noise_level(step_index[0] + 1)
    return (layer_out, latent + (level_next - level_now) * velocity, latent - level_now * velocity)


def solution(mesh):
    placed = (
        P("tok", None, None),
        P("tok", ("section", "head"), None),
        P(None, None, None, ("section", "head")),
        P(None, ("section", "head"), None),
        P(),
        P(),
        P(),
        P(None, None, "tok", None, ("section", "head")),
        P(),
        P(),
        P(),
    )
    return jax.shard_map(
        shards,
        mesh=mesh,
        in_specs=placed,
        out_specs=(
            P(None, "tok", ("section", "head"), None),
            P("tok", ("section", "head"), None),
            P("tok", ("section", "head"), None),
        ),
        check_vma=False,
    )
```

```python
import functools
import math

import jax
import jax.numpy as jnp
from jax import lax
from jax.experimental import pallas as pl
from jax.experimental.pallas import tpu as pltpu
from jax.sharding import PartitionSpec as P

STEPS = 28
MOST = 8


norm_eps = 1e-06
time_shift = 3.0
rope_base = 10000.0


def layer_norm(inputs):
    average = jnp.mean(inputs, axis=-1, keepdims=True)
    centred = inputs - average
    variance = jnp.mean(centred * centred, axis=-1, keepdims=True)
    return centred * lax.rsqrt(variance + norm_eps)


def rms_norm(inputs, gains):
    return inputs * lax.rsqrt(jnp.mean(inputs * inputs, axis=-1, keepdims=True) + norm_eps) * gains


def rotate(inputs, positions):
    half_dim = inputs.shape[-1] // 2
    frequency = rope_base ** (-2.0 * jnp.arange(half_dim, dtype=jnp.float32) / inputs.shape[-1])
    angles = positions[..., None, None] * frequency
    pairs = inputs.reshape(inputs.shape[:-1] + (half_dim, 2))
    even_lane = pairs[..., 0]
    odd_lane = pairs[..., 1]
    cosine = jnp.cos(angles)
    sine = jnp.sin(angles)
    turned = jnp.stack(
        [even_lane * cosine - odd_lane * sine, even_lane * sine + odd_lane * cosine], axis=-1
    )
    return turned.reshape(inputs.shape)


def slot_layout(request_patches, patch_order):
    request_ends = jnp.cumsum(request_patches)
    starts = request_ends - request_patches
    request_of = jnp.sum((request_ends[None, :] <= patch_order[:, None]).astype(jnp.int32), axis=1)
    chosen = request_of[:, None] == jnp.arange(request_patches.shape[0], dtype=jnp.int32)[None, :]
    first_patch = jnp.sum(jnp.where(chosen, starts[None, :], 0), axis=1)
    return (request_of, patch_order - first_patch)


def project(inputs, layer_mod, weight, gains, positions, head_dim):
    normed = (layer_norm(inputs.astype(jnp.float32)) * (1.0 + layer_mod[1]) + layer_mod[0]).astype(
        jnp.bfloat16
    )
    rows = inputs.shape[0]
    column_count = weight.shape[2]
    heads = column_count // head_dim
    pieces = [
        jnp.dot(normed, weight[:, part, :], preferred_element_type=jnp.float32).reshape(
            rows, heads, head_dim
        )
        for part in range(3)
    ]
    queries = rotate(rms_norm(pieces[0], gains[0]), positions).astype(jnp.bfloat16)
    keys_fresh = rotate(rms_norm(pieces[1], gains[1]), positions).astype(jnp.bfloat16)
    values_fresh = pieces[2].astype(jnp.bfloat16)
    return (
        queries.reshape(rows, column_count),
        keys_fresh.reshape(rows, column_count),
        values_fresh.reshape(rows, column_count),
    )


def fresh_kernel(head_dim, q_ref, kf_ref, vf_ref, qt_ref, m_ref, l_ref, acc_ref):
    heads = q_ref.shape[1] // head_dim
    scaling = 1.0 / math.sqrt(head_dim)
    by_key = (((0,), (0,)), ((), ()))
    for h in range(heads):
        lanes = slice(h * head_dim, (h + 1) * head_dim)
        qt_ref[h] = q_ref[:, lanes].T
        scores = jnp.dot(kf_ref[:, lanes], qt_ref[h], preferred_element_type=jnp.float32) * scaling
        col_max = jnp.max(scores, axis=0, keepdims=True)
        weights = jnp.exp(scores - col_max)
        m_ref[h] = col_max
        l_ref[h] = jnp.sum(weights, axis=0, keepdims=True)
        acc_ref[h] = lax.dot_general(
            vf_ref[:, lanes], weights.astype(jnp.bfloat16), by_key,
            preferred_element_type=jnp.float32,
        )


def attention_kernel(
    head_dim, fetch_ref, allow_ref, qt_ref, m0_ref, l0_ref, acc0_ref, ks_ref, vs_ref, mine_ref,
    theirs_ref, m_sc, l_sc, acc_sc
):
    slot = pl.program_id(0)
    heads = qt_ref.shape[0]
    scaling = 1.0 / math.sqrt(head_dim)
    by_key = (((0,), (0,)), ((), ()))

    @pl.when(slot == 0)
    def _start():
        m_sc[...] = m0_ref[...]
        l_sc[...] = l0_ref[...]
        acc_sc[...] = acc0_ref[...]

    @pl.when(allow_ref[slot] != 0)
    def _stale():
        for h in range(heads):
            lanes = slice(h * head_dim, (h + 1) * head_dim)
            scores = (
                jnp.dot(ks_ref[:, lanes], qt_ref[h], preferred_element_type=jnp.float32) * scaling
            )
            old_max = m_sc[h]
            new_max = jnp.maximum(old_max, jnp.max(scores, axis=0, keepdims=True))
            factor = jnp.exp(old_max - new_max)
            weights = jnp.exp(scores - new_max)
            l_sc[h] = l_sc[h] * factor + jnp.sum(weights, axis=0, keepdims=True)
            acc_sc[h] = acc_sc[h] * factor + lax.dot_general(
                vs_ref[:, lanes], weights.astype(jnp.bfloat16), by_key,
                preferred_element_type=jnp.float32,
            )
            m_sc[h] = new_max

    @pl.when(slot == pl.num_programs(0) - 1)
    def _finish():
        first = lax.axis_index("section") == 0
        half_rows = mine_ref.shape[0]
        for h in range(heads):
            lanes = slice(h * head_dim, (h + 1) * head_dim)
            result = (acc_sc[h] / l_sc[h]).T.astype(mine_ref.dtype)
            top = result[:half_rows]
            bottom = result[half_rows:]
            mine_ref[:, lanes] = jnp.where(first, top, bottom)
            theirs_ref[:, lanes] = jnp.where(first, bottom, top)


def attend(queries, keys_fresh, values_fresh, stale, fetch, allow, head_dim):
    rows, features = queries.shape
    slot_total = fetch.shape[0]
    heads = features // head_dim
    vmem = pl.BlockSpec(memory_space=pltpu.VMEM)
    state = pl.pallas_call(
        functools.partial(fresh_kernel, head_dim),
        out_shape=(
            jax.ShapeDtypeStruct((heads, head_dim, rows), jnp.bfloat16),
            jax.ShapeDtypeStruct((heads, 1, rows), jnp.float32),
            jax.ShapeDtypeStruct((heads, 1, rows), jnp.float32),
            jax.ShapeDtypeStruct((heads, head_dim, rows), jnp.float32),
        ),
        in_specs=[vmem] * 3,
        out_specs=(vmem,) * 4,
    )(queries, keys_fresh, values_fresh)
    half = pl.BlockSpec((rows // 2, features), lambda j, f, a: (0, 0))
    qt_spec = pl.BlockSpec((heads, head_dim, rows), lambda j, f, a: (0, 0, 0))
    stat_spec = pl.BlockSpec((heads, 1, rows), lambda j, f, a: (0, 0, 0))
    key_spec = pl.BlockSpec(
        (None, None, rows, features), lambda j, f, a: (f[j], 0, 0, 0)
    )
    value_spec = pl.BlockSpec(
        (None, None, rows, features), lambda j, f, a: (f[j], 1, 0, 0)
    )
    return pl.pallas_call(
        functools.partial(attention_kernel, head_dim),
        out_shape=(
            jax.ShapeDtypeStruct((rows // 2, features), jnp.bfloat16),
            jax.ShapeDtypeStruct((rows // 2, features), jnp.bfloat16),
        ),
        grid_spec=pltpu.PrefetchScalarGridSpec(
            num_scalar_prefetch=2,
            grid=(slot_total,),
            in_specs=[qt_spec, stat_spec, stat_spec, qt_spec, key_spec, value_spec],
            out_specs=(half, half),
            scratch_shapes=[
                pltpu.VMEM((heads, 1, rows), jnp.float32),
                pltpu.VMEM((heads, 1, rows), jnp.float32),
                pltpu.VMEM((heads, head_dim, rows), jnp.float32),
            ],
        ),
        compiler_params=pltpu.CompilerParams(dimension_semantics=("arbitrary",)),
    )(fetch, allow, *state, stale, stale)


def exchange_kernel(head_count, own_rows, split, gather, part_ref, own_ref, gate_ref, *rest):
    if gather:
        (out_ref, full_ref, land_a, land_b, sums_a, sums_b, acc,
         r_send, r_recv, a_send, a_recv, g2_send, g2_recv) = rest
    else:
        (out_ref, land_a, land_b, sums_a, sums_b, acc, r_send, r_recv) = rest
    mesh_ids = pl.DeviceIdType.MESH
    section = lax.axis_index("section")
    head = lax.axis_index("head")
    tok = lax.axis_index("tok")
    other = 1 - section
    up = lax.rem(head + 1, head_count)
    down = lax.rem(head + head_count - 1, head_count)
    opposite = lax.rem(head + 2, head_count)
    low = pl.ds(0, split)
    high = pl.ds(split, own_rows - split)

    def rows_of(block, offset, count):
        return pl.ds(pl.multiple_of(block * own_rows + offset, 16), count)

    barrier = pltpu.get_barrier_semaphore()
    pl.semaphore_signal(barrier, inc=1, device_id=(other, head, tok), device_id_type=mesh_ids)
    for h in range(head_count):
        @pl.when(h != head)
        def _greet():
            pl.semaphore_signal(barrier, inc=1, device_id=(section, h, tok), device_id_type=mesh_ids)
    pl.semaphore_wait(barrier, head_count)

    def ring(kind, src, dst, target, send_sem, recv_sem):
        return pltpu.make_async_remote_copy(
            src_ref=src,
            dst_ref=dst,
            send_sem=send_sem.at[kind],
            recv_sem=recv_sem.at[kind],
            device_id=(section, target, tok),
            device_id_type=mesh_ids,
        )

    low_count = split
    high_count = own_rows - split
    pass_a = ring(0, part_ref.at[rows_of(opposite, 0, low_count)], land_a.at[0], up, r_send, r_recv)
    pass_b = ring(1, part_ref.at[rows_of(opposite, split, high_count)], land_b.at[0], down, r_send, r_recv)
    direct_a = ring(2, part_ref.at[rows_of(down, 0, low_count)], land_a.at[1], down, r_send, r_recv)
    direct_b = ring(3, part_ref.at[rows_of(up, split, high_count)], land_b.at[1], up, r_send, r_recv)
    pass_a.start()
    pass_b.start()
    direct_a.start()
    direct_b.start()
    acc[...] = part_ref[rows_of(head, 0, own_rows), :].astype(jnp.float32)
    pass_a.wait()
    sums_a[...] = (
        part_ref[rows_of(up, 0, low_count), :].astype(jnp.float32) + land_a[0].astype(jnp.float32)
    ).astype(sums_a.dtype)
    joined_a = ring(4, sums_a, land_a.at[2], up, r_send, r_recv)
    joined_a.start()
    pass_b.wait()
    sums_b[...] = (
        part_ref[rows_of(down, split, high_count), :].astype(jnp.float32)
        + land_b[0].astype(jnp.float32)
    ).astype(sums_b.dtype)
    joined_b = ring(5, sums_b, land_b.at[2], down, r_send, r_recv)
    joined_b.start()
    direct_a.wait()
    direct_b.wait()
    joined_a.wait()
    joined_b.wait()
    acc[low, :] += land_a[1].astype(jnp.float32) + land_a[2].astype(jnp.float32)
    acc[high, :] += land_b[1].astype(jnp.float32) + land_b[2].astype(jnp.float32)
    if not gather:
        out_ref[...] = acc[...]
        return
    result = (own_ref[...].astype(jnp.float32) + gate_ref[...] * acc[...]).astype(full_ref.dtype)
    full_ref[section, head] = result
    out_ref[...] = result

    def pass_copy(h):
        return pltpu.make_async_remote_copy(
            src_ref=full_ref.at[section, h],
            dst_ref=full_ref.at[section, h],
            send_sem=g2_send.at[h],
            recv_sem=g2_recv.at[h],
            device_id=(other, head, tok),
            device_id_type=mesh_ids,
        )

    to_up = ring(0, full_ref.at[section, head], full_ref.at[section, head], up, a_send, a_recv)
    to_down = ring(1, full_ref.at[section, head], full_ref.at[section, head], down, a_send, a_recv)
    to_up.start()
    to_down.start()
    pass_copy(head).start()
    to_up.wait()
    onward_a = ring(
        2, full_ref.at[section, down, low], full_ref.at[section, down, low], up, a_send, a_recv
    )
    onward_a.start()
    pass_copy(down).start()
    to_down.wait()
    onward_b = ring(
        3, full_ref.at[section, up, high], full_ref.at[section, up, high], down, a_send, a_recv
    )
    onward_b.start()
    pass_copy(up).start()
    onward_a.wait()
    onward_b.wait()
    pass_copy(opposite).start()
    pass_copy(head).wait()
    pass_copy(down).wait()
    pass_copy(up).wait()
    pass_copy(opposite).wait()


def exchange(partial, own_input, gate, layer_idx, gather, head_count, own_rows):
    rows, width = partial.shape
    split = (own_rows * 2 // 3) // 16 * 16
    vmem = pl.BlockSpec(memory_space=pltpu.VMEM)
    scratch = [
        pltpu.VMEM((3, split, width), partial.dtype),
        pltpu.VMEM((3, own_rows - split, width), partial.dtype),
        pltpu.VMEM((split, width), partial.dtype),
        pltpu.VMEM((own_rows - split, width), partial.dtype),
        pltpu.VMEM((own_rows, width), jnp.float32),
        pltpu.SemaphoreType.DMA((6,)),
        pltpu.SemaphoreType.DMA((6,)),
    ]
    if gather:
        out_shape = (
            jax.ShapeDtypeStruct((own_rows, width), jnp.bfloat16),
            jax.ShapeDtypeStruct((2, head_count, own_rows, width), jnp.bfloat16),
        )
        out_specs = (vmem, vmem)
        scratch += [pltpu.SemaphoreType.DMA((head_count,))] * 4
    else:
        out_shape = jax.ShapeDtypeStruct((own_rows, width), jnp.float32)
        out_specs = vmem
    return pl.pallas_call(
        functools.partial(exchange_kernel, head_count, own_rows, split, gather),
        out_shape=out_shape,
        in_specs=[vmem, vmem, vmem],
        out_specs=out_specs,
        scratch_shapes=scratch,
        compiler_params=pltpu.CompilerParams(
            collective_id=layer_idx, has_side_effects=True, vmem_limit_bytes=48 * 1024 * 1024
        ),
    )(partial, own_input, gate.reshape(1, width))


def noise_level(position):
    time_left = 1.0 - position.astype(jnp.float32) / STEPS
    return time_shift * time_left / (1.0 + (time_shift - 1.0) * time_left)


def shards(
    hidden,
    latent,
    w_qkv,
    w_out,
    w_final,
    qk_gain,
    modulation,
    stale_kv,
    request_patches,
    patch_order,
    step_index,
):
    section_count = lax.axis_size("section")
    head_count = lax.axis_size("head")
    group_count = section_count * head_count
    section_index = lax.axis_index("section")
    head_index = lax.axis_index("head")
    tok_index = lax.axis_index("tok")
    group_index = section_index * head_count + head_index
    patch_len = hidden.shape[1]
    width = hidden.shape[2]
    head_dim = qk_gain.shape[-1]
    own_rows = patch_len // group_count
    layer_count = w_qkv.shape[0]
    request_of, offsets = slot_layout(request_patches, patch_order)
    slot_total = request_of.shape[0]
    my_request = request_of[tok_index]
    my_offset = offsets[tok_index]
    positions = (my_offset * patch_len + jnp.arange(patch_len, dtype=jnp.int32)).astype(jnp.float32)
    slot_ids = jnp.arange(slot_total, dtype=jnp.int32)
    allowed = (request_of == my_request) & (slot_ids != tok_index)
    rank = jnp.cumsum(allowed.astype(jnp.int32)) - 1
    count = jnp.sum(allowed.astype(jnp.int32))
    step_ids = jnp.arange(MOST - 1, dtype=jnp.int32)
    picked = allowed[None, :] & (rank[None, :] == step_ids[:, None])
    compact = jnp.sum(jnp.where(picked, slot_ids[None, :], 0), axis=1)
    last_pick = jnp.sum(jnp.where(allowed & (rank == count - 1), slot_ids, 0))
    fetch = jnp.where(step_ids < count, compact, last_pick).astype(jnp.int32)
    allow = (step_ids < count).astype(jnp.int32)
    stale_layers = [
        lax.all_gather(jnp.swapaxes(stale_kv[layer], 0, 1), "tok", axis=0, tiled=True)
        for layer in range(layer_count)
    ]
    current_full = hidden[0]
    w_partner = lax.ppermute(w_out, "section", perm=[(0, 1), (1, 0)])
    own_input = lax.dynamic_slice_in_dim(current_full, group_index * own_rows, own_rows, 0)
    outputs = []
    for layer_idx in range(layer_count):
        queries, keys_fresh, values_fresh = project(
            current_full,
            modulation[layer_idx],
            w_qkv[layer_idx],
            qk_gain[layer_idx],
            positions,
            head_dim,
        )
        attended = attend(
            queries, keys_fresh, values_fresh, stale_layers[layer_idx], fetch, allow, head_dim
        )
        mine, theirs = attended
        swapped = lax.ppermute(theirs, "section", perm=[(0, 1), (1, 0)])
        partial = (
            jnp.dot(mine, w_out[layer_idx], preferred_element_type=jnp.float32)
            + jnp.dot(swapped, w_partner[layer_idx], preferred_element_type=jnp.float32)
        ).astype(jnp.bfloat16)
        gate = modulation[layer_idx, 2]
        if layer_idx + 1 < layer_count:
            own_out, gathered = exchange(
                partial, own_input, gate, layer_idx, True, head_count, own_rows
            )
            current_full = gathered.reshape(patch_len, width)
        else:
            summed = exchange(partial, own_input, gate, layer_idx, False, head_count, own_rows)
            own_out = (own_input.astype(jnp.float32) + gate * summed).astype(jnp.bfloat16)
        own_input = own_out
        outputs.append(own_out)
    last_own = outputs[-1]
    layer_out = jnp.stack(outputs)[:, None]
    normed = layer_norm(last_own.astype(jnp.float32)).astype(jnp.bfloat16)
    velocity = jnp.dot(normed, w_final, preferred_element_type=jnp.float32)[None]
    level_now = noise_level(step_index[0])
    level_next = noise_level(step_index[0] + 1)
    return (layer_out, latent + (level_next - level_now) * velocity, latent - level_now * velocity)


def solution(mesh):
    placed = (
        P("tok", None, None),
        P("tok", ("section", "head"), None),
        P(None, None, None, ("section", "head")),
        P(None, ("section", "head"), None),
        P(),
        P(),
        P(),
        P(None, None, "tok", None, ("section", "head")),
        P(),
        P(),
        P(),
    )
    return jax.shard_map(
        shards,
        mesh=mesh,
        in_specs=placed,
        out_specs=(
            P(None, "tok", ("section", "head"), None),
            P("tok", ("section", "head"), None),
            P("tok", ("section", "head"), None),
        ),
        check_vma=False,
    )
```

```python
import functools
import math

import jax
import jax.numpy as jnp
from jax import lax
from jax.experimental import pallas as pl
from jax.experimental.pallas import tpu as pltpu
from jax.sharding import PartitionSpec as P

STEPS = 28
MOST = 8


norm_eps = 1e-06
time_shift = 3.0
rope_base = 10000.0


def layer_norm(inputs):
    average = jnp.mean(inputs, axis=-1, keepdims=True)
    centred = inputs - average
    variance = jnp.mean(centred * centred, axis=-1, keepdims=True)
    return centred * lax.rsqrt(variance + norm_eps)


def rms_norm(inputs, gains):
    return inputs * lax.rsqrt(jnp.mean(inputs * inputs, axis=-1, keepdims=True) + norm_eps) * gains


def rotate(inputs, positions):
    half_dim = inputs.shape[-1] // 2
    frequency = rope_base ** (-2.0 * jnp.arange(half_dim, dtype=jnp.float32) / inputs.shape[-1])
    angles = positions[..., None, None] * frequency
    pairs = inputs.reshape(inputs.shape[:-1] + (half_dim, 2))
    even_lane = pairs[..., 0]
    odd_lane = pairs[..., 1]
    cosine = jnp.cos(angles)
    sine = jnp.sin(angles)
    turned = jnp.stack(
        [even_lane * cosine - odd_lane * sine, even_lane * sine + odd_lane * cosine], axis=-1
    )
    return turned.reshape(inputs.shape)


def slot_layout(request_patches, patch_order):
    request_ends = jnp.cumsum(request_patches)
    starts = request_ends - request_patches
    request_of = jnp.sum((request_ends[None, :] <= patch_order[:, None]).astype(jnp.int32), axis=1)
    chosen = request_of[:, None] == jnp.arange(request_patches.shape[0], dtype=jnp.int32)[None, :]
    first_patch = jnp.sum(jnp.where(chosen, starts[None, :], 0), axis=1)
    return (request_of, patch_order - first_patch)


def project(inputs, layer_mod, weight, gains, positions, head_dim):
    normed = (layer_norm(inputs.astype(jnp.float32)) * (1.0 + layer_mod[1]) + layer_mod[0]).astype(
        jnp.bfloat16
    )
    rows = inputs.shape[0]
    column_count = weight.shape[2]
    heads = column_count // head_dim
    pieces = [
        jnp.dot(normed, weight[:, part, :], preferred_element_type=jnp.float32).reshape(
            rows, heads, head_dim
        )
        for part in range(3)
    ]
    queries = rotate(rms_norm(pieces[0], gains[0]), positions).astype(jnp.bfloat16)
    keys_fresh = rotate(rms_norm(pieces[1], gains[1]), positions).astype(jnp.bfloat16)
    values_fresh = pieces[2].astype(jnp.bfloat16)
    return (
        queries.reshape(rows, column_count),
        keys_fresh.reshape(rows, column_count),
        values_fresh.reshape(rows, column_count),
    )


def fresh_kernel(head_dim, q_ref, kf_ref, vf_ref, qt_ref, m_ref, l_ref, acc_ref):
    heads = q_ref.shape[1] // head_dim
    scaling = 1.0 / math.sqrt(head_dim)
    by_key = (((0,), (0,)), ((), ()))
    for h in range(heads):
        lanes = slice(h * head_dim, (h + 1) * head_dim)
        qt_ref[h] = q_ref[:, lanes].T
        scores = jnp.dot(kf_ref[:, lanes], qt_ref[h], preferred_element_type=jnp.float32) * scaling
        col_max = jnp.max(scores, axis=0, keepdims=True)
        weights = jnp.exp(scores - col_max)
        m_ref[h] = col_max
        l_ref[h] = jnp.sum(weights, axis=0, keepdims=True)
        acc_ref[h] = lax.dot_general(
            vf_ref[:, lanes], weights.astype(jnp.bfloat16), by_key,
            preferred_element_type=jnp.float32,
        )


def attention_kernel(
    head_dim, fetch_ref, allow_ref, qt_ref, m0_ref, l0_ref, acc0_ref, ks_ref, vs_ref, mine_ref,
    theirs_ref, m_sc, l_sc, acc_sc
):
    slot = pl.program_id(0)
    heads = qt_ref.shape[0]
    scaling = 1.0 / math.sqrt(head_dim)
    by_key = (((0,), (0,)), ((), ()))

    @pl.when(slot == 0)
    def _start():
        m_sc[...] = m0_ref[...]
        l_sc[...] = l0_ref[...]
        acc_sc[...] = acc0_ref[...]

    @pl.when(allow_ref[slot] != 0)
    def _stale():
        for h in range(heads):
            lanes = slice(h * head_dim, (h + 1) * head_dim)
            scores = (
                jnp.dot(ks_ref[:, lanes], qt_ref[h], preferred_element_type=jnp.float32) * scaling
            )
            old_max = m_sc[h]
            new_max = jnp.maximum(old_max, jnp.max(scores, axis=0, keepdims=True))
            factor = jnp.exp(old_max - new_max)
            weights = jnp.exp(scores - new_max)
            l_sc[h] = l_sc[h] * factor + jnp.sum(weights, axis=0, keepdims=True)
            acc_sc[h] = acc_sc[h] * factor + lax.dot_general(
                vs_ref[:, lanes], weights.astype(jnp.bfloat16), by_key,
                preferred_element_type=jnp.float32,
            )
            m_sc[h] = new_max

    @pl.when(slot == pl.num_programs(0) - 1)
    def _finish():
        first = lax.axis_index("section") == 0
        half_rows = mine_ref.shape[0]
        for h in range(heads):
            lanes = slice(h * head_dim, (h + 1) * head_dim)
            result = (acc_sc[h] / l_sc[h]).T.astype(mine_ref.dtype)
            top = result[:half_rows]
            bottom = result[half_rows:]
            mine_ref[:, lanes] = jnp.where(first, top, bottom)
            theirs_ref[:, lanes] = jnp.where(first, bottom, top)


def attend(queries, keys_fresh, values_fresh, stale, fetch, allow, head_dim):
    rows, features = queries.shape
    slot_total = fetch.shape[0]
    heads = features // head_dim
    vmem = pl.BlockSpec(memory_space=pltpu.VMEM)
    state = pl.pallas_call(
        functools.partial(fresh_kernel, head_dim),
        out_shape=(
            jax.ShapeDtypeStruct((heads, head_dim, rows), jnp.bfloat16),
            jax.ShapeDtypeStruct((heads, 1, rows), jnp.float32),
            jax.ShapeDtypeStruct((heads, 1, rows), jnp.float32),
            jax.ShapeDtypeStruct((heads, head_dim, rows), jnp.float32),
        ),
        in_specs=[vmem] * 3,
        out_specs=(vmem,) * 4,
    )(queries, keys_fresh, values_fresh)
    half = pl.BlockSpec((rows // 2, features), lambda j, f, a: (0, 0))
    qt_spec = pl.BlockSpec((heads, head_dim, rows), lambda j, f, a: (0, 0, 0))
    stat_spec = pl.BlockSpec((heads, 1, rows), lambda j, f, a: (0, 0, 0))
    key_spec = pl.BlockSpec(
        (None, None, rows, features), lambda j, f, a: (f[j], 0, 0, 0)
    )
    value_spec = pl.BlockSpec(
        (None, None, rows, features), lambda j, f, a: (f[j], 1, 0, 0)
    )
    return pl.pallas_call(
        functools.partial(attention_kernel, head_dim),
        out_shape=(
            jax.ShapeDtypeStruct((rows // 2, features), jnp.bfloat16),
            jax.ShapeDtypeStruct((rows // 2, features), jnp.bfloat16),
        ),
        grid_spec=pltpu.PrefetchScalarGridSpec(
            num_scalar_prefetch=2,
            grid=(slot_total,),
            in_specs=[qt_spec, stat_spec, stat_spec, qt_spec, key_spec, value_spec],
            out_specs=(half, half),
            scratch_shapes=[
                pltpu.VMEM((heads, 1, rows), jnp.float32),
                pltpu.VMEM((heads, 1, rows), jnp.float32),
                pltpu.VMEM((heads, head_dim, rows), jnp.float32),
            ],
        ),
        compiler_params=pltpu.CompilerParams(dimension_semantics=("arbitrary",)),
    )(fetch, allow, *state, stale, stale)


def exchange_kernel(head_count, own_rows, split, gather, part_ref, own_ref, gate_ref, *rest):
    if gather:
        (out_ref, full_ref, land_a, land_b, sums_a, sums_b, acc,
         r_send, r_recv, a_send, a_recv, g2_send, g2_recv) = rest
    else:
        (out_ref, land_a, land_b, sums_a, sums_b, acc, r_send, r_recv) = rest
    mesh_ids = pl.DeviceIdType.MESH
    section = lax.axis_index("section")
    head = lax.axis_index("head")
    tok = lax.axis_index("tok")
    other = 1 - section
    up = lax.rem(head + 1, head_count)
    down = lax.rem(head + head_count - 1, head_count)
    opposite = lax.rem(head + 2, head_count)
    low = pl.ds(0, split)
    high = pl.ds(split, own_rows - split)

    def rows_of(block, offset, count):
        return pl.ds(pl.multiple_of(block * own_rows + offset, 16), count)

    barrier = pltpu.get_barrier_semaphore()
    if gather:
        pl.semaphore_signal(barrier, inc=1, device_id=(other, head, tok), device_id_type=mesh_ids)
    for neighbour in (up, down):
        pl.semaphore_signal(barrier, inc=1, device_id=(section, neighbour, tok), device_id_type=mesh_ids)
    pl.semaphore_wait(barrier, 3 if gather else 2)

    def ring(kind, src, dst, target, send_sem, recv_sem):
        return pltpu.make_async_remote_copy(
            src_ref=src,
            dst_ref=dst,
            send_sem=send_sem.at[kind],
            recv_sem=recv_sem.at[kind],
            device_id=(section, target, tok),
            device_id_type=mesh_ids,
        )

    low_count = split
    high_count = own_rows - split
    pass_a = ring(0, part_ref.at[rows_of(opposite, 0, low_count)], land_a.at[0], up, r_send, r_recv)
    pass_b = ring(1, part_ref.at[rows_of(opposite, split, high_count)], land_b.at[0], down, r_send, r_recv)
    direct_a = ring(2, part_ref.at[rows_of(down, 0, low_count)], land_a.at[1], down, r_send, r_recv)
    direct_b = ring(3, part_ref.at[rows_of(up, split, high_count)], land_b.at[1], up, r_send, r_recv)
    pass_a.start()
    pass_b.start()
    direct_a.start()
    direct_b.start()
    acc[...] = part_ref[rows_of(head, 0, own_rows), :].astype(jnp.float32)
    pass_a.wait()
    sums_a[...] = (
        part_ref[rows_of(up, 0, low_count), :].astype(jnp.float32) + land_a[0].astype(jnp.float32)
    ).astype(sums_a.dtype)
    joined_a = ring(4, sums_a, land_a.at[2], up, r_send, r_recv)
    joined_a.start()
    pass_b.wait()
    sums_b[...] = (
        part_ref[rows_of(down, split, high_count), :].astype(jnp.float32)
        + land_b[0].astype(jnp.float32)
    ).astype(sums_b.dtype)
    joined_b = ring(5, sums_b, land_b.at[2], down, r_send, r_recv)
    joined_b.start()
    direct_a.wait()
    direct_b.wait()
    joined_a.wait()
    joined_b.wait()
    acc[low, :] += land_a[1].astype(jnp.float32) + land_a[2].astype(jnp.float32)
    acc[high, :] += land_b[1].astype(jnp.float32) + land_b[2].astype(jnp.float32)
    if not gather:
        out_ref[...] = acc[...]
        return
    result = (own_ref[...].astype(jnp.float32) + gate_ref[...] * acc[...]).astype(full_ref.dtype)
    full_ref[section, head] = result
    out_ref[...] = result

    def pass_copy(h):
        return pltpu.make_async_remote_copy(
            src_ref=full_ref.at[section, h],
            dst_ref=full_ref.at[section, h],
            send_sem=g2_send.at[h],
            recv_sem=g2_recv.at[h],
            device_id=(other, head, tok),
            device_id_type=mesh_ids,
        )

    to_up = ring(0, full_ref.at[section, head], full_ref.at[section, head], up, a_send, a_recv)
    to_down = ring(1, full_ref.at[section, head], full_ref.at[section, head], down, a_send, a_recv)
    to_up.start()
    to_down.start()
    pass_copy(head).start()
    to_up.wait()
    onward_a = ring(
        2, full_ref.at[section, down, low], full_ref.at[section, down, low], up, a_send, a_recv
    )
    onward_a.start()
    pass_copy(down).start()
    to_down.wait()
    onward_b = ring(
        3, full_ref.at[section, up, high], full_ref.at[section, up, high], down, a_send, a_recv
    )
    onward_b.start()
    pass_copy(up).start()
    onward_a.wait()
    onward_b.wait()
    pass_copy(opposite).start()
    pass_copy(head).wait()
    pass_copy(down).wait()
    pass_copy(up).wait()
    pass_copy(opposite).wait()


def exchange(partial, own_input, gate, layer_idx, gather, head_count, own_rows):
    rows, width = partial.shape
    split = (own_rows * 2 // 3) // 16 * 16
    vmem = pl.BlockSpec(memory_space=pltpu.VMEM)
    scratch = [
        pltpu.VMEM((3, split, width), partial.dtype),
        pltpu.VMEM((3, own_rows - split, width), partial.dtype),
        pltpu.VMEM((split, width), partial.dtype),
        pltpu.VMEM((own_rows - split, width), partial.dtype),
        pltpu.VMEM((own_rows, width), jnp.float32),
        pltpu.SemaphoreType.DMA((6,)),
        pltpu.SemaphoreType.DMA((6,)),
    ]
    if gather:
        out_shape = (
            jax.ShapeDtypeStruct((own_rows, width), jnp.bfloat16),
            jax.ShapeDtypeStruct((2, head_count, own_rows, width), jnp.bfloat16),
        )
        out_specs = (vmem, vmem)
        scratch += [pltpu.SemaphoreType.DMA((head_count,))] * 4
    else:
        out_shape = jax.ShapeDtypeStruct((own_rows, width), jnp.float32)
        out_specs = vmem
    return pl.pallas_call(
        functools.partial(exchange_kernel, head_count, own_rows, split, gather),
        out_shape=out_shape,
        in_specs=[vmem, vmem, vmem],
        out_specs=out_specs,
        scratch_shapes=scratch,
        compiler_params=pltpu.CompilerParams(
            collective_id=layer_idx, has_side_effects=True, vmem_limit_bytes=48 * 1024 * 1024
        ),
    )(partial, own_input, gate.reshape(1, width))


def noise_level(position):
    time_left = 1.0 - position.astype(jnp.float32) / STEPS
    return time_shift * time_left / (1.0 + (time_shift - 1.0) * time_left)


def shards(
    hidden,
    latent,
    w_qkv,
    w_out,
    w_final,
    qk_gain,
    modulation,
    stale_kv,
    request_patches,
    patch_order,
    step_index,
):
    section_count = lax.axis_size("section")
    head_count = lax.axis_size("head")
    group_count = section_count * head_count
    section_index = lax.axis_index("section")
    head_index = lax.axis_index("head")
    tok_index = lax.axis_index("tok")
    group_index = section_index * head_count + head_index
    patch_len = hidden.shape[1]
    width = hidden.shape[2]
    head_dim = qk_gain.shape[-1]
    own_rows = patch_len // group_count
    layer_count = w_qkv.shape[0]
    request_of, offsets = slot_layout(request_patches, patch_order)
    slot_total = request_of.shape[0]
    my_request = request_of[tok_index]
    my_offset = offsets[tok_index]
    positions = (my_offset * patch_len + jnp.arange(patch_len, dtype=jnp.int32)).astype(jnp.float32)
    slot_ids = jnp.arange(slot_total, dtype=jnp.int32)
    allowed = (request_of == my_request) & (slot_ids != tok_index)
    rank = jnp.cumsum(allowed.astype(jnp.int32)) - 1
    count = jnp.sum(allowed.astype(jnp.int32))
    step_ids = jnp.arange(MOST - 1, dtype=jnp.int32)
    picked = allowed[None, :] & (rank[None, :] == step_ids[:, None])
    compact = jnp.sum(jnp.where(picked, slot_ids[None, :], 0), axis=1)
    last_pick = jnp.sum(jnp.where(allowed & (rank == count - 1), slot_ids, 0))
    fetch = jnp.where(step_ids < count, compact, last_pick).astype(jnp.int32)
    allow = (step_ids < count).astype(jnp.int32)
    stale_layers = [
        lax.all_gather(jnp.swapaxes(stale_kv[layer], 0, 1), "tok", axis=0, tiled=True)
        for layer in range(layer_count)
    ]
    current_full = hidden[0]
    w_partner = lax.ppermute(w_out, "section", perm=[(0, 1), (1, 0)])
    own_input = lax.dynamic_slice_in_dim(current_full, group_index * own_rows, own_rows, 0)
    outputs = []
    for layer_idx in range(layer_count):
        queries, keys_fresh, values_fresh = project(
            current_full,
            modulation[layer_idx],
            w_qkv[layer_idx],
            qk_gain[layer_idx],
            positions,
            head_dim,
        )
        attended = attend(
            queries, keys_fresh, values_fresh, stale_layers[layer_idx], fetch, allow, head_dim
        )
        mine, theirs = attended
        swapped = lax.ppermute(theirs, "section", perm=[(0, 1), (1, 0)])
        partial = (
            jnp.dot(mine, w_out[layer_idx], preferred_element_type=jnp.float32)
            + jnp.dot(swapped, w_partner[layer_idx], preferred_element_type=jnp.float32)
        ).astype(jnp.bfloat16)
        gate = modulation[layer_idx, 2]
        if layer_idx + 1 < layer_count:
            own_out, gathered = exchange(
                partial, own_input, gate, layer_idx, True, head_count, own_rows
            )
            current_full = gathered.reshape(patch_len, width)
        else:
            summed = exchange(partial, own_input, gate, layer_idx, False, head_count, own_rows)
            own_out = (own_input.astype(jnp.float32) + gate * summed).astype(jnp.bfloat16)
        own_input = own_out
        outputs.append(own_out)
    last_own = outputs[-1]
    layer_out = jnp.stack(outputs)[:, None]
    normed = layer_norm(last_own.astype(jnp.float32)).astype(jnp.bfloat16)
    velocity = jnp.dot(normed, w_final, preferred_element_type=jnp.float32)[None]
    level_now = noise_level(step_index[0])
    level_next = noise_level(step_index[0] + 1)
    return (layer_out, latent + (level_next - level_now) * velocity, latent - level_now * velocity)


def solution(mesh):
    placed = (
        P("tok", None, None),
        P("tok", ("section", "head"), None),
        P(None, None, None, ("section", "head")),
        P(None, ("section", "head"), None),
        P(),
        P(),
        P(),
        P(None, None, "tok", None, ("section", "head")),
        P(),
        P(),
        P(),
    )
    return jax.shard_map(
        shards,
        mesh=mesh,
        in_specs=placed,
        out_specs=(
            P(None, "tok", ("section", "head"), None),
            P("tok", ("section", "head"), None),
            P("tok", ("section", "head"), None),
        ),
        check_vma=False,
    )
```

```python
import functools
import math

import jax
import jax.numpy as jnp
from jax import lax
from jax.experimental import pallas as pl
from jax.experimental.pallas import tpu as pltpu
from jax.sharding import PartitionSpec as P

STEPS = 28
MOST = 8


norm_eps = 1e-06
time_shift = 3.0
rope_base = 10000.0


def layer_norm(inputs):
    average = jnp.mean(inputs, axis=-1, keepdims=True)
    centred = inputs - average
    variance = jnp.mean(centred * centred, axis=-1, keepdims=True)
    return centred * lax.rsqrt(variance + norm_eps)


def rms_norm(inputs, gains):
    return inputs * lax.rsqrt(jnp.mean(inputs * inputs, axis=-1, keepdims=True) + norm_eps) * gains


def rotate(inputs, positions):
    half_dim = inputs.shape[-1] // 2
    frequency = rope_base ** (-2.0 * jnp.arange(half_dim, dtype=jnp.float32) / inputs.shape[-1])
    angles = positions[..., None, None] * frequency
    pairs = inputs.reshape(inputs.shape[:-1] + (half_dim, 2))
    even_lane = pairs[..., 0]
    odd_lane = pairs[..., 1]
    cosine = jnp.cos(angles)
    sine = jnp.sin(angles)
    turned = jnp.stack(
        [even_lane * cosine - odd_lane * sine, even_lane * sine + odd_lane * cosine], axis=-1
    )
    return turned.reshape(inputs.shape)


def slot_layout(request_patches, patch_order):
    request_ends = jnp.cumsum(request_patches)
    starts = request_ends - request_patches
    request_of = jnp.sum((request_ends[None, :] <= patch_order[:, None]).astype(jnp.int32), axis=1)
    chosen = request_of[:, None] == jnp.arange(request_patches.shape[0], dtype=jnp.int32)[None, :]
    first_patch = jnp.sum(jnp.where(chosen, starts[None, :], 0), axis=1)
    return (request_of, patch_order - first_patch)


def project(inputs, layer_mod, weight, gains, positions, head_dim):
    normed = (layer_norm(inputs.astype(jnp.float32)) * (1.0 + layer_mod[1]) + layer_mod[0]).astype(
        jnp.bfloat16
    )
    rows = inputs.shape[0]
    column_count = weight.shape[2]
    heads = column_count // head_dim
    pieces = [
        jnp.dot(normed, weight[:, part, :], preferred_element_type=jnp.float32).reshape(
            rows, heads, head_dim
        )
        for part in range(3)
    ]
    queries = rotate(rms_norm(pieces[0], gains[0]), positions).astype(jnp.bfloat16)
    keys_fresh = rotate(rms_norm(pieces[1], gains[1]), positions).astype(jnp.bfloat16)
    values_fresh = pieces[2].astype(jnp.bfloat16)
    return (
        queries.reshape(rows, column_count),
        keys_fresh.reshape(rows, column_count),
        values_fresh.reshape(rows, column_count),
    )


def fresh_kernel(head_dim, q_ref, kf_ref, vf_ref, qt_ref, m_ref, l_ref, acc_ref):
    heads = q_ref.shape[1] // head_dim
    scaling = 1.0 / math.sqrt(head_dim)
    by_key = (((0,), (0,)), ((), ()))
    for h in range(heads):
        lanes = slice(h * head_dim, (h + 1) * head_dim)
        qt_ref[h] = q_ref[:, lanes].T
        scores = jnp.dot(kf_ref[:, lanes], qt_ref[h], preferred_element_type=jnp.float32) * scaling
        col_max = jnp.max(scores, axis=0, keepdims=True)
        weights = jnp.exp(scores - col_max)
        m_ref[h] = col_max
        l_ref[h] = jnp.sum(weights, axis=0, keepdims=True)
        acc_ref[h] = lax.dot_general(
            vf_ref[:, lanes], weights.astype(jnp.bfloat16), by_key,
            preferred_element_type=jnp.float32,
        )


def attention_kernel(
    head_dim, fetch_ref, allow_ref, qt_ref, m0_ref, l0_ref, acc0_ref, ks_ref, vs_ref, mine_ref,
    theirs_ref, m_sc, l_sc, acc_sc
):
    slot = pl.program_id(0)
    heads = qt_ref.shape[0]
    scaling = 1.0 / math.sqrt(head_dim)
    by_key = (((0,), (0,)), ((), ()))

    @pl.when(slot == 0)
    def _start():
        m_sc[...] = m0_ref[...]
        l_sc[...] = l0_ref[...]
        acc_sc[...] = acc0_ref[...]

    @pl.when(allow_ref[slot] != 0)
    def _stale():
        for h in range(heads):
            lanes = slice(h * head_dim, (h + 1) * head_dim)
            scores = (
                jnp.dot(ks_ref[:, lanes], qt_ref[h], preferred_element_type=jnp.float32) * scaling
            )
            old_max = m_sc[h]
            new_max = jnp.maximum(old_max, jnp.max(scores, axis=0, keepdims=True))
            factor = jnp.exp(old_max - new_max)
            weights = jnp.exp(scores - new_max)
            l_sc[h] = l_sc[h] * factor + jnp.sum(weights, axis=0, keepdims=True)
            acc_sc[h] = acc_sc[h] * factor + lax.dot_general(
                vs_ref[:, lanes], weights.astype(jnp.bfloat16), by_key,
                preferred_element_type=jnp.float32,
            )
            m_sc[h] = new_max

    @pl.when(slot == pl.num_programs(0) - 1)
    def _finish():
        first = lax.axis_index("section") == 0
        half_rows = mine_ref.shape[0]
        for h in range(heads):
            lanes = slice(h * head_dim, (h + 1) * head_dim)
            result = (acc_sc[h] / l_sc[h]).T.astype(mine_ref.dtype)
            top = result[:half_rows]
            bottom = result[half_rows:]
            mine_ref[:, lanes] = jnp.where(first, top, bottom)
            theirs_ref[:, lanes] = jnp.where(first, bottom, top)


def attend(queries, keys_fresh, values_fresh, stale, fetch, allow, head_dim):
    rows, features = queries.shape
    slot_total = fetch.shape[0]
    heads = features // head_dim
    vmem = pl.BlockSpec(memory_space=pltpu.VMEM)
    state = pl.pallas_call(
        functools.partial(fresh_kernel, head_dim),
        out_shape=(
            jax.ShapeDtypeStruct((heads, head_dim, rows), jnp.bfloat16),
            jax.ShapeDtypeStruct((heads, 1, rows), jnp.float32),
            jax.ShapeDtypeStruct((heads, 1, rows), jnp.float32),
            jax.ShapeDtypeStruct((heads, head_dim, rows), jnp.float32),
        ),
        in_specs=[vmem] * 3,
        out_specs=(vmem,) * 4,
    )(queries, keys_fresh, values_fresh)
    half = pl.BlockSpec((rows // 2, features), lambda j, f, a: (0, 0))
    qt_spec = pl.BlockSpec((heads, head_dim, rows), lambda j, f, a: (0, 0, 0))
    stat_spec = pl.BlockSpec((heads, 1, rows), lambda j, f, a: (0, 0, 0))
    key_spec = pl.BlockSpec(
        (None, None, rows, features), lambda j, f, a: (f[j], 0, 0, 0)
    )
    value_spec = pl.BlockSpec(
        (None, None, rows, features), lambda j, f, a: (f[j], 1, 0, 0)
    )
    return pl.pallas_call(
        functools.partial(attention_kernel, head_dim),
        out_shape=(
            jax.ShapeDtypeStruct((rows // 2, features), jnp.bfloat16),
            jax.ShapeDtypeStruct((rows // 2, features), jnp.bfloat16),
        ),
        grid_spec=pltpu.PrefetchScalarGridSpec(
            num_scalar_prefetch=2,
            grid=(slot_total,),
            in_specs=[qt_spec, stat_spec, stat_spec, qt_spec, key_spec, value_spec],
            out_specs=(half, half),
            scratch_shapes=[
                pltpu.VMEM((heads, 1, rows), jnp.float32),
                pltpu.VMEM((heads, 1, rows), jnp.float32),
                pltpu.VMEM((heads, head_dim, rows), jnp.float32),
            ],
        ),
        compiler_params=pltpu.CompilerParams(dimension_semantics=("arbitrary",)),
    )(fetch, allow, *state, stale, stale)


def exchange_kernel(head_count, own_rows, split, gather, part_ref, own_ref, gate_ref, *rest):
    if gather:
        (out_ref, full_ref, land_a, land_b, sums_a, sums_b, acc,
         r_send, r_recv, a_send, a_recv, g2_send, g2_recv) = rest
    else:
        (wf_ref, latent_ref, levels_ref, out_ref, next_ref, denoised_ref,
         land_a, land_b, sums_a, sums_b, acc, r_send, r_recv) = rest
    mesh_ids = pl.DeviceIdType.MESH
    section = lax.axis_index("section")
    head = lax.axis_index("head")
    tok = lax.axis_index("tok")
    other = 1 - section
    up = lax.rem(head + 1, head_count)
    down = lax.rem(head + head_count - 1, head_count)
    opposite = lax.rem(head + 2, head_count)
    low = pl.ds(0, split)
    high = pl.ds(split, own_rows - split)

    def rows_of(block, offset, count):
        return pl.ds(pl.multiple_of(block * own_rows + offset, 16), count)

    barrier = pltpu.get_barrier_semaphore()
    if gather:
        pl.semaphore_signal(barrier, inc=1, device_id=(other, head, tok), device_id_type=mesh_ids)
    for neighbour in (up, down):
        pl.semaphore_signal(barrier, inc=1, device_id=(section, neighbour, tok), device_id_type=mesh_ids)
    pl.semaphore_wait(barrier, 3 if gather else 2)

    def ring(kind, src, dst, target, send_sem, recv_sem):
        return pltpu.make_async_remote_copy(
            src_ref=src,
            dst_ref=dst,
            send_sem=send_sem.at[kind],
            recv_sem=recv_sem.at[kind],
            device_id=(section, target, tok),
            device_id_type=mesh_ids,
        )

    low_count = split
    high_count = own_rows - split
    pass_a = ring(0, part_ref.at[rows_of(opposite, 0, low_count)], land_a.at[0], up, r_send, r_recv)
    pass_b = ring(1, part_ref.at[rows_of(opposite, split, high_count)], land_b.at[0], down, r_send, r_recv)
    direct_a = ring(2, part_ref.at[rows_of(down, 0, low_count)], land_a.at[1], down, r_send, r_recv)
    direct_b = ring(3, part_ref.at[rows_of(up, split, high_count)], land_b.at[1], up, r_send, r_recv)
    pass_a.start()
    pass_b.start()
    direct_a.start()
    direct_b.start()
    acc[...] = part_ref[rows_of(head, 0, own_rows), :].astype(jnp.float32)
    pass_a.wait()
    sums_a[...] = (
        part_ref[rows_of(up, 0, low_count), :].astype(jnp.float32) + land_a[0].astype(jnp.float32)
    ).astype(sums_a.dtype)
    joined_a = ring(4, sums_a, land_a.at[2], up, r_send, r_recv)
    joined_a.start()
    pass_b.wait()
    sums_b[...] = (
        part_ref[rows_of(down, split, high_count), :].astype(jnp.float32)
        + land_b[0].astype(jnp.float32)
    ).astype(sums_b.dtype)
    joined_b = ring(5, sums_b, land_b.at[2], down, r_send, r_recv)
    joined_b.start()
    direct_a.wait()
    direct_b.wait()
    joined_a.wait()
    joined_b.wait()
    acc[low, :] += land_a[1].astype(jnp.float32) + land_a[2].astype(jnp.float32)
    acc[high, :] += land_b[1].astype(jnp.float32) + land_b[2].astype(jnp.float32)
    if not gather:
        final = (own_ref[...].astype(jnp.float32) + gate_ref[...] * acc[...]).astype(out_ref.dtype)
        out_ref[...] = final
        normed = layer_norm(final.astype(jnp.float32)).astype(jnp.bfloat16)
        velocity = jnp.dot(normed, wf_ref[...], preferred_element_type=jnp.float32)
        level_now = levels_ref[:, 0:1]
        level_step = levels_ref[:, 1:2]
        next_ref[...] = latent_ref[...] + level_step * velocity
        denoised_ref[...] = latent_ref[...] - level_now * velocity
        return
    result = (own_ref[...].astype(jnp.float32) + gate_ref[...] * acc[...]).astype(full_ref.dtype)
    full_ref[section, head] = result
    out_ref[...] = result

    def pass_copy(h):
        return pltpu.make_async_remote_copy(
            src_ref=full_ref.at[section, h],
            dst_ref=full_ref.at[section, h],
            send_sem=g2_send.at[h],
            recv_sem=g2_recv.at[h],
            device_id=(other, head, tok),
            device_id_type=mesh_ids,
        )

    to_up = ring(0, full_ref.at[section, head], full_ref.at[section, head], up, a_send, a_recv)
    to_down = ring(1, full_ref.at[section, head], full_ref.at[section, head], down, a_send, a_recv)
    to_up.start()
    to_down.start()
    pass_copy(head).start()
    to_up.wait()
    onward_a = ring(
        2, full_ref.at[section, down, low], full_ref.at[section, down, low], up, a_send, a_recv
    )
    onward_a.start()
    pass_copy(down).start()
    to_down.wait()
    onward_b = ring(
        3, full_ref.at[section, up, high], full_ref.at[section, up, high], down, a_send, a_recv
    )
    onward_b.start()
    pass_copy(up).start()
    onward_a.wait()
    onward_b.wait()
    pass_copy(opposite).start()
    pass_copy(head).wait()
    pass_copy(down).wait()
    pass_copy(up).wait()
    pass_copy(opposite).wait()


def exchange(partial, own_input, gate, layer_idx, gather, head_count, own_rows, tail=()):
    rows, width = partial.shape
    split = (own_rows * 2 // 3) // 16 * 16
    vmem = pl.BlockSpec(memory_space=pltpu.VMEM)
    scratch = [
        pltpu.VMEM((3, split, width), partial.dtype),
        pltpu.VMEM((3, own_rows - split, width), partial.dtype),
        pltpu.VMEM((split, width), partial.dtype),
        pltpu.VMEM((own_rows - split, width), partial.dtype),
        pltpu.VMEM((own_rows, width), jnp.float32),
        pltpu.SemaphoreType.DMA((6,)),
        pltpu.SemaphoreType.DMA((6,)),
    ]
    if gather:
        out_shape = (
            jax.ShapeDtypeStruct((own_rows, width), jnp.bfloat16),
            jax.ShapeDtypeStruct((2, head_count, own_rows, width), jnp.bfloat16),
        )
        out_specs = (vmem, vmem)
        scratch += [pltpu.SemaphoreType.DMA((head_count,))] * 4
    else:
        latent_width = tail[1].shape[1]
        out_shape = (
            jax.ShapeDtypeStruct((own_rows, width), jnp.bfloat16),
            jax.ShapeDtypeStruct((own_rows, latent_width), jnp.float32),
            jax.ShapeDtypeStruct((own_rows, latent_width), jnp.float32),
        )
        out_specs = (vmem, vmem, vmem)
    return pl.pallas_call(
        functools.partial(exchange_kernel, head_count, own_rows, split, gather),
        out_shape=out_shape,
        in_specs=[vmem] * (3 + len(tail)),
        out_specs=out_specs,
        scratch_shapes=scratch,
        compiler_params=pltpu.CompilerParams(
            collective_id=layer_idx, has_side_effects=True, vmem_limit_bytes=48 * 1024 * 1024
        ),
    )(partial, own_input, gate.reshape(1, width), *tail)


def noise_level(position):
    time_left = 1.0 - position.astype(jnp.float32) / STEPS
    return time_shift * time_left / (1.0 + (time_shift - 1.0) * time_left)


def shards(
    hidden,
    latent,
    w_qkv,
    w_out,
    w_final,
    qk_gain,
    modulation,
    stale_kv,
    request_patches,
    patch_order,
    step_index,
):
    section_count = lax.axis_size("section")
    head_count = lax.axis_size("head")
    group_count = section_count * head_count
    section_index = lax.axis_index("section")
    head_index = lax.axis_index("head")
    tok_index = lax.axis_index("tok")
    group_index = section_index * head_count + head_index
    patch_len = hidden.shape[1]
    width = hidden.shape[2]
    head_dim = qk_gain.shape[-1]
    own_rows = patch_len // group_count
    layer_count = w_qkv.shape[0]
    request_of, offsets = slot_layout(request_patches, patch_order)
    slot_total = request_of.shape[0]
    my_request = request_of[tok_index]
    my_offset = offsets[tok_index]
    positions = (my_offset * patch_len + jnp.arange(patch_len, dtype=jnp.int32)).astype(jnp.float32)
    slot_ids = jnp.arange(slot_total, dtype=jnp.int32)
    allowed = (request_of == my_request) & (slot_ids != tok_index)
    rank = jnp.cumsum(allowed.astype(jnp.int32)) - 1
    count = jnp.sum(allowed.astype(jnp.int32))
    step_ids = jnp.arange(MOST - 1, dtype=jnp.int32)
    picked = allowed[None, :] & (rank[None, :] == step_ids[:, None])
    compact = jnp.sum(jnp.where(picked, slot_ids[None, :], 0), axis=1)
    last_pick = jnp.sum(jnp.where(allowed & (rank == count - 1), slot_ids, 0))
    fetch = jnp.where(step_ids < count, compact, last_pick).astype(jnp.int32)
    allow = (step_ids < count).astype(jnp.int32)
    stale_layers = [
        lax.all_gather(jnp.swapaxes(stale_kv[layer], 0, 1), "tok", axis=0, tiled=True)
        for layer in range(layer_count)
    ]
    current_full = hidden[0]
    w_partner = lax.ppermute(w_out, "section", perm=[(0, 1), (1, 0)])
    own_input = lax.dynamic_slice_in_dim(current_full, group_index * own_rows, own_rows, 0)
    outputs = []
    for layer_idx in range(layer_count):
        queries, keys_fresh, values_fresh = project(
            current_full,
            modulation[layer_idx],
            w_qkv[layer_idx],
            qk_gain[layer_idx],
            positions,
            head_dim,
        )
        attended = attend(
            queries, keys_fresh, values_fresh, stale_layers[layer_idx], fetch, allow, head_dim
        )
        mine, theirs = attended
        swapped = lax.ppermute(theirs, "section", perm=[(0, 1), (1, 0)])
        partial = (
            jnp.dot(mine, w_out[layer_idx], preferred_element_type=jnp.float32)
            + jnp.dot(swapped, w_partner[layer_idx], preferred_element_type=jnp.float32)
        ).astype(jnp.bfloat16)
        gate = modulation[layer_idx, 2]
        if layer_idx + 1 < layer_count:
            own_out, gathered = exchange(
                partial, own_input, gate, layer_idx, True, head_count, own_rows
            )
            current_full = gathered.reshape(patch_len, width)
        else:
            level_now = noise_level(step_index[0])
            level_next = noise_level(step_index[0] + 1)
            levels = jnp.stack([level_now, level_next - level_now]).reshape(1, 2)
            own_out, latent_next, denoised = exchange(
                partial, own_input, gate, layer_idx, False, head_count, own_rows,
                tail=(w_final, latent[0], levels),
            )
        own_input = own_out
        outputs.append(own_out)
    layer_out = jnp.stack(outputs)[:, None]
    return (layer_out, latent_next[None], denoised[None])


def solution(mesh):
    placed = (
        P("tok", None, None),
        P("tok", ("section", "head"), None),
        P(None, None, None, ("section", "head")),
        P(None, ("section", "head"), None),
        P(),
        P(),
        P(),
        P(None, None, "tok", None, ("section", "head")),
        P(),
        P(),
        P(),
    )
    return jax.shard_map(
        shards,
        mesh=mesh,
        in_specs=placed,
        out_specs=(
            P(None, "tok", ("section", "head"), None),
            P("tok", ("section", "head"), None),
            P("tok", ("section", "head"), None),
        ),
        check_vma=False,
    )
```

```python
import functools
import math

import jax
import jax.numpy as jnp
from jax import lax
from jax.experimental import pallas as pl
from jax.experimental.pallas import tpu as pltpu
from jax.sharding import PartitionSpec as P

STEPS = 28
MOST = 8


norm_eps = 1e-06
time_shift = 3.0
rope_base = 10000.0


def layer_norm(inputs):
    average = jnp.mean(inputs, axis=-1, keepdims=True)
    centred = inputs - average
    variance = jnp.mean(centred * centred, axis=-1, keepdims=True)
    return centred * lax.rsqrt(variance + norm_eps)


def rms_norm(inputs, gains):
    return inputs * lax.rsqrt(jnp.mean(inputs * inputs, axis=-1, keepdims=True) + norm_eps) * gains


def rotate(inputs, positions):
    half_dim = inputs.shape[-1] // 2
    frequency = rope_base ** (-2.0 * jnp.arange(half_dim, dtype=jnp.float32) / inputs.shape[-1])
    angles = positions[..., None, None] * frequency
    pairs = inputs.reshape(inputs.shape[:-1] + (half_dim, 2))
    even_lane = pairs[..., 0]
    odd_lane = pairs[..., 1]
    cosine = jnp.cos(angles)
    sine = jnp.sin(angles)
    turned = jnp.stack(
        [even_lane * cosine - odd_lane * sine, even_lane * sine + odd_lane * cosine], axis=-1
    )
    return turned.reshape(inputs.shape)


def slot_layout(request_patches, patch_order):
    request_ends = jnp.cumsum(request_patches)
    starts = request_ends - request_patches
    request_of = jnp.sum((request_ends[None, :] <= patch_order[:, None]).astype(jnp.int32), axis=1)
    chosen = request_of[:, None] == jnp.arange(request_patches.shape[0], dtype=jnp.int32)[None, :]
    first_patch = jnp.sum(jnp.where(chosen, starts[None, :], 0), axis=1)
    return (request_of, patch_order - first_patch)


def project(inputs, layer_mod, weight, gains, positions, head_dim):
    normed = (layer_norm(inputs.astype(jnp.float32)) * (1.0 + layer_mod[1]) + layer_mod[0]).astype(
        jnp.bfloat16
    )
    rows = inputs.shape[0]
    column_count = weight.shape[2]
    heads = column_count // head_dim
    pieces = [
        jnp.dot(normed, weight[:, part, :], preferred_element_type=jnp.float32).reshape(
            rows, heads, head_dim
        )
        for part in range(3)
    ]
    queries = rotate(rms_norm(pieces[0], gains[0]), positions).astype(jnp.bfloat16)
    keys_fresh = rotate(rms_norm(pieces[1], gains[1]), positions).astype(jnp.bfloat16)
    values_fresh = pieces[2].astype(jnp.bfloat16)
    return (
        queries.reshape(rows, column_count),
        keys_fresh.reshape(rows, column_count),
        values_fresh.reshape(rows, column_count),
    )


def fresh_kernel(head_dim, q_ref, kf_ref, vf_ref, qt_ref, m_ref, l_ref, acc_ref):
    heads = q_ref.shape[1] // head_dim
    scaling = 1.0 / math.sqrt(head_dim)
    by_key = (((0,), (0,)), ((), ()))
    for h in range(heads):
        lanes = slice(h * head_dim, (h + 1) * head_dim)
        qt_ref[h] = q_ref[:, lanes].T
        scores = jnp.dot(kf_ref[:, lanes], qt_ref[h], preferred_element_type=jnp.float32) * scaling
        col_max = jnp.max(scores, axis=0, keepdims=True)
        weights = jnp.exp(scores - col_max)
        m_ref[h] = col_max
        l_ref[h] = jnp.sum(weights, axis=0, keepdims=True)
        acc_ref[h] = lax.dot_general(
            vf_ref[:, lanes], weights.astype(jnp.bfloat16), by_key,
            preferred_element_type=jnp.float32,
        )


def attention_kernel(
    head_dim, fetch_ref, allow_ref, qt_ref, m0_ref, l0_ref, acc0_ref, ks_ref, vs_ref, ks2_ref, vs2_ref,
    mine_ref, theirs_ref, m_sc, l_sc, acc_sc
):
    slot = pl.program_id(0)
    heads = qt_ref.shape[0]
    scaling = 1.0 / math.sqrt(head_dim)
    by_key = (((0,), (0,)), ((), ()))

    @pl.when(slot == 0)
    def _start():
        m_sc[...] = m0_ref[...]
        l_sc[...] = l0_ref[...]
        acc_sc[...] = acc0_ref[...]

    def update(key_ref, value_ref):
        for h in range(heads):
            lanes = slice(h * head_dim, (h + 1) * head_dim)
            scores = (
                jnp.dot(key_ref[:, lanes], qt_ref[h], preferred_element_type=jnp.float32) * scaling
            )
            old_max = m_sc[h]
            new_max = jnp.maximum(old_max, jnp.max(scores, axis=0, keepdims=True))
            factor = jnp.exp(old_max - new_max)
            weights = jnp.exp(scores - new_max)
            l_sc[h] = l_sc[h] * factor + jnp.sum(weights, axis=0, keepdims=True)
            acc_sc[h] = acc_sc[h] * factor + lax.dot_general(
                value_ref[:, lanes], weights.astype(jnp.bfloat16), by_key,
                preferred_element_type=jnp.float32,
            )
            m_sc[h] = new_max

    @pl.when(allow_ref[2 * slot] != 0)
    def _first():
        update(ks_ref, vs_ref)

    @pl.when(allow_ref[2 * slot + 1] != 0)
    def _second():
        update(ks2_ref, vs2_ref)

    @pl.when(slot == pl.num_programs(0) - 1)
    def _finish():
        first = lax.axis_index("section") == 0
        half_rows = mine_ref.shape[0]
        for h in range(heads):
            lanes = slice(h * head_dim, (h + 1) * head_dim)
            result = (acc_sc[h] / l_sc[h]).T.astype(mine_ref.dtype)
            top = result[:half_rows]
            bottom = result[half_rows:]
            mine_ref[:, lanes] = jnp.where(first, top, bottom)
            theirs_ref[:, lanes] = jnp.where(first, bottom, top)


def attend(queries, keys_fresh, values_fresh, stale, fetch, allow, head_dim):
    rows, features = queries.shape
    slot_total = fetch.shape[0] // 2
    heads = features // head_dim
    vmem = pl.BlockSpec(memory_space=pltpu.VMEM)
    state = pl.pallas_call(
        functools.partial(fresh_kernel, head_dim),
        out_shape=(
            jax.ShapeDtypeStruct((heads, head_dim, rows), jnp.bfloat16),
            jax.ShapeDtypeStruct((heads, 1, rows), jnp.float32),
            jax.ShapeDtypeStruct((heads, 1, rows), jnp.float32),
            jax.ShapeDtypeStruct((heads, head_dim, rows), jnp.float32),
        ),
        in_specs=[vmem] * 3,
        out_specs=(vmem,) * 4,
    )(queries, keys_fresh, values_fresh)
    half = pl.BlockSpec((rows // 2, features), lambda j, f, a: (0, 0))
    qt_spec = pl.BlockSpec((heads, head_dim, rows), lambda j, f, a: (0, 0, 0))
    stat_spec = pl.BlockSpec((heads, 1, rows), lambda j, f, a: (0, 0, 0))
    key_spec = pl.BlockSpec(
        (None, None, rows, features), lambda j, f, a: (f[2 * j], 0, 0, 0)
    )
    value_spec = pl.BlockSpec(
        (None, None, rows, features), lambda j, f, a: (f[2 * j], 1, 0, 0)
    )
    key2_spec = pl.BlockSpec(
        (None, None, rows, features), lambda j, f, a: (f[2 * j + 1], 0, 0, 0)
    )
    value2_spec = pl.BlockSpec(
        (None, None, rows, features), lambda j, f, a: (f[2 * j + 1], 1, 0, 0)
    )
    return pl.pallas_call(
        functools.partial(attention_kernel, head_dim),
        out_shape=(
            jax.ShapeDtypeStruct((rows // 2, features), jnp.bfloat16),
            jax.ShapeDtypeStruct((rows // 2, features), jnp.bfloat16),
        ),
        grid_spec=pltpu.PrefetchScalarGridSpec(
            num_scalar_prefetch=2,
            grid=(slot_total,),
            in_specs=[qt_spec, stat_spec, stat_spec, qt_spec, key_spec, value_spec, key2_spec, value2_spec],
            out_specs=(half, half),
            scratch_shapes=[
                pltpu.VMEM((heads, 1, rows), jnp.float32),
                pltpu.VMEM((heads, 1, rows), jnp.float32),
                pltpu.VMEM((heads, head_dim, rows), jnp.float32),
            ],
        ),
        compiler_params=pltpu.CompilerParams(dimension_semantics=("arbitrary",)),
    )(fetch, allow, *state, stale, stale, stale, stale)


def exchange_kernel(head_count, own_rows, split, gather, part_ref, own_ref, gate_ref, *rest):
    if gather:
        (out_ref, full_ref, land_a, land_b, sums_a, sums_b, acc,
         r_send, r_recv, a_send, a_recv, g2_send, g2_recv) = rest
    else:
        (wf_ref, latent_ref, levels_ref, out_ref, next_ref, denoised_ref,
         land_a, land_b, sums_a, sums_b, acc, r_send, r_recv) = rest
    mesh_ids = pl.DeviceIdType.MESH
    section = lax.axis_index("section")
    head = lax.axis_index("head")
    tok = lax.axis_index("tok")
    other = 1 - section
    up = lax.rem(head + 1, head_count)
    down = lax.rem(head + head_count - 1, head_count)
    opposite = lax.rem(head + 2, head_count)
    low = pl.ds(0, split)
    high = pl.ds(split, own_rows - split)

    def rows_of(block, offset, count):
        return pl.ds(pl.multiple_of(block * own_rows + offset, 16), count)

    barrier = pltpu.get_barrier_semaphore()
    if gather:
        pl.semaphore_signal(barrier, inc=1, device_id=(other, head, tok), device_id_type=mesh_ids)
    for neighbour in (up, down):
        pl.semaphore_signal(barrier, inc=1, device_id=(section, neighbour, tok), device_id_type=mesh_ids)
    pl.semaphore_wait(barrier, 3 if gather else 2)

    def ring(kind, src, dst, target, send_sem, recv_sem):
        return pltpu.make_async_remote_copy(
            src_ref=src,
            dst_ref=dst,
            send_sem=send_sem.at[kind],
            recv_sem=recv_sem.at[kind],
            device_id=(section, target, tok),
            device_id_type=mesh_ids,
        )

    low_count = split
    high_count = own_rows - split
    pass_a = ring(0, part_ref.at[rows_of(opposite, 0, low_count)], land_a.at[0], up, r_send, r_recv)
    pass_b = ring(1, part_ref.at[rows_of(opposite, split, high_count)], land_b.at[0], down, r_send, r_recv)
    direct_a = ring(2, part_ref.at[rows_of(down, 0, low_count)], land_a.at[1], down, r_send, r_recv)
    direct_b = ring(3, part_ref.at[rows_of(up, split, high_count)], land_b.at[1], up, r_send, r_recv)
    pass_a.start()
    pass_b.start()
    direct_a.start()
    direct_b.start()
    acc[...] = part_ref[rows_of(head, 0, own_rows), :].astype(jnp.float32)
    pass_a.wait()
    sums_a[...] = (
        part_ref[rows_of(up, 0, low_count), :].astype(jnp.float32) + land_a[0].astype(jnp.float32)
    ).astype(sums_a.dtype)
    joined_a = ring(4, sums_a, land_a.at[2], up, r_send, r_recv)
    joined_a.start()
    pass_b.wait()
    sums_b[...] = (
        part_ref[rows_of(down, split, high_count), :].astype(jnp.float32)
        + land_b[0].astype(jnp.float32)
    ).astype(sums_b.dtype)
    joined_b = ring(5, sums_b, land_b.at[2], down, r_send, r_recv)
    joined_b.start()
    direct_a.wait()
    direct_b.wait()
    joined_a.wait()
    joined_b.wait()
    acc[low, :] += land_a[1].astype(jnp.float32) + land_a[2].astype(jnp.float32)
    acc[high, :] += land_b[1].astype(jnp.float32) + land_b[2].astype(jnp.float32)
    if not gather:
        final = (own_ref[...].astype(jnp.float32) + gate_ref[...] * acc[...]).astype(out_ref.dtype)
        out_ref[...] = final
        normed = layer_norm(final.astype(jnp.float32)).astype(jnp.bfloat16)
        velocity = jnp.dot(normed, wf_ref[...], preferred_element_type=jnp.float32)
        level_now = levels_ref[:, 0:1]
        level_step = levels_ref[:, 1:2]
        next_ref[...] = latent_ref[...] + level_step * velocity
        denoised_ref[...] = latent_ref[...] - level_now * velocity
        return
    result = (own_ref[...].astype(jnp.float32) + gate_ref[...] * acc[...]).astype(full_ref.dtype)
    full_ref[section, head] = result
    out_ref[...] = result

    def pass_copy(h):
        return pltpu.make_async_remote_copy(
            src_ref=full_ref.at[section, h],
            dst_ref=full_ref.at[section, h],
            send_sem=g2_send.at[h],
            recv_sem=g2_recv.at[h],
            device_id=(other, head, tok),
            device_id_type=mesh_ids,
        )

    to_up = ring(0, full_ref.at[section, head], full_ref.at[section, head], up, a_send, a_recv)
    to_down = ring(1, full_ref.at[section, head], full_ref.at[section, head], down, a_send, a_recv)
    to_up.start()
    to_down.start()
    pass_copy(head).start()
    to_up.wait()
    onward_a = ring(
        2, full_ref.at[section, down, low], full_ref.at[section, down, low], up, a_send, a_recv
    )
    onward_a.start()
    pass_copy(down).start()
    to_down.wait()
    onward_b = ring(
        3, full_ref.at[section, up, high], full_ref.at[section, up, high], down, a_send, a_recv
    )
    onward_b.start()
    pass_copy(up).start()
    onward_a.wait()
    onward_b.wait()
    pass_copy(opposite).start()
    pass_copy(head).wait()
    pass_copy(down).wait()
    pass_copy(up).wait()
    pass_copy(opposite).wait()


def exchange(partial, own_input, gate, layer_idx, gather, head_count, own_rows, tail=()):
    rows, width = partial.shape
    split = (own_rows * 2 // 3) // 16 * 16
    vmem = pl.BlockSpec(memory_space=pltpu.VMEM)
    scratch = [
        pltpu.VMEM((3, split, width), partial.dtype),
        pltpu.VMEM((3, own_rows - split, width), partial.dtype),
        pltpu.VMEM((split, width), partial.dtype),
        pltpu.VMEM((own_rows - split, width), partial.dtype),
        pltpu.VMEM((own_rows, width), jnp.float32),
        pltpu.SemaphoreType.DMA((6,)),
        pltpu.SemaphoreType.DMA((6,)),
    ]
    if gather:
        out_shape = (
            jax.ShapeDtypeStruct((own_rows, width), jnp.bfloat16),
            jax.ShapeDtypeStruct((2, head_count, own_rows, width), jnp.bfloat16),
        )
        out_specs = (vmem, vmem)
        scratch += [pltpu.SemaphoreType.DMA((head_count,))] * 4
    else:
        latent_width = tail[1].shape[1]
        out_shape = (
            jax.ShapeDtypeStruct((own_rows, width), jnp.bfloat16),
            jax.ShapeDtypeStruct((own_rows, latent_width), jnp.float32),
            jax.ShapeDtypeStruct((own_rows, latent_width), jnp.float32),
        )
        out_specs = (vmem, vmem, vmem)
    return pl.pallas_call(
        functools.partial(exchange_kernel, head_count, own_rows, split, gather),
        out_shape=out_shape,
        in_specs=[vmem] * (3 + len(tail)),
        out_specs=out_specs,
        scratch_shapes=scratch,
        compiler_params=pltpu.CompilerParams(
            collective_id=layer_idx, has_side_effects=True, vmem_limit_bytes=48 * 1024 * 1024
        ),
    )(partial, own_input, gate.reshape(1, width), *tail)


def noise_level(position):
    time_left = 1.0 - position.astype(jnp.float32) / STEPS
    return time_shift * time_left / (1.0 + (time_shift - 1.0) * time_left)


def shards(
    hidden,
    latent,
    w_qkv,
    w_out,
    w_final,
    qk_gain,
    modulation,
    stale_kv,
    request_patches,
    patch_order,
    step_index,
):
    section_count = lax.axis_size("section")
    head_count = lax.axis_size("head")
    group_count = section_count * head_count
    section_index = lax.axis_index("section")
    head_index = lax.axis_index("head")
    tok_index = lax.axis_index("tok")
    group_index = section_index * head_count + head_index
    patch_len = hidden.shape[1]
    width = hidden.shape[2]
    head_dim = qk_gain.shape[-1]
    own_rows = patch_len // group_count
    layer_count = w_qkv.shape[0]
    request_of, offsets = slot_layout(request_patches, patch_order)
    slot_total = request_of.shape[0]
    my_request = request_of[tok_index]
    my_offset = offsets[tok_index]
    positions = (my_offset * patch_len + jnp.arange(patch_len, dtype=jnp.int32)).astype(jnp.float32)
    slot_ids = jnp.arange(slot_total, dtype=jnp.int32)
    allowed = (request_of == my_request) & (slot_ids != tok_index)
    rank = jnp.cumsum(allowed.astype(jnp.int32)) - 1
    count = jnp.sum(allowed.astype(jnp.int32))
    step_ids = jnp.arange(MOST - 1 + (MOST - 1) % 2, dtype=jnp.int32)
    picked = allowed[None, :] & (rank[None, :] == step_ids[:, None])
    compact = jnp.sum(jnp.where(picked, slot_ids[None, :], 0), axis=1)
    last_pick = jnp.sum(jnp.where(allowed & (rank == count - 1), slot_ids, 0))
    fetch = jnp.where(step_ids < count, compact, last_pick).astype(jnp.int32)
    allow = (step_ids < count).astype(jnp.int32)
    stale_layers = [
        lax.all_gather(jnp.swapaxes(stale_kv[layer], 0, 1), "tok", axis=0, tiled=True)
        for layer in range(layer_count)
    ]
    current_full = hidden[0]
    w_partner = lax.ppermute(w_out, "section", perm=[(0, 1), (1, 0)])
    own_input = lax.dynamic_slice_in_dim(current_full, group_index * own_rows, own_rows, 0)
    outputs = []
    for layer_idx in range(layer_count):
        queries, keys_fresh, values_fresh = project(
            current_full,
            modulation[layer_idx],
            w_qkv[layer_idx],
            qk_gain[layer_idx],
            positions,
            head_dim,
        )
        attended = attend(
            queries, keys_fresh, values_fresh, stale_layers[layer_idx], fetch, allow, head_dim
        )
        mine, theirs = attended
        swapped = lax.ppermute(theirs, "section", perm=[(0, 1), (1, 0)])
        partial = (
            jnp.dot(mine, w_out[layer_idx], preferred_element_type=jnp.float32)
            + jnp.dot(swapped, w_partner[layer_idx], preferred_element_type=jnp.float32)
        ).astype(jnp.bfloat16)
        gate = modulation[layer_idx, 2]
        if layer_idx + 1 < layer_count:
            own_out, gathered = exchange(
                partial, own_input, gate, layer_idx, True, head_count, own_rows
            )
            current_full = gathered.reshape(patch_len, width)
        else:
            level_now = noise_level(step_index[0])
            level_next = noise_level(step_index[0] + 1)
            levels = jnp.stack([level_now, level_next - level_now]).reshape(1, 2)
            own_out, latent_next, denoised = exchange(
                partial, own_input, gate, layer_idx, False, head_count, own_rows,
                tail=(w_final, latent[0], levels),
            )
        own_input = own_out
        outputs.append(own_out)
    layer_out = jnp.stack(outputs)[:, None]
    return (layer_out, latent_next[None], denoised[None])


def solution(mesh):
    placed = (
        P("tok", None, None),
        P("tok", ("section", "head"), None),
        P(None, None, None, ("section", "head")),
        P(None, ("section", "head"), None),
        P(),
        P(),
        P(),
        P(None, None, "tok", None, ("section", "head")),
        P(),
        P(),
        P(),
    )
    return jax.shard_map(
        shards,
        mesh=mesh,
        in_specs=placed,
        out_specs=(
            P(None, "tok", ("section", "head"), None),
            P("tok", ("section", "head"), None),
            P("tok", ("section", "head"), None),
        ),
        check_vma=False,
    )
```

```python
import functools
import math

import jax
import jax.numpy as jnp
from jax import lax
from jax.experimental import pallas as pl
from jax.experimental.pallas import tpu as pltpu
from jax.sharding import PartitionSpec as P

STEPS = 28
MOST = 8


norm_eps = 1e-06
time_shift = 3.0
rope_base = 10000.0


def layer_norm(inputs):
    average = jnp.mean(inputs, axis=-1, keepdims=True)
    centred = inputs - average
    variance = jnp.mean(centred * centred, axis=-1, keepdims=True)
    return centred * lax.rsqrt(variance + norm_eps)


def rms_norm(inputs, gains):
    return inputs * lax.rsqrt(jnp.mean(inputs * inputs, axis=-1, keepdims=True) + norm_eps) * gains


def rotate(inputs, positions):
    half_dim = inputs.shape[-1] // 2
    frequency = rope_base ** (-2.0 * jnp.arange(half_dim, dtype=jnp.float32) / inputs.shape[-1])
    angles = positions[..., None, None] * frequency
    pairs = inputs.reshape(inputs.shape[:-1] + (half_dim, 2))
    even_lane = pairs[..., 0]
    odd_lane = pairs[..., 1]
    cosine = jnp.cos(angles)
    sine = jnp.sin(angles)
    turned = jnp.stack(
        [even_lane * cosine - odd_lane * sine, even_lane * sine + odd_lane * cosine], axis=-1
    )
    return turned.reshape(inputs.shape)


def slot_layout(request_patches, patch_order):
    request_ends = jnp.cumsum(request_patches)
    starts = request_ends - request_patches
    request_of = jnp.sum((request_ends[None, :] <= patch_order[:, None]).astype(jnp.int32), axis=1)
    chosen = request_of[:, None] == jnp.arange(request_patches.shape[0], dtype=jnp.int32)[None, :]
    first_patch = jnp.sum(jnp.where(chosen, starts[None, :], 0), axis=1)
    return (request_of, patch_order - first_patch)


def project(inputs, layer_mod, weight, gains, positions, head_dim):
    normed = (layer_norm(inputs.astype(jnp.float32)) * (1.0 + layer_mod[1]) + layer_mod[0]).astype(
        jnp.bfloat16
    )
    rows = inputs.shape[0]
    column_count = weight.shape[2]
    heads = column_count // head_dim
    pieces = [
        jnp.dot(normed, weight[:, part, :], preferred_element_type=jnp.float32).reshape(
            rows, heads, head_dim
        )
        for part in range(3)
    ]
    queries = rotate(rms_norm(pieces[0], gains[0]), positions).astype(jnp.bfloat16)
    keys_fresh = rotate(rms_norm(pieces[1], gains[1]), positions).astype(jnp.bfloat16)
    values_fresh = pieces[2].astype(jnp.bfloat16)
    return (
        queries.reshape(rows, column_count),
        keys_fresh.reshape(rows, column_count),
        values_fresh.reshape(rows, column_count),
    )


def fresh_kernel(head_dim, q_ref, kf_ref, vf_ref, qt_ref, m_ref, l_ref, acc_ref):
    heads = q_ref.shape[1] // head_dim
    scaling = 1.0 / math.sqrt(head_dim)
    by_key = (((0,), (0,)), ((), ()))
    for h in range(heads):
        lanes = slice(h * head_dim, (h + 1) * head_dim)
        qt_ref[h] = q_ref[:, lanes].T
        scores = jnp.dot(kf_ref[:, lanes], qt_ref[h], preferred_element_type=jnp.float32) * scaling
        col_max = jnp.max(scores, axis=0, keepdims=True)
        weights = jnp.exp(scores - col_max)
        m_ref[h] = col_max
        l_ref[h] = jnp.sum(weights, axis=0, keepdims=True)
        acc_ref[h] = lax.dot_general(
            vf_ref[:, lanes], weights.astype(jnp.bfloat16), by_key,
            preferred_element_type=jnp.float32,
        )


def attention_kernel(
    head_dim, fetch_ref, allow_ref, qt_ref, m0_ref, l0_ref, acc0_ref, ks_ref, vs_ref, mine_ref,
    theirs_ref, m_sc, l_sc, acc_sc
):
    slot = pl.program_id(0)
    heads = qt_ref.shape[0]
    scaling = 1.0 / math.sqrt(head_dim)
    by_key = (((0,), (0,)), ((), ()))

    @pl.when(slot == 0)
    def _start():
        m_sc[...] = m0_ref[...]
        l_sc[...] = l0_ref[...]
        acc_sc[...] = acc0_ref[...]

    @pl.when(allow_ref[slot] != 0)
    def _stale():
        for h in range(heads):
            lanes = slice(h * head_dim, (h + 1) * head_dim)
            scores = (
                jnp.dot(ks_ref[:, lanes], qt_ref[h], preferred_element_type=jnp.float32) * scaling
            )
            old_max = m_sc[h]
            new_max = jnp.maximum(old_max, jnp.max(scores, axis=0, keepdims=True))
            factor = jnp.exp(old_max - new_max)
            weights = jnp.exp(scores - new_max)
            l_sc[h] = l_sc[h] * factor + jnp.sum(weights, axis=0, keepdims=True)
            acc_sc[h] = acc_sc[h] * factor + lax.dot_general(
                vs_ref[:, lanes], weights.astype(jnp.bfloat16), by_key,
                preferred_element_type=jnp.float32,
            )
            m_sc[h] = new_max

    @pl.when(slot == pl.num_programs(0) - 1)
    def _finish():
        first = lax.axis_index("section") == 0
        half_rows = mine_ref.shape[0]
        for h in range(heads):
            lanes = slice(h * head_dim, (h + 1) * head_dim)
            result = (acc_sc[h] / l_sc[h]).T.astype(mine_ref.dtype)
            top = result[:half_rows]
            bottom = result[half_rows:]
            mine_ref[:, lanes] = jnp.where(first, top, bottom)
            theirs_ref[:, lanes] = jnp.where(first, bottom, top)


def attend(queries, keys_fresh, values_fresh, stale, fetch, allow, head_dim):
    rows, features = queries.shape
    slot_total = fetch.shape[0]
    heads = features // head_dim
    vmem = pl.BlockSpec(memory_space=pltpu.VMEM)
    state = pl.pallas_call(
        functools.partial(fresh_kernel, head_dim),
        out_shape=(
            jax.ShapeDtypeStruct((heads, head_dim, rows), jnp.bfloat16),
            jax.ShapeDtypeStruct((heads, 1, rows), jnp.float32),
            jax.ShapeDtypeStruct((heads, 1, rows), jnp.float32),
            jax.ShapeDtypeStruct((heads, head_dim, rows), jnp.float32),
        ),
        in_specs=[vmem] * 3,
        out_specs=(vmem,) * 4,
    )(queries, keys_fresh, values_fresh)
    half = pl.BlockSpec((rows // 2, features), lambda j, f, a: (0, 0))
    qt_spec = pl.BlockSpec((heads, head_dim, rows), lambda j, f, a: (0, 0, 0))
    stat_spec = pl.BlockSpec((heads, 1, rows), lambda j, f, a: (0, 0, 0))
    key_spec = pl.BlockSpec(
        (None, None, rows, features), lambda j, f, a: (f[j], 0, 0, 0)
    )
    value_spec = pl.BlockSpec(
        (None, None, rows, features), lambda j, f, a: (f[j], 1, 0, 0)
    )
    return pl.pallas_call(
        functools.partial(attention_kernel, head_dim),
        out_shape=(
            jax.ShapeDtypeStruct((rows // 2, features), jnp.bfloat16),
            jax.ShapeDtypeStruct((rows // 2, features), jnp.bfloat16),
        ),
        grid_spec=pltpu.PrefetchScalarGridSpec(
            num_scalar_prefetch=2,
            grid=(slot_total,),
            in_specs=[qt_spec, stat_spec, stat_spec, qt_spec, key_spec, value_spec],
            out_specs=(half, half),
            scratch_shapes=[
                pltpu.VMEM((heads, 1, rows), jnp.float32),
                pltpu.VMEM((heads, 1, rows), jnp.float32),
                pltpu.VMEM((heads, head_dim, rows), jnp.float32),
            ],
        ),
        compiler_params=pltpu.CompilerParams(dimension_semantics=("arbitrary",)),
    )(fetch, allow, *state, stale, stale)


def exchange_kernel(head_count, own_rows, split, gather, part_ref, own_ref, gate_ref, *rest):
    if gather:
        (out_ref, full_ref, land_a, land_b, sums_a, sums_b, acc,
         r_send, r_recv, a_send, a_recv, g2_send, g2_recv) = rest
    else:
        (wf_ref, latent_ref, levels_ref, out_ref, next_ref, denoised_ref,
         land_a, land_b, sums_a, sums_b, acc, r_send, r_recv) = rest
    mesh_ids = pl.DeviceIdType.MESH
    section = lax.axis_index("section")
    head = lax.axis_index("head")
    tok = lax.axis_index("tok")
    other = 1 - section
    up = lax.rem(head + 1, head_count)
    down = lax.rem(head + head_count - 1, head_count)
    opposite = lax.rem(head + 2, head_count)
    low = pl.ds(0, split)
    high = pl.ds(split, own_rows - split)

    def rows_of(block, offset, count):
        return pl.ds(pl.multiple_of(block * own_rows + offset, 16), count)

    barrier = pltpu.get_barrier_semaphore()
    if gather:
        pl.semaphore_signal(barrier, inc=1, device_id=(other, head, tok), device_id_type=mesh_ids)
    for neighbour in (up, down):
        pl.semaphore_signal(barrier, inc=1, device_id=(section, neighbour, tok), device_id_type=mesh_ids)
    pl.semaphore_wait(barrier, 3 if gather else 2)

    def ring(kind, src, dst, target, send_sem, recv_sem):
        return pltpu.make_async_remote_copy(
            src_ref=src,
            dst_ref=dst,
            send_sem=send_sem.at[kind],
            recv_sem=recv_sem.at[kind],
            device_id=(section, target, tok),
            device_id_type=mesh_ids,
        )

    low_count = split
    high_count = own_rows - split
    pass_a = ring(0, part_ref.at[rows_of(opposite, 0, low_count)], land_a.at[0], up, r_send, r_recv)
    pass_b = ring(1, part_ref.at[rows_of(opposite, split, high_count)], land_b.at[0], down, r_send, r_recv)
    direct_a = ring(2, part_ref.at[rows_of(down, 0, low_count)], land_a.at[1], down, r_send, r_recv)
    direct_b = ring(3, part_ref.at[rows_of(up, split, high_count)], land_b.at[1], up, r_send, r_recv)
    pass_a.start()
    pass_b.start()
    direct_a.start()
    direct_b.start()
    acc[...] = part_ref[rows_of(head, 0, own_rows), :].astype(jnp.float32)
    pass_a.wait()
    sums_a[...] = (
        part_ref[rows_of(up, 0, low_count), :].astype(jnp.float32) + land_a[0].astype(jnp.float32)
    ).astype(sums_a.dtype)
    joined_a = ring(4, sums_a, land_a.at[2], up, r_send, r_recv)
    joined_a.start()
    pass_b.wait()
    sums_b[...] = (
        part_ref[rows_of(down, split, high_count), :].astype(jnp.float32)
        + land_b[0].astype(jnp.float32)
    ).astype(sums_b.dtype)
    joined_b = ring(5, sums_b, land_b.at[2], down, r_send, r_recv)
    joined_b.start()
    direct_a.wait()
    direct_b.wait()
    joined_a.wait()
    joined_b.wait()
    acc[low, :] += land_a[1].astype(jnp.float32) + land_a[2].astype(jnp.float32)
    acc[high, :] += land_b[1].astype(jnp.float32) + land_b[2].astype(jnp.float32)
    if not gather:
        final = (own_ref[...].astype(jnp.float32) + gate_ref[...] * acc[...]).astype(out_ref.dtype)
        out_ref[...] = final
        normed = layer_norm(final.astype(jnp.float32)).astype(jnp.bfloat16)
        velocity = jnp.dot(normed, wf_ref[...], preferred_element_type=jnp.float32)
        level_now = levels_ref[:, 0:1]
        level_step = levels_ref[:, 1:2]
        next_ref[...] = latent_ref[...] + level_step * velocity
        denoised_ref[...] = latent_ref[...] - level_now * velocity
        return
    result = (own_ref[...].astype(jnp.float32) + gate_ref[...] * acc[...]).astype(full_ref.dtype)
    full_ref[section, head] = result
    out_ref[...] = result

    def pass_copy(h):
        return pltpu.make_async_remote_copy(
            src_ref=full_ref.at[section, h],
            dst_ref=full_ref.at[section, h],
            send_sem=g2_send.at[h],
            recv_sem=g2_recv.at[h],
            device_id=(other, head, tok),
            device_id_type=mesh_ids,
        )

    to_up = ring(0, full_ref.at[section, head], full_ref.at[section, head], up, a_send, a_recv)
    to_down = ring(1, full_ref.at[section, head], full_ref.at[section, head], down, a_send, a_recv)
    to_up.start()
    to_down.start()
    pass_copy(head).start()
    to_up.wait()
    onward_a = ring(
        2, full_ref.at[section, down, low], full_ref.at[section, down, low], up, a_send, a_recv
    )
    onward_a.start()
    pass_copy(down).start()
    to_down.wait()
    onward_b = ring(
        3, full_ref.at[section, up, high], full_ref.at[section, up, high], down, a_send, a_recv
    )
    onward_b.start()
    pass_copy(up).start()
    onward_a.wait()
    onward_b.wait()
    pass_copy(opposite).start()
    pass_copy(head).wait()
    pass_copy(down).wait()
    pass_copy(up).wait()
    pass_copy(opposite).wait()


def exchange(partial, own_input, gate, layer_idx, gather, head_count, own_rows, tail=()):
    rows, width = partial.shape
    split = (own_rows * 2 // 3) // 16 * 16
    vmem = pl.BlockSpec(memory_space=pltpu.VMEM)
    scratch = [
        pltpu.VMEM((3, split, width), partial.dtype),
        pltpu.VMEM((3, own_rows - split, width), partial.dtype),
        pltpu.VMEM((split, width), partial.dtype),
        pltpu.VMEM((own_rows - split, width), partial.dtype),
        pltpu.VMEM((own_rows, width), jnp.float32),
        pltpu.SemaphoreType.DMA((6,)),
        pltpu.SemaphoreType.DMA((6,)),
    ]
    if gather:
        out_shape = (
            jax.ShapeDtypeStruct((own_rows, width), jnp.bfloat16),
            jax.ShapeDtypeStruct((2, head_count, own_rows, width), jnp.bfloat16),
        )
        out_specs = (vmem, vmem)
        scratch += [pltpu.SemaphoreType.DMA((head_count,))] * 4
    else:
        latent_width = tail[1].shape[1]
        out_shape = (
            jax.ShapeDtypeStruct((own_rows, width), jnp.bfloat16),
            jax.ShapeDtypeStruct((own_rows, latent_width), jnp.float32),
            jax.ShapeDtypeStruct((own_rows, latent_width), jnp.float32),
        )
        out_specs = (vmem, vmem, vmem)
    return pl.pallas_call(
        functools.partial(exchange_kernel, head_count, own_rows, split, gather),
        out_shape=out_shape,
        in_specs=[vmem] * (3 + len(tail)),
        out_specs=out_specs,
        scratch_shapes=scratch,
        compiler_params=pltpu.CompilerParams(
            collective_id=layer_idx, has_side_effects=True, vmem_limit_bytes=48 * 1024 * 1024
        ),
    )(partial, own_input, gate.reshape(1, width), *tail)


def noise_level(position):
    time_left = 1.0 - position.astype(jnp.float32) / STEPS
    return time_shift * time_left / (1.0 + (time_shift - 1.0) * time_left)


def shards(
    hidden,
    latent,
    w_qkv,
    w_out,
    w_final,
    qk_gain,
    modulation,
    stale_kv,
    request_patches,
    patch_order,
    step_index,
):
    section_count = lax.axis_size("section")
    head_count = lax.axis_size("head")
    group_count = section_count * head_count
    section_index = lax.axis_index("section")
    head_index = lax.axis_index("head")
    tok_index = lax.axis_index("tok")
    group_index = section_index * head_count + head_index
    patch_len = hidden.shape[1]
    width = hidden.shape[2]
    head_dim = qk_gain.shape[-1]
    own_rows = patch_len // group_count
    layer_count = w_qkv.shape[0]
    request_of, offsets = slot_layout(request_patches, patch_order)
    slot_total = request_of.shape[0]
    my_request = request_of[tok_index]
    my_offset = offsets[tok_index]
    positions = (my_offset * patch_len + jnp.arange(patch_len, dtype=jnp.int32)).astype(jnp.float32)
    slot_ids = jnp.arange(slot_total, dtype=jnp.int32)
    allowed = (request_of == my_request) & (slot_ids != tok_index)
    rank = jnp.cumsum(allowed.astype(jnp.int32)) - 1
    count = jnp.sum(allowed.astype(jnp.int32))
    step_ids = jnp.arange(MOST - 1, dtype=jnp.int32)
    picked = allowed[None, :] & (rank[None, :] == step_ids[:, None])
    compact = jnp.sum(jnp.where(picked, slot_ids[None, :], 0), axis=1)
    last_pick = jnp.sum(jnp.where(allowed & (rank == count - 1), slot_ids, 0))
    fetch = jnp.where(step_ids < count, compact, last_pick).astype(jnp.int32)
    allow = (step_ids < count).astype(jnp.int32)
    stale_layers = [
        lax.all_gather(jnp.swapaxes(stale_kv[layer], 0, 1), "tok", axis=0, tiled=True)
        for layer in range(layer_count)
    ]
    current_full = hidden[0]
    w_partner = lax.ppermute(w_out, "section", perm=[(0, 1), (1, 0)])
    w_joined = jnp.concatenate([w_out, w_partner], axis=1)
    own_input = lax.dynamic_slice_in_dim(current_full, group_index * own_rows, own_rows, 0)
    outputs = []
    for layer_idx in range(layer_count):
        queries, keys_fresh, values_fresh = project(
            current_full,
            modulation[layer_idx],
            w_qkv[layer_idx],
            qk_gain[layer_idx],
            positions,
            head_dim,
        )
        attended = attend(
            queries, keys_fresh, values_fresh, stale_layers[layer_idx], fetch, allow, head_dim
        )
        mine, theirs = attended
        swapped = lax.ppermute(theirs, "section", perm=[(0, 1), (1, 0)])
        partial = jnp.dot(
            jnp.concatenate([mine, swapped], axis=1),
            w_joined[layer_idx],
            preferred_element_type=jnp.float32,
        ).astype(jnp.bfloat16)
        gate = modulation[layer_idx, 2]
        if layer_idx + 1 < layer_count:
            own_out, gathered = exchange(
                partial, own_input, gate, layer_idx, True, head_count, own_rows
            )
            current_full = gathered.reshape(patch_len, width)
        else:
            level_now = noise_level(step_index[0])
            level_next = noise_level(step_index[0] + 1)
            levels = jnp.stack([level_now, level_next - level_now]).reshape(1, 2)
            own_out, latent_next, denoised = exchange(
                partial, own_input, gate, layer_idx, False, head_count, own_rows,
                tail=(w_final, latent[0], levels),
            )
        own_input = own_out
        outputs.append(own_out)
    layer_out = jnp.stack(outputs)[:, None]
    return (layer_out, latent_next[None], denoised[None])


def solution(mesh):
    placed = (
        P("tok", None, None),
        P("tok", ("section", "head"), None),
        P(None, None, None, ("section", "head")),
        P(None, ("section", "head"), None),
        P(),
        P(),
        P(),
        P(None, None, "tok", None, ("section", "head")),
        P(),
        P(),
        P(),
    )
    return jax.shard_map(
        shards,
        mesh=mesh,
        in_specs=placed,
        out_specs=(
            P(None, "tok", ("section", "head"), None),
            P("tok", ("section", "head"), None),
            P("tok", ("section", "head"), None),
        ),
        check_vma=False,
    )
```
